128 devices in a mesh: dom: 16 (over x_hi, z, core), slab: 8 (over y, x_lo).
Axes of the slice: x: 4 (x_hi: 2, x_lo: 2; x = x_hi * 2 + x_lo), y: 4, z: 4, core: 2. Of those that a mesh axis runs over, the one named last changes fastest.
Arguments:
- displacement: float32 [3, 5, 5, 5, 32, 2048], P(None, None, None, None, 'dom', 'slab'), may hold values from -0.6 to 0.6
- velocity: float32 [3, 5, 5, 5, 32, 2048], P(None, None, None, None, 'dom', 'slab'), may hold values from -6 to 6
- lame_lambda: float32 [5, 5, 5, 32, 2048], P(None, None, None, 'dom', 'slab'), may hold values from 0.5 to 1.5
- shear_modulus: float32 [5, 5, 5, 32, 2048], P(None, None, None, 'dom', 'slab'), may hold values from 0.3 to 1.2
- density: float32 [5, 5, 5, 32, 2048], P(None, None, None, 'dom', 'slab'), may hold values from 0.7 to 1.4
- traces: bfloat16 [32768, 3072], P(('dom', 'slab')), may hold values from -6 to 6
- section_weights: bfloat16 [4, 256], replicated, may hold values from -0.375 to 0.375
- owner: int32 [32768, 1], P(('dom', 'slab')), may hold values from 0 to 127; in each aligned block of 256 rows (0 to 255, 256 to 511, ...) at most 4 rows name the same one
- element_idx: int32 [32768], P(('dom', 'slab')), may hold values from 0 to 511
- node_weights: bfloat16 [32768, 125], P(('dom', 'slab')), may hold values from -1.796875 to 1.796875
- encode_bits: int32 [32768, 4], P(('dom', 'slab')), may hold values from 0 to 1
Outputs:
- disp_out: float32 [3, 5, 5, 5, 32, 2048], P(None, None, None, None, 'dom', 'slab')
- veloc_out: float32 [3, 5, 5, 5, 32, 2048], P(None, None, None, None, 'dom', 'slab')
The draws below stay inside these ranges and needn't reach their ends.
Inputs may be any that keep to these rules, and one draw needn't show every extreme that they name: Among the rows of one device at most 4 name the same owner, a bound that some of them reach.
All inputs are finite; a program needn't handle non-finite values.
Results may differ from the reference program's by a relative error of at most 0.0006.
Values may be sent and summed in bfloat16 or wider, within the bound.
A program may use at most 128 MiB of HBM per device.

```python
import math
import jax
import jax.numpy as jnp
import numpy as np
from jax import lax

EA = 2
EB = 2
EC = 128
CAP = 4
RECV_DEV = 256
G = 4
NT = 256
STEPS = 4
NA = 32
NB = 16
E_DEV = 512
RECV_TOT = 32768
N_SLAB = 8
DEVICES = 128


def with_ends(values, stream_key, smallest, top_value):
    longest = values.shape.index(max(values.shape))
    spots = []
    for shift in (0, 1):
        where = [jax.random.randint(jax.random.fold_in(stream_key, axis), (), 0, length) for axis, length in enumerate(values.shape)]
        where[longest] = (where[longest] + shift) % values.shape[longest]
        spots.append(tuple(where))
    return values.at[spots[0]].set(smallest).at[spots[1]].set(top_value)


def block_levels(stream_key, dims, cuts, low, high):
    def one(position, parts):
        draws = jax.random.uniform(jax.random.fold_in(jax.random.fold_in(stream_key, 6), position), (parts,), jnp.float32, low / len(cuts), high / len(cuts))
        return jnp.repeat(jnp.exp(draws), dims[position] // parts).reshape((-1,) + (1,) * (len(dims) - position - 1))

    factor_of = one(*cuts[0])
    for cut in cuts[1:]:
        factor_of = factor_of * one(*cut)
    return factor_of


def shared_out(rng, own, number, rows, count, top, limit, lean):
    order = jax.random.permutation(rng, count)
    packed, ordinary = load_shares(count, rows * top, limit, lean, True), load_shares(count, rows * top, limit, lean, False)
    places = jnp.arange(count)

    def named(tallies, turn):
        used = int((tallies > 0).sum())
        fixed = max(1, used // 4)
        passed = fixed + (places - fixed + turn * (used - fixed)) % max(1, count - fixed)
        return jnp.zeros((count,), jnp.int32).at[order[jnp.where(places < fixed, places, passed)]].set(jnp.asarray(tallies, jnp.int32))

    tallies = jnp.where(number % 4 == 0, named(packed, number // 4), named(ordinary, number - number // 4 - 1))
    mixed = jax.random.permutation(jax.random.fold_in(own, 3), count)
    source_of, sink = mixed[0:count // 2 * 2:2], mixed[1:count // 2 * 2:2]
    room = jnp.minimum(tallies[source_of] - 1, limit - tallies[sink]) // 2
    room = jnp.where((source_of == order[0]) | (sink == order[0]) | (tallies[sink] == 0), 0, jnp.maximum(room, 0))
    passed = jax.random.randint(jax.random.fold_in(own, 4), (count // 2,), 0, 1 << 20) % (room + 1)
    tallies = tallies.at[source_of].add(-passed).at[sink].add(passed)
    labels = jnp.searchsorted(jnp.cumsum(tallies), jnp.arange(rows * top), side="right").astype(jnp.int32)
    grid = labels.reshape(top, rows).T
    grid = grid[jax.random.permutation(jax.random.fold_in(own, 1), rows)]
    turn = jax.random.randint(jax.random.fold_in(own, 2), (rows, 1), 0, top)
    return jnp.take_along_axis(grid, (jnp.arange(top)[None, :] + turn) % top, axis=1)


def load_shares(count, total, limit, slope, full):
    portions = [(1 << 20) // math.isqrt(grade ** slope) + 1 for grade in range(1, count + 1)]
    largest = limit if full else min(limit, max(-(-total // count), total * portions[0] // sum(portions)))
    least = 1 if total - largest >= count - 1 else 0
    holding, rest = [largest] + [least] * (count - 1), total - largest - least * (count - 1)
    while rest > 0:
        movable = [i for i in range(1, count) if holding[i] < largest] or [i for i in range(1, count) if holding[i] < limit]
        whole, left = sum([portions[i] for i in movable]), rest
        for i in movable:
            addition = min(limit - holding[i], max(1, left * portions[i] // whole), rest)
            holding[i] = holding[i] + addition
            rest = rest - addition
    return np.array(holding)


def normal_values(key, shape, width, most, pieces=(), held_as=jnp.bfloat16):
    drawn = jax.random.normal(key, shape, jnp.float32) * width
    if len(pieces) > 0:
        drawn = block_levels(key, shape, pieces, -0.22, 0.18) * drawn
    return jnp.clip(drawn, min=-most, max=most).astype(held_as)


def setup_inputs(seed: int = 0) -> dict:
    streams_of = jax.random.split(jax.random.key(seed), 12)
    displacement = normal_values(streams_of[0], (3, 5, 5, 5, NA, NB * EC), 0.1, 0.6, ((4, 16), (5, 8)), jnp.float32)
    velocity = normal_values(streams_of[1], (3, 5, 5, 5, NA, NB * EC), 1.0, 6.0, ((4, 16), (5, 8)), jnp.float32)
    lame_lambda = jnp.clip(0.5 + 1.0 * jax.random.uniform(streams_of[2], (5, 5, 5, NA, NB * EC), jnp.float32) ** block_levels(streams_of[2], (5, 5, 5, NA, NB * EC), ((3, 16), (4, 8)), -0.2, 0.2), 0.5, 1.5)
    shear_modulus = jnp.clip(0.3 + 0.90000004 * jax.random.uniform(streams_of[3], (5, 5, 5, NA, NB * EC), jnp.float32) ** block_levels(streams_of[3], (5, 5, 5, NA, NB * EC), ((3, 16), (4, 8)), -0.2, 0.2), 0.3, 1.2)
    density = jnp.clip(0.7 + 0.7 * jax.random.uniform(streams_of[4], (5, 5, 5, NA, NB * EC), jnp.float32) ** block_levels(streams_of[4], (5, 5, 5, NA, NB * EC), ((3, 16), (4, 8)), -0.2, 0.2), 0.7, 1.4)
    traces = normal_values(streams_of[5], (RECV_TOT, G * 3 * NT), 1.0, 6.0, ((0, 128),))
    section_weights = normal_values(streams_of[6], (STEPS, NT), NT ** -0.5, 0.375)
    owner_keys = jax.random.split(jax.random.fold_in(streams_of[7], 1), RECV_TOT // RECV_DEV)
    owner_turns = jax.random.permutation(jax.random.fold_in(streams_of[7], 3), RECV_TOT // RECV_DEV)
    owner = jax.vmap(lambda own, number: shared_out(jax.random.fold_in(streams_of[7], 2), own, number, RECV_DEV, DEVICES, 1, CAP, 2))(owner_keys, owner_turns).reshape((RECV_TOT, 1))
    element_idx = with_ends(jax.random.randint(streams_of[8], (RECV_TOT,), 0, E_DEV), jax.random.fold_in(streams_of[8], 1), 0, E_DEV - 1).astype(jnp.int32)
    node_weights = normal_values(streams_of[9], (RECV_TOT, 125), 0.3, 1.796875, ((0, 128),))
    encode_bits = with_ends(jax.random.randint(streams_of[10], (RECV_TOT, G), 0, 2), jax.random.fold_in(streams_of[10], 1), 0, 1).astype(jnp.int32)
    return dict(displacement=displacement, velocity=velocity, lame_lambda=lame_lambda, shear_modulus=shear_modulus, density=density, traces=traces, section_weights=section_weights, owner=owner, element_idx=element_idx, node_weights=node_weights, encode_bits=encode_bits)


time_step = 0.025
forward_forms = ['il,cljkabe->cijkabe', 'jl,cilkabe->cijkabe', 'kl,cijlabe->cijkabe']
backward_forms = ['il,cijkabe->cljkabe', 'jl,cijkabe->cilkabe', 'kl,cijkabe->cijlabe']

def tables():
    inner_point = math.sqrt(3.0 / 7.0)
    points = np.array([-1.0, -inner_point, 0.0, inner_point, 1.0])
    weights = np.array([0.1, 49.0 / 90.0, 32.0 / 45.0, 49.0 / 90.0, 0.1])
    legendre = (35.0 * points ** 4 - 30.0 * points ** 2 + 3.0) / 8.0
    derivative = np.zeros((5, 5))
    for i in range(5):
        for j in range(5):
            if i != j:
                derivative[i, j] = legendre[i] / (legendre[j] * (points[i] - points[j]))
    derivative[0, 0] = -5.0
    derivative[4, 4] = 5.0
    quadrature = weights[:, None, None] * weights[None, :, None] * weights[None, None, :] / 8.0
    return (jnp.asarray(2.0 * derivative, jnp.float32), jnp.asarray(quadrature[:, :, :, None, None, None], jnp.float32))

def apply_matrix(form, matrix, field):
    return jnp.einsum(form, matrix, field, precision=lax.Precision.HIGHEST)

def internal(field, lame, shear, matrix, quadrature):
    grads = [apply_matrix(forward_forms[d], matrix, field) for d in range(3)]
    volume = grads[0][0] + grads[1][1] + grads[2][2]
    force = jnp.zeros_like(field)
    for d in range(3):
        stresses = []
        for c in range(3):
            stress = shear * (grads[d][c] + grads[c][d])
            if c == d:
                stress = stress + lame * volume
            stresses.append(stress * quadrature)
        force = force - apply_matrix(backward_forms[d], matrix, jnp.stack(stresses))
    return force

def pair_sum(field, node_dim, elem_dim, fetch):
    face_dim = elem_dim - 1
    count = field.shape[elem_dim]
    low = lax.index_in_dim(field, 0, node_dim, keepdims=False)
    high = lax.index_in_dim(field, 4, node_dim, keepdims=False)
    first_low = lax.slice_in_dim(low, 0, 1, axis=face_dim)
    last_high = lax.slice_in_dim(high, count - 1, count, axis=face_dim)
    from_next, from_prev = fetch(first_low, last_high)
    next_low = jnp.concatenate([lax.slice_in_dim(low, 1, count, axis=face_dim), from_next], face_dim)
    prev_high = jnp.concatenate([from_prev, lax.slice_in_dim(high, 0, count - 1, axis=face_dim)], face_dim)
    middle = lax.slice_in_dim(field, 1, 4, axis=node_dim)
    return jnp.concatenate([jnp.expand_dims(low + prev_high, node_dim), middle, jnp.expand_dims(high + next_low, node_dim)], node_dim)

def no_faces(first_low, last_high):
    return (jnp.zeros_like(first_low), jnp.zeros_like(last_high))

def assemble(field):
    field = pair_sum(field, 1, 4, no_faces)
    field = pair_sum(field, 2, 5, no_faces)
    return pair_sum(field, 3, 6, no_faces)

def to_view(field):
    return field.reshape(field.shape[:-1] + (field.shape[-1] // EC, EC))

def reduce_rows(traces, encode_bits, section_weights):
    rows = traces.shape[0]
    shaped = traces.reshape(rows, G, 3, NT).astype(jnp.float32)
    partial_value = jnp.einsum('rgct,st->rsgc', shaped, section_weights.astype(jnp.float32), precision=lax.Precision.HIGHEST)
    signs = (2 * encode_bits - 1).astype(jnp.float32)
    return lax.optimization_barrier(jnp.sum(partial_value * signs[:, None, :, None], axis=2))

def reference(displacement, velocity, lame_lambda, shear_modulus, density, traces, section_weights, owner, element_idx, node_weights, encode_bits):
    matrix, quadrature = tables()
    lame = to_view(lame_lambda)
    shear = to_view(shear_modulus)
    mass_local = to_view(density) * quadrature
    ones = jnp.ones_like(mass_local)
    stacked = jnp.concatenate([to_view(displacement), to_view(velocity), mass_local[None], ones[None]], 0)
    summed = assemble(stacked)
    count = summed[7]
    disp = summed[0:3] / count
    veloc = summed[3:6] / count
    mass = summed[6]
    sources = reduce_rows(traces, encode_bits, section_weights)
    rows = traces.shape[0]
    term = sources[:, :, :, None] * node_weights.astype(jnp.float32)[:, None, None, :]
    local = EB * EC
    device = owner[:, 0]
    flat = (device // N_SLAB * EA + element_idx // local) * (NB * EC) + device % N_SLAB * local + element_idx % local
    for step in range(STEPS):
        deposit = jnp.zeros((375, NA * NB * EC), jnp.float32).at[:, flat].add(term[:, step].reshape(rows, 375).T)
        deposit = deposit.reshape(3, 5, 5, 5, NA, NB, EC)
        total = assemble(internal(disp, lame, shear, matrix, quadrature) + deposit)
        veloc = veloc + time_step * total / mass
        disp = disp + time_step * veloc
    return (disp.reshape(displacement.shape), veloc.reshape(velocity.shape))
```

```python
import functools
import math

import jax
import jax.numpy as jnp
import numpy as np
from jax import lax
from jax.experimental import pallas as pl
from jax.experimental.pallas import tpu as pltpu
from jax.sharding import PartitionSpec as P

EC = 128
CAP = 4
G = 4
STEPS = 4
DT = 0.025
NODES6 = 150
HI, LO, EL = 160, 176, 192
F32, BF16 = jnp.float32, jnp.bfloat16
MESH = pl.DeviceIdType.MESH


def gll():
    inner_point = math.sqrt(3.0 / 7.0)
    points = np.array([-1.0, -inner_point, 0.0, inner_point, 1.0])
    weights = np.array([0.1, 49.0 / 90.0, 32.0 / 45.0, 49.0 / 90.0, 0.1])
    legendre = (35.0 * points**4 - 30.0 * points**2 + 3.0) / 8.0
    derivative = np.zeros((5, 5))
    for i in range(5):
        for j in range(5):
            if i != j:
                derivative[i, j] = legendre[i] / (legendre[j] * (points[i] - points[j]))
    derivative[0, 0] = -5.0
    derivative[4, 4] = 5.0
    return 2.0 * derivative, weights


D2, WEIGHTS = gll()
FORWARD, BACKWARD = D2, -D2.T


def pack_kernel(devices, traces, weights, owner, element, nodew, bits, out, wsel):
    rows = traces.shape[0]
    nt = weights.shape[1]
    signs = (2 * bits[...] - 1).astype(F32).T.astype(BF16)
    wsel[...] = jnp.zeros_like(wsel)
    for c in range(3):
        wsel[c, c * STEPS : (c + 1) * STEPS, :] = weights[...].astype(F32)
    source = jnp.zeros((rows, 128), F32)
    for g in range(G):
        sign = signs[:, g : g + 1]
        for c in range(3):
            first = (g * 3 + c) * nt
            block = traces[:, first : first + nt] * sign
            source = source + lax.dot_general(
                block,
                wsel[c].astype(BF16),
                (((1,), (1,)), ((), ())),
                preferred_element_type=F32,
            )
    high = source.astype(BF16).astype(F32)
    low = source - high
    lane = lax.broadcasted_iota(jnp.int32, (rows, 128), 1)
    where_el = jnp.broadcast_to(element[...], (128, rows)).astype(F32).T
    el_high = jnp.floor(where_el * (1.0 / 256.0))
    el_low = where_el - 256.0 * el_high
    base = HI - 128
    extra = pltpu.roll(high, base, 1) + pltpu.roll(low, LO - 128, 1)
    extra = jnp.where(lane == EL - 128, el_low, extra)
    extra = jnp.where(lane == EL - 127, el_high, extra)
    node = lax.broadcasted_iota(jnp.int32, (125, 256), 0)
    column = lax.broadcasted_iota(jnp.int32, (125, 256), 1)
    slot6 = (node // 5) * 6 + node % 5
    spread = (column == slot6) | ((node % 5 == 4) & (column == slot6 + 1))
    wide = jnp.dot(nodew[...], spread.astype(F32).astype(BF16), preferred_element_type=F32)
    right = jnp.concatenate([wide[:, :128], wide[:, 128:] + extra], axis=1).astype(BF16)
    device = lax.broadcasted_iota(jnp.int32, (devices, rows), 0)
    member = (owner[...] == device).astype(F32)
    earlier = lax.broadcasted_iota(jnp.int32, (rows, rows), 0) < lax.broadcasted_iota(
        jnp.int32, (rows, rows), 1
    )
    before = jnp.dot(
        member.astype(BF16), earlier.astype(F32).astype(BF16), preferred_element_type=F32
    )
    for k in range(CAP):
        choose = jnp.where(before == float(k), member, 0.0).astype(BF16)
        packed = jnp.dot(choose, right, preferred_element_type=F32)
        out[:, k * 256 : (k + 1) * 256] = packed.astype(BF16)


def line(m, u):
    e0, e1, o0, o1 = u[0] + u[4], u[1] + u[3], u[0] - u[4], u[1] - u[3]
    even, odd = [], []
    for i in range(2):
        ce = [float((m[i, l] + m[i, 4 - l]) / 2) for l in range(2)]
        co = [float((m[i, l] - m[i, 4 - l]) / 2) for l in range(2)]
        even.append(ce[0] * e0 + ce[1] * e1 + float(m[i, 2]) * u[2])
        odd.append(co[0] * o0 + co[1] * o1)
    middle = float(m[2, 0]) * o0 + float(m[2, 1]) * o1
    return [even[0] + odd[0], even[1] + odd[1], middle, odd[1] - even[1], odd[0] - even[0]]


def half_row(lower, upper, half):
    return jnp.where(half == 0, float(lower), float(upper)).astype(F32)


def kline(m, p0, p1, p2, half):
    first = half == 0
    ce = [[(m[i, l] + m[i, 4 - l]) / 2 for l in range(2)] for i in range(2)]
    co = [[(m[i, l] - m[i, 4 - l]) / 2 for l in range(2)] for i in range(2)]
    back = jnp.where(first, p2, p1)
    even, odd = p0 + back, p0 - back
    mid = jnp.where(first, p1, pltpu.roll(p1, 4, 1))
    evens, odds = pltpu.roll(even, 4, 1), pltpu.roll(odd, 4, 1)
    eout = (
        half_row(ce[0][0], ce[1][1], half) * even
        + half_row(ce[0][1], ce[1][0], half) * evens
        + half_row(m[0, 2], m[1, 2], half) * mid
    )
    oout = half_row(co[0][0], co[1][1], half) * odd + half_row(co[0][1], co[1][0], half) * odds
    q0 = eout + oout
    q43 = oout - eout
    q22 = half_row(m[2, 0], m[2, 1], half) * odd + half_row(m[2, 1], m[2, 0], half) * odds
    q1 = jnp.where(first, q22, q43)
    q2 = jnp.where(first, q43, pltpu.roll(q43, 4, 1))
    return q0, q1, q2


SIDES = [(-1, 0), (1, 0), (0, -1), (0, 1), (-1, -1), (-1, 1), (1, -1), (1, 1)]
OPPOSITE = [1, 0, 3, 2, 7, 6, 5, 4]


def message_rows(side, comps):
    if side < 4:
        return comps * 8
    return comps + (comps + 1) // 2


def step_kernel(
    nd,
    ns,
    disp,
    veloc,
    lame,
    shear,
    density,
    got,
    disp_out,
    veloc_out,
    U,
    W,
    LAM,
    MU,
    CM,
    GR,
    SG,
    F,
    DEP,
    TT,
    OH,
    *rest,
):
    send, recv = rest[0:8], rest[8:16]
    send_sem, recv_sem = rest[16], rest[17]
    dom, slab = lax.axis_index("dom"), lax.axis_index("slab")

    def exists(side):
        da, db = SIDES[side]
        cond = None
        for shift, index, count in ((da, dom, nd), (db, slab, ns)):
            if shift:
                one = index > 0 if shift < 0 else index < count - 1
                cond = one if cond is None else jnp.logical_and(cond, one)
        return cond

    def target(side):
        return (dom + SIDES[side][0], slab + SIDES[side][1])

    for side in range(8):
        recv[side][...] = jnp.zeros_like(recv[side])
    barrier = pltpu.get_barrier_semaphore()
    count = 0
    for side in range(8):
        count = count + exists(side).astype(jnp.int32)

        @pl.when(exists(side))
        def _():
            pl.semaphore_signal(barrier, inc=1, device_id=target(side), device_id_type=MESH)

    sub = lax.broadcasted_iota(jnp.int32, (1, 8, 128), 1)
    lane = lax.broadcasted_iota(jnp.int32, (1, 8, 128), 2)
    half, bit_b, bit_a = sub // 4, (sub // 2) % 2, sub % 2

    def roll_s(x, shift):
        return pltpu.roll(x, shift % 8, 1)

    def roll_l(x, shift):
        return pltpu.roll(x, shift % 128, 2)

    def load_pairs(dst, src):
        lead = (slice(None),) * (len(dst.shape) - 3)
        for kp in range(3):
            dst[lead + (kp, slice(0, 4))] = src[lead + (2 * kp,)]
            dst[lead + (kp, slice(4, 8))] = src[lead + (min(2 * kp + 1, 4),)]

    def store_pairs(dst, src):
        lead = (slice(None),) * (len(src.shape) - 3)
        for k in range(5):
            first = 4 * (k % 2)
            dst[lead + (k,)] = src[lead + (k // 2, slice(first, first + 4))]

    def local_sums(comps):
        for c in range(comps):
            for i in range(5):
                p0, p2 = F[c, i, :, 0], F[c, i, :, 2]
                dup = jnp.where(half == 0, p0, roll_s(p0, 4))
                F[c, i, :, 0] = p0 + jnp.where((half == 0) & (lane > 0), roll_l(p2, 1), 0.0)
                F[c, i, :, 2] = p2 + jnp.where(lane < 127, roll_l(dup, -1), 0.0)
            for j in range(5):
                x0, x4 = F[c, 0, j], F[c, 4, j]
                F[c, 0, j] = x0 + jnp.where(bit_a == 1, roll_s(x4, 1), 0.0)
                F[c, 4, j] = x4 + jnp.where(bit_a == 0, roll_s(x0, -1), 0.0)
            for i in range(5):
                x0, x4 = F[c, i, 0], F[c, i, 4]
                F[c, i, 0] = x0 + jnp.where(bit_b == 1, roll_s(x4, 2), 0.0)
                F[c, i, 4] = x4 + jnp.where(bit_b == 0, roll_s(x0, -2), 0.0)

    def merge(x, y, bit, width, value):
        toward = width if value == 0 else -width
        return jnp.where(bit == value, x, roll_s(y, toward))

    def pack(comps, slot):
        for side in range(4):
            axis, value = side // 2, side % 2
            bit, width = ((bit_a, 1), (bit_b, 2))[axis]
            node = 4 * value
            buf = send[side]
            for c in range(comps):
                if axis == 0:
                    faces = [F[c, node, :, kp] for kp in range(3)]
                else:
                    faces = [F[c, :, node, kp] for kp in range(3)]
                buf[slot, c * 8 : c * 8 + 5] = merge(faces[0], faces[1], bit, width, value)
                z = faces[2]
                for n, (x, y) in enumerate(((0, 1), (2, 3), (4, 4))):
                    buf[slot, c * 8 + 5 + n : c * 8 + 6 + n] = merge(
                        z[x : x + 1], z[y : y + 1], bit, width, value
                    )
        for side in range(4, 8):
            da, db = SIDES[side]
            va, vb = (da + 1) // 2, (db + 1) // 2
            buf = send[side]
            for c in range(comps):
                x = F[c, 4 * va, 4 * vb]
                buf[slot, c : c + 1] = merge(x[0:1], x[1:2], bit_a, 1, va)
            for n in range((comps + 1) // 2):
                x = F[2 * n, 4 * va, 4 * vb, 2:3]
                y = F[min(2 * n + 1, comps - 1), 4 * va, 4 * vb, 2:3]
                buf[slot, comps + n : comps + n + 1] = merge(x, y, bit_a, 1, va)

    def unmerge(m, bit, width, value):
        toward = -width if value == 0 else width
        keep = bit == value
        return jnp.where(keep, roll_s(m, toward), 0.0), jnp.where(keep, m, 0.0)

    def unpack(comps, slot):
        for side in range(4):
            axis, value = side // 2, side % 2
            bit, width = ((bit_a, 1), (bit_b, 2))[axis]
            node = 4 * value
            buf = recv[side]
            for c in range(comps):
                adds = list(unmerge(buf[slot, c * 8 : c * 8 + 5], bit, width, value))
                pieces = []
                for n in range(3):
                    pieces.extend(
                        unmerge(buf[slot, c * 8 + 5 + n : c * 8 + 6 + n], bit, width, value)
                    )
                adds.append(jnp.concatenate(pieces[:5], axis=0))
                for kp in range(3):
                    if axis == 0:
                        F[c, node, :, kp] = F[c, node, :, kp] + adds[kp]
                    else:
                        F[c, :, node, kp] = F[c, :, node, kp] + adds[kp]
        for side in range(4, 8):
            da, db = SIDES[side]
            va, vb = (da + 1) // 2, (db + 1) // 2
            buf = recv[side]
            keep = bit_b == vb
            toward = -2 if vb == 0 else 2
            for n in range(message_rows(side, comps)):
                x, y = unmerge(buf[slot, n : n + 1], bit_a, 1, va)
                x = jnp.where(keep, roll_s(x, toward), 0.0)
                y = jnp.where(keep, roll_s(y, toward), 0.0)
                if n < comps:
                    at = [(n, 0, x), (n, 1, y)]
                else:
                    first = 2 * (n - comps)
                    at = [(first, 2, x)]
                    if first + 1 < comps:
                        at.append((first + 1, 2, y))
                for c, kp, v in at:
                    F[c, 4 * va, 4 * vb, kp : kp + 1] = F[c, 4 * va, 4 * vb, kp : kp + 1] + v

    def copy(side, comps, slot):
        rows = message_rows(side, comps)
        return pltpu.make_async_remote_copy(
            src_ref=send[side].at[slot, pl.ds(0, rows)],
            dst_ref=recv[OPPOSITE[side]].at[slot, pl.ds(0, rows)],
            send_sem=send_sem.at[side, slot],
            recv_sem=recv_sem.at[OPPOSITE[side], slot],
            device_id=target(side),
            device_id_type=MESH,
        )

    def arrival(side, comps, slot):
        rows = message_rows(side, comps)
        return pltpu.make_async_remote_copy(
            src_ref=send[side].at[slot, pl.ds(0, rows)],
            dst_ref=recv[side].at[slot, pl.ds(0, rows)],
            send_sem=send_sem.at[side, slot],
            recv_sem=recv_sem.at[side, slot],
            device_id=target(side),
            device_id_type=MESH,
        )

    def start(comps, slot):
        for side in range(8):

            @pl.when(exists(side))
            def _():
                copy(side, comps, slot).start()

    def finish(comps, slot):
        for side in range(8):

            @pl.when(exists(side))
            def _():
                arrival(side, comps, slot).wait()

    def quad(i, j):
        w = WEIGHTS
        scale = w[i] * w[j] / 8.0
        return jnp.concatenate(
            [half_row(scale * w[2 * kp], scale * w[min(2 * kp + 1, 4)], half) for kp in range(3)],
            axis=0,
        )

    def share(i, j):
        one = jnp.ones((1, 8, 128), F32)

        def along(n, bit, index, devices):
            if n == 0:
                return jnp.where((bit == 1) | (index > 0), 0.5, 1.0)
            if n == 4:
                return jnp.where((bit == 0) | (index < devices - 1), 0.5, 1.0)
            return one

        ab = along(i, bit_a, dom, nd) * along(j, bit_b, slab, ns)
        k0 = jnp.where((half == 0) & (lane > 0), 0.5, 1.0)
        k4 = jnp.where(lane < 127, 0.5, 1.0)
        return jnp.concatenate([ab * k0, ab * one, ab * k4], axis=0)

    load_pairs(U, disp)
    load_pairs(W, veloc)
    load_pairs(LAM, lame)
    load_pairs(MU, shear)
    load_pairs(CM, density)
    for i in range(5):
        for j in range(5):
            q = quad(i, j)
            F[3, i, j] = CM[i, j] * q
            LAM[i, j] = LAM[i, j] * q
            MU[i, j] = MU[i, j] * q
            for c in range(3):
                F[c, i, j] = U[c, i, j]
    local_sums(4)
    pack(4, 0)
    pl.semaphore_wait(barrier, count)
    start(4, 0)

    slots = got.shape[0]
    for k in range(CAP):
        block = got[:, k * 256 : (k + 1) * 256].astype(F32)
        TT[:, k * slots : (k + 1) * slots] = block.T
        el = block[:, EL : EL + 1] + 256.0 * block[:, EL + 1 : EL + 2]
        cols = lax.broadcasted_iota(jnp.int32, (slots, 512), 1)
        OH[k * slots : (k + 1) * slots, :] = (
            (cols == el.astype(jnp.int32)).astype(F32).astype(BF16)
        )

    def deposit(s):
        for c in range(3):
            row = c * STEPS + s
            src = TT[pl.ds(HI + row, 1), :] + TT[pl.ds(LO + row, 1), :]
            term = TT[0:152, :] * src
            high = term.astype(BF16)
            low = (term - high.astype(F32)).astype(BF16)
            sums = jnp.dot(high, OH[...], preferred_element_type=F32) + jnp.dot(
                low, OH[...], preferred_element_type=F32
            )
            for a in range(2):
                for b in range(2):
                    q, first = b * 2 + a, (a * 2 + b) * 128
                    DEP[pl.ds(c * 600 + q, NODES6, stride=4), :] = sums[
                        0:NODES6, first : first + 128
                    ]

    deposit(0)
    finish(4, 0)
    unpack(4, 0)
    for i in range(5):
        for j in range(5):
            part = share(i, j)
            mass = F[3, i, j]
            CM[i, j] = (DT * DT) / mass
            scaled = mass * part * (1.0 / DT)
            for c in range(3):
                U[c, i, j] = F[c, i, j] * part
                at = (c * 75 + (i * 5 + j) * 3) * 8
                DEP[at : at + 24, :] = DEP[at : at + 24, :] + (W[c, i, j] * scaled).reshape(
                    24, 128
                )
                W[c, i, j] = jnp.zeros((3, 8, 128), F32)

    pair = {(0, 0): 0, (1, 1): 1, (2, 2): 2, (0, 1): 3, (0, 2): 4, (1, 2): 5}

    def stress(c, d):
        return pair[(min(c, d), max(c, d))]

    def one_step(s, carry):
        for c in range(3):
            for j in range(5):
                outs = line(FORWARD, [U[c, i, j] for i in range(5)])
                for i in range(5):
                    GR[0, c, i, j] = outs[i]
            for i in range(5):
                outs = line(FORWARD, [U[c, i, j] for j in range(5)])
                for j in range(5):
                    GR[1, c, i, j] = outs[j]
                outs = kline(FORWARD, U[c, i, :, 0], U[c, i, :, 1], U[c, i, :, 2], half)
                for kp in range(3):
                    GR[2, c, i, :, kp] = outs[kp]
        for i in range(5):
            for j in range(5):
                g = [[GR[d, c, i, j] for c in range(3)] for d in range(3)]
                mu = MU[i, j]
                mu2 = mu + mu
                vol = LAM[i, j] * (g[0][0] + g[1][1] + g[2][2])
                for c in range(3):
                    SG[c, i, j] = mu2 * g[c][c] + vol
                    for d in range(c):
                        SG[stress(c, d), i, j] = mu * (g[c][d] + g[d][c])
        for c in range(3):
            for j in range(5):
                outs = line(BACKWARD, [SG[stress(c, 0), i, j] for i in range(5)])
                for i in range(5):
                    at = (c * 75 + (i * 5 + j) * 3) * 8
                    F[c, i, j] = outs[i] + DEP[at : at + 24, :].reshape(3, 8, 128)
            for i in range(5):
                outs = line(BACKWARD, [SG[stress(c, 1), i, j] for j in range(5)])
                for j in range(5):
                    F[c, i, j] = F[c, i, j] + outs[j]
                p = stress(c, 2)
                outs = kline(BACKWARD, SG[p, i, :, 0], SG[p, i, :, 1], SG[p, i, :, 2], half)
                for kp in range(3):
                    F[c, i, :, kp] = F[c, i, :, kp] + outs[kp]
        slot = (s + 1) % 2
        local_sums(3)
        pack(3, slot)
        start(3, slot)

        @pl.when(s < STEPS - 1)
        def _():
            deposit(s + 1)

        finish(3, slot)
        unpack(3, slot)
        for i in range(5):
            for j in range(5):
                cm = CM[i, j]
                for c in range(3):
                    w = W[c, i, j] + F[c, i, j] * cm
                    W[c, i, j] = w
                    U[c, i, j] = U[c, i, j] + w
        return carry

    lax.fori_loop(0, STEPS, one_step, 0)
    for i in range(5):
        for j in range(5):
            for c in range(3):
                W[c, i, j] = W[c, i, j] * (1.0 / DT)
    store_pairs(disp_out, U)
    store_pairs(veloc_out, W)


def to_rows(x):
    lead = x.shape[:-2]
    n = len(lead)
    y = x.reshape(lead + (2, 2, EC))
    return jnp.swapaxes(y, n, n + 1).reshape(lead + (4, EC))


def from_rows(x):
    lead = x.shape[:-2]
    n = len(lead)
    y = jnp.swapaxes(x.reshape(lead + (2, 2, EC)), n, n + 1)
    return y.reshape(lead + (2, 2 * EC))


def shards(
    nd,
    ns,
    displacement,
    velocity,
    lame_lambda,
    shear_modulus,
    density,
    traces,
    section_weights,
    owner,
    element_idx,
    node_weights,
    encode_bits,
):
    devices = nd * ns
    rows = traces.shape[0]
    payload = pl.pallas_call(
        functools.partial(pack_kernel, devices),
        out_shape=jax.ShapeDtypeStruct((devices, CAP * 256), BF16),
        scratch_shapes=[pltpu.VMEM((3, 128, section_weights.shape[1]), F32)],
        name="pack_rows",
    )(
        traces,
        section_weights,
        owner.reshape(1, rows),
        element_idx.reshape(1, rows),
        node_weights,
        encode_bits.T,
    )
    got = lax.all_to_all(payload, ("dom", "slab"), split_axis=0, concat_axis=0, tiled=True)
    field = (5, 5, 3, 8, 128)
    vm = lambda *shape: pltpu.VMEM(shape, F32)
    messages = [vm(2, message_rows(side, 4), 8, 128) for side in range(8)]
    out = jax.ShapeDtypeStruct((3, 5, 5, 5, 4, EC), F32)
    disp, veloc = pl.pallas_call(
        functools.partial(step_kernel, nd, ns),
        out_shape=(out, out),
        scratch_shapes=[
            vm(3, *field),
            vm(3, *field),
            vm(*field),
            vm(*field),
            vm(*field),
            vm(3, 3, *field),
            vm(6, *field),
            vm(4, *field),
            vm(1808, 128),
            vm(256, CAP * devices),
            pltpu.VMEM((CAP * devices, 512), BF16),
            *messages,
            *messages,
            pltpu.SemaphoreType.DMA((8, 2)),
            pltpu.SemaphoreType.DMA((8, 2)),
        ],
        compiler_params=pltpu.CompilerParams(collective_id=1, has_side_effects=True),
        name="time_steps",
    )(
        to_rows(displacement),
        to_rows(velocity),
        to_rows(lame_lambda),
        to_rows(shear_modulus),
        to_rows(density),
        got,
    )
    return from_rows(disp), from_rows(veloc)


def solution(mesh):
    nd, ns = mesh.shape["dom"], mesh.shape["slab"]
    both = P(("dom", "slab"), None)
    fields = P(None, None, None, None, "dom", "slab")
    params = P(None, None, None, "dom", "slab")
    return jax.shard_map(
        functools.partial(shards, nd, ns),
        mesh=mesh,
        in_specs=(
            fields,
            fields,
            params,
            params,
            params,
            both,
            P(),
            both,
            P(("dom", "slab")),
            both,
            both,
        ),
        out_specs=(fields, fields),
        check_vma=False,
    )
```

```python
import functools
import math

import jax
import jax.numpy as jnp
import numpy as np
from jax import lax
from jax.experimental import pallas as pl
from jax.experimental.pallas import tpu as pltpu
from jax.sharding import PartitionSpec as P

EC = 128
CAP = 4
G = 4
STEPS = 4
DT = 0.025
NODES6 = 150
HI, LO, EL = 160, 176, 192
F32, BF16 = jnp.float32, jnp.bfloat16
MESH = pl.DeviceIdType.MESH


def gll():
    inner_point = math.sqrt(3.0 / 7.0)
    points = np.array([-1.0, -inner_point, 0.0, inner_point, 1.0])
    weights = np.array([0.1, 49.0 / 90.0, 32.0 / 45.0, 49.0 / 90.0, 0.1])
    legendre = (35.0 * points**4 - 30.0 * points**2 + 3.0) / 8.0
    derivative = np.zeros((5, 5))
    for i in range(5):
        for j in range(5):
            if i != j:
                derivative[i, j] = legendre[i] / (legendre[j] * (points[i] - points[j]))
    derivative[0, 0] = -5.0
    derivative[4, 4] = 5.0
    return 2.0 * derivative, weights


D2, WEIGHTS = gll()
FORWARD, BACKWARD = D2, -D2.T


def pack_kernel(devices, traces, weights, owner, element, nodew, bits, out, wsel):
    rows = traces.shape[0]
    nt = weights.shape[1]
    signs = (2 * bits[...] - 1).astype(F32).T.astype(BF16)
    wsel[...] = jnp.zeros_like(wsel)
    for c in range(3):
        wsel[c, c * STEPS : (c + 1) * STEPS, :] = weights[...].astype(F32)
    source = jnp.zeros((rows, 128), F32)
    for g in range(G):
        sign = signs[:, g : g + 1]
        for c in range(3):
            first = (g * 3 + c) * nt
            block = traces[:, first : first + nt] * sign
            source = source + lax.dot_general(
                block,
                wsel[c].astype(BF16),
                (((1,), (1,)), ((), ())),
                preferred_element_type=F32,
            )
    high = source.astype(BF16).astype(F32)
    low = source - high
    lane = lax.broadcasted_iota(jnp.int32, (rows, 128), 1)
    where_el = jnp.broadcast_to(element[...], (128, rows)).astype(F32).T
    el_high = jnp.floor(where_el * (1.0 / 256.0))
    el_low = where_el - 256.0 * el_high
    base = HI - 128
    extra = pltpu.roll(high, base, 1) + pltpu.roll(low, LO - 128, 1)
    extra = jnp.where(lane == EL - 128, el_low, extra)
    extra = jnp.where(lane == EL - 127, el_high, extra)
    node = lax.broadcasted_iota(jnp.int32, (125, 256), 0)
    column = lax.broadcasted_iota(jnp.int32, (125, 256), 1)
    slot6 = (node // 5) * 6 + node % 5
    spread = (column == slot6) | ((node % 5 == 4) & (column == slot6 + 1))
    wide = jnp.dot(nodew[...], spread.astype(F32).astype(BF16), preferred_element_type=F32)
    right = jnp.concatenate([wide[:, :128], wide[:, 128:] + extra], axis=1).astype(BF16)
    device = lax.broadcasted_iota(jnp.int32, (devices, rows), 0)
    member = (owner[...] == device).astype(F32)
    earlier = lax.broadcasted_iota(jnp.int32, (rows, rows), 0) < lax.broadcasted_iota(
        jnp.int32, (rows, rows), 1
    )
    before = jnp.dot(
        member.astype(BF16), earlier.astype(F32).astype(BF16), preferred_element_type=F32
    )
    for k in range(CAP):
        choose = jnp.where(before == float(k), member, 0.0).astype(BF16)
        packed = jnp.dot(choose, right, preferred_element_type=F32)
        out[:, k * 256 : (k + 1) * 256] = packed.astype(BF16)


def line(m, u):
    e0, e1, o0, o1 = u[0] + u[4], u[1] + u[3], u[0] - u[4], u[1] - u[3]
    even, odd = [], []
    for i in range(2):
        ce = [float((m[i, l] + m[i, 4 - l]) / 2) for l in range(2)]
        co = [float((m[i, l] - m[i, 4 - l]) / 2) for l in range(2)]
        even.append(ce[0] * e0 + ce[1] * e1 + float(m[i, 2]) * u[2])
        odd.append(co[0] * o0 + co[1] * o1)
    middle = float(m[2, 0]) * o0 + float(m[2, 1]) * o1
    return [even[0] + odd[0], even[1] + odd[1], middle, odd[1] - even[1], odd[0] - even[0]]


def half_row(lower, upper, half):
    return jnp.where(half == 0, float(lower), float(upper)).astype(F32)


def kline(m, p0, p1, p2, half):
    first = half == 0
    ce = [[(m[i, l] + m[i, 4 - l]) / 2 for l in range(2)] for i in range(2)]
    co = [[(m[i, l] - m[i, 4 - l]) / 2 for l in range(2)] for i in range(2)]
    back = jnp.where(first, p2, p1)
    even, odd = p0 + back, p0 - back
    mid = jnp.where(first, p1, pltpu.roll(p1, 4, 1))
    evens, odds = pltpu.roll(even, 4, 1), pltpu.roll(odd, 4, 1)
    eout = (
        half_row(ce[0][0], ce[1][1], half) * even
        + half_row(ce[0][1], ce[1][0], half) * evens
        + half_row(m[0, 2], m[1, 2], half) * mid
    )
    oout = half_row(co[0][0], co[1][1], half) * odd + half_row(co[0][1], co[1][0], half) * odds
    q0 = eout + oout
    q43 = oout - eout
    q22 = half_row(m[2, 0], m[2, 1], half) * odd + half_row(m[2, 1], m[2, 0], half) * odds
    q1 = jnp.where(first, q22, q43)
    q2 = jnp.where(first, q43, pltpu.roll(q43, 4, 1))
    return q0, q1, q2


SIDES = [(-1, 0), (1, 0), (0, -1), (0, 1), (-1, -1), (-1, 1), (1, -1), (1, 1)]
OPPOSITE = [1, 0, 3, 2, 7, 6, 5, 4]


GROUPS = {3: ((0, 1, 2),), 4: ((0, 1, 2), (3,))}


def tiles_of(group):
    return (5 * len(group) + 2) // 2


def sizes(comps):
    groups = GROUPS[comps]
    return sum(tiles_of(g) for g in groups), len(groups), (comps + 2) // 2


def step_kernel(
    nd,
    ns,
    disp,
    veloc,
    lame,
    shear,
    density,
    got,
    disp_out,
    veloc_out,
    U,
    W,
    LAM,
    MU,
    CM,
    GR,
    SG,
    F,
    DEP,
    TT,
    OH,
    *rest,
):
    send, recv = rest[0:8], rest[8:16]
    send_scale, recv_scale = rest[16:20], rest[20:24]
    send_sem, recv_sem = rest[24], rest[25]
    dom, slab = lax.axis_index("dom"), lax.axis_index("slab")

    def exists(side):
        da, db = SIDES[side]
        cond = None
        for shift, index, count in ((da, dom, nd), (db, slab, ns)):
            if shift:
                one = index > 0 if shift < 0 else index < count - 1
                cond = one if cond is None else jnp.logical_and(cond, one)
        return cond

    def target(side):
        return (dom + SIDES[side][0], slab + SIDES[side][1])

    for side in range(8):
        recv[side][...] = jnp.zeros_like(recv[side])
        if side < 4:
            recv_scale[side][...] = jnp.zeros_like(recv_scale[side])
    barrier = pltpu.get_barrier_semaphore()
    count = 0
    for side in range(8):
        count = count + exists(side).astype(jnp.int32)

        @pl.when(exists(side))
        def _():
            pl.semaphore_signal(barrier, inc=1, device_id=target(side), device_id_type=MESH)

    sub = lax.broadcasted_iota(jnp.int32, (1, 8, 128), 1)
    lane = lax.broadcasted_iota(jnp.int32, (1, 8, 128), 2)
    half, bit_b, bit_a = sub // 4, (sub // 2) % 2, sub % 2

    def roll_s(x, shift):
        return pltpu.roll(x, shift % 8, 1)

    def roll_l(x, shift):
        return pltpu.roll(x, shift % 128, 2)

    def load_pairs(dst, src):
        lead = (slice(None),) * (len(dst.shape) - 3)
        for kp in range(3):
            dst[lead + (kp, slice(0, 4))] = src[lead + (2 * kp,)]
            dst[lead + (kp, slice(4, 8))] = src[lead + (min(2 * kp + 1, 4),)]

    def store_pairs(dst, src):
        lead = (slice(None),) * (len(src.shape) - 3)
        for k in range(5):
            first = 4 * (k % 2)
            dst[lead + (k,)] = src[lead + (k // 2, slice(first, first + 4))]

    def local_sums(comps):
        for c in range(comps):
            for i in range(5):
                p0, p2 = F[c, i, :, 0], F[c, i, :, 2]
                F[c, i, :, 0] = p0 + jnp.where((half == 0) & (lane > 0), roll_l(p2, 1), 0.0)
            for j in range(5):
                x0, x4 = F[c, 0, j], F[c, 4, j]
                F[c, 0, j] = x0 + jnp.where(bit_a == 1, roll_s(x4, 1), 0.0)
                F[c, 4, j] = x4 + jnp.where(bit_a == 0, roll_s(x0, -1), 0.0)
            for i in range(5):
                x0, x4 = F[c, i, 0], F[c, i, 4]
                F[c, i, 0] = x0 + jnp.where(bit_b == 1, roll_s(x4, 2), 0.0)
                F[c, i, 4] = x4 + jnp.where(bit_b == 0, roll_s(x0, -2), 0.0)

    def close_k(x):
        x0 = x[0:1]
        dup = jnp.where(half == 0, x0, roll_s(x0, 4))
        x2 = jnp.where(lane < 127, roll_l(dup, -1), x[2:3])
        return jnp.concatenate([x[0:2], x2], axis=0)

    def merge(x, y, bit, width, value):
        toward = width if value == 0 else -width
        return jnp.where(bit == value, x, roll_s(y, toward))

    def unmerge(m, bit, width, value):
        toward = -width if value == 0 else width
        keep = bit == value
        return jnp.where(keep, roll_s(m, toward), 0.0), jnp.where(keep, m, 0.0)

    def ends(zs):
        out = jnp.zeros((1, 8, 128), F32)
        for n, z in enumerate(zs):
            out = jnp.where(lane == n, roll_l(z, n + 1), out)
        return out

    def end_of(row, n):
        return jnp.where(lane == 127, roll_l(row, 127 - n), 0.0)

    def face(side):
        axis, value = side // 2, side % 2
        bit, width = ((bit_a, 1), (bit_b, 2))[axis]
        node = 4 * value

        def at(c, n, kp):
            return (c, node, n, kp) if axis == 0 else (c, n, node, kp)

        def line_at(c, kp):
            return (c, node, slice(None), kp) if axis == 0 else (c, slice(None), node, kp)

        return bit, width, value, at, line_at

    def pack(comps, slot):
        for side in range(4):
            bit, width, value, at, line_at = face(side)
            tile = 0
            for g, group in enumerate(GROUPS[comps]):
                rows = []
                for c in group:
                    merged = merge(F[line_at(c, 0)], F[line_at(c, 1)], bit, width, value)
                    rows.extend(merged[n : n + 1] for n in range(5))
                rows.append(ends([F[at(c, n, 2)][None] for c in group for n in range(5)]))
                largest = jnp.abs(rows[0])
                for row in rows[1:]:
                    largest = jnp.maximum(largest, jnp.abs(row))
                scale = largest * (1.0 / 32000.0) + 1e-30
                send_scale[side][slot, g : g + 1] = scale
                inverse = 1.0 / scale
                for n in range(0, len(rows), 2):
                    x = jnp.concatenate([rows[n][0] * inverse[0], rows[n + 1][0] * inverse[0]], 0)
                    x = x + jnp.where(x < 0.0, -0.5, 0.5)
                    send[side][slot, tile] = x.astype(jnp.int32).astype(jnp.int16)
                    tile += 1
        for side in range(4, 8):
            da, db = SIDES[side]
            va, vb = (da + 1) // 2, (db + 1) // 2
            items = []
            for c in range(comps):
                x = F[c, 4 * va, 4 * vb]
                items.append(merge(x[0:1], x[1:2], bit_a, 1, va))
            items.append(ends([F[c, 4 * va, 4 * vb, 2:3] for c in range(comps)]))
            for n in range(0, len(items), 2):
                y = items[min(n + 1, len(items) - 1)]
                send[side][slot, n // 2 : n // 2 + 1] = merge(items[n], y, bit_b, 2, vb)

    def unpack(comps, slot):
        for side in range(4):
            bit, width, value, at, line_at = face(side)
            tile = 0
            for g, group in enumerate(GROUPS[comps]):
                scale = recv_scale[side][slot, g : g + 1]
                rows = []
                for _ in range(tiles_of(group)):
                    x = recv[side][slot, tile].astype(jnp.int32).astype(F32)
                    rows.extend([x[None, 0:8] * scale, x[None, 8:16] * scale])
                    tile += 1
                for m, c in enumerate(group):
                    merged = jnp.concatenate(rows[5 * m : 5 * m + 5], axis=0)
                    for kp, add in enumerate(unmerge(merged, bit, width, value)):
                        F[line_at(c, kp)] = F[line_at(c, kp)] + add
                last, _ = unmerge(rows[5 * len(group)], bit, width, value)
                for m, c in enumerate(group):
                    for n in range(5):
                        F[at(c, n, 2)] = F[at(c, n, 2)] + end_of(last, 5 * m + n)[0]
        for side in range(4, 8):
            da, db = SIDES[side]
            va, vb = (da + 1) // 2, (db + 1) // 2
            items = []
            for n in range(sizes(comps)[2]):
                items.extend(unmerge(recv[side][slot, n : n + 1], bit_b, 2, vb))
            last, _ = unmerge(items[comps], bit_a, 1, va)
            for c in range(comps):
                x, y = unmerge(items[c], bit_a, 1, va)
                add = jnp.concatenate([x, y, end_of(last, c)], axis=0)
                F[c, 4 * va, 4 * vb] = F[c, 4 * va, 4 * vb] + add

    def copies(side, comps, slot, source):
        tiles, scales, rows = sizes(comps)
        parts = [(send, recv, tiles, side)] if side < 4 else [(send, recv, rows, side)]
        if side < 4:
            parts.append((send_scale, recv_scale, scales, 8 + side))
        out = []
        for src, dst, count, number in parts:
            there = number - side + OPPOSITE[side] if source else number
            out.append(
                pltpu.make_async_remote_copy(
                    src_ref=src[side].at[slot, pl.ds(0, count)],
                    dst_ref=dst[OPPOSITE[side] if source else side].at[slot, pl.ds(0, count)],
                    send_sem=send_sem.at[number, slot],
                    recv_sem=recv_sem.at[there, slot],
                    device_id=target(side),
                    device_id_type=MESH,
                )
            )
        return out

    def start(comps, slot):
        for side in (0, 1, 2, 3, 4, 5, 6, 7):

            @pl.when(exists(side))
            def _():
                for one in copies(side, comps, slot, True):
                    one.start()

    def finish(comps, slot):
        for side in range(8):

            @pl.when(exists(side))
            def _():
                for one in copies(side, comps, slot, False):
                    one.wait()

    def quad(i, j):
        w = WEIGHTS
        scale = w[i] * w[j] / 8.0
        return jnp.concatenate(
            [half_row(scale * w[2 * kp], scale * w[min(2 * kp + 1, 4)], half) for kp in range(3)],
            axis=0,
        )

    def share(i, j):
        one = jnp.ones((1, 8, 128), F32)

        def along(n, bit, index, devices):
            if n == 0:
                return jnp.where((bit == 1) | (index > 0), 0.5, 1.0)
            if n == 4:
                return jnp.where((bit == 0) | (index < devices - 1), 0.5, 1.0)
            return one

        ab = along(i, bit_a, dom, nd) * along(j, bit_b, slab, ns)
        k0 = jnp.where((half == 0) & (lane > 0), 0.5, 1.0)
        k4 = jnp.where(lane < 127, 0.5, 1.0)
        return jnp.concatenate([ab * k0, ab * one, ab * k4], axis=0)

    load_pairs(U, disp)
    load_pairs(W, veloc)
    load_pairs(LAM, lame)
    load_pairs(MU, shear)
    load_pairs(CM, density)
    for i in range(5):
        for j in range(5):
            q = quad(i, j)
            F[3, i, j] = CM[i, j] * q
            LAM[i, j] = LAM[i, j] * q
            MU[i, j] = MU[i, j] * q
            for c in range(3):
                F[c, i, j] = U[c, i, j]
    local_sums(4)
    pack(4, 0)
    pl.semaphore_wait(barrier, count)
    start(4, 0)

    slots = got.shape[0]
    for k in range(CAP):
        block = got[:, k * 256 : (k + 1) * 256].astype(F32)
        TT[:, k * slots : (k + 1) * slots] = block.T
        el = block[:, EL : EL + 1] + 256.0 * block[:, EL + 1 : EL + 2]
        cols = lax.broadcasted_iota(jnp.int32, (slots, 512), 1)
        OH[k * slots : (k + 1) * slots, :] = (
            (cols == el.astype(jnp.int32)).astype(F32).astype(BF16)
        )

    def deposit(s):
        for c in range(3):
            row = c * STEPS + s
            src = TT[pl.ds(HI + row, 1), :] + TT[pl.ds(LO + row, 1), :]
            term = TT[0:152, :] * src
            high = term.astype(BF16)
            low = (term - high.astype(F32)).astype(BF16)
            sums = jnp.dot(high, OH[...], preferred_element_type=F32) + jnp.dot(
                low, OH[...], preferred_element_type=F32
            )
            for a in range(2):
                for b in range(2):
                    q, first = b * 2 + a, (a * 2 + b) * 128
                    DEP[pl.ds(c * 600 + q, NODES6, stride=4), :] = sums[
                        0:NODES6, first : first + 128
                    ]

    deposit(0)
    finish(4, 0)
    unpack(4, 0)
    for i in range(5):
        for j in range(5):
            part = share(i, j)
            mass = close_k(F[3, i, j])
            CM[i, j] = (DT * DT) / mass
            scaled = mass * part * (1.0 / DT)
            for c in range(3):
                U[c, i, j] = close_k(F[c, i, j]) * part
                at = (c * 75 + (i * 5 + j) * 3) * 8
                DEP[at : at + 24, :] = DEP[at : at + 24, :] + (W[c, i, j] * scaled).reshape(
                    24, 128
                )
                W[c, i, j] = jnp.zeros((3, 8, 128), F32)

    pair = {(0, 0): 0, (1, 1): 1, (2, 2): 2, (0, 1): 3, (0, 2): 4, (1, 2): 5}

    def stress(c, d):
        return pair[(min(c, d), max(c, d))]

    def one_step(s, carry):
        for c in range(3):
            for j in range(5):
                outs = line(FORWARD, [U[c, i, j] for i in range(5)])
                for i in range(5):
                    GR[0, c, i, j] = outs[i]
            for i in range(5):
                outs = line(FORWARD, [U[c, i, j] for j in range(5)])
                for j in range(5):
                    GR[1, c, i, j] = outs[j]
                outs = kline(FORWARD, U[c, i, :, 0], U[c, i, :, 1], U[c, i, :, 2], half)
                for kp in range(3):
                    GR[2, c, i, :, kp] = outs[kp]
        for i in range(5):
            for j in range(5):
                g = [[GR[d, c, i, j] for c in range(3)] for d in range(3)]
                mu = MU[i, j]
                mu2 = mu + mu
                vol = LAM[i, j] * (g[0][0] + g[1][1] + g[2][2])
                for c in range(3):
                    SG[c, i, j] = mu2 * g[c][c] + vol
                    for d in range(c):
                        SG[stress(c, d), i, j] = mu * (g[c][d] + g[d][c])
        for c in range(3):
            for j in range(5):
                outs = line(BACKWARD, [SG[stress(c, 0), i, j] for i in range(5)])
                for i in range(5):
                    at = (c * 75 + (i * 5 + j) * 3) * 8
                    F[c, i, j] = outs[i] + DEP[at : at + 24, :].reshape(3, 8, 128)
            for i in range(5):
                outs = line(BACKWARD, [SG[stress(c, 1), i, j] for j in range(5)])
                for j in range(5):
                    F[c, i, j] = F[c, i, j] + outs[j]
                p = stress(c, 2)
                outs = kline(BACKWARD, SG[p, i, :, 0], SG[p, i, :, 1], SG[p, i, :, 2], half)
                for kp in range(3):
                    F[c, i, :, kp] = F[c, i, :, kp] + outs[kp]
        slot = (s + 1) % 2
        local_sums(3)
        pack(3, slot)
        start(3, slot)

        @pl.when(s < STEPS - 1)
        def _():
            deposit(s + 1)

        finish(3, slot)
        unpack(3, slot)
        for i in range(5):
            for j in range(5):
                cm = CM[i, j]
                for c in range(3):
                    w = W[c, i, j] + close_k(F[c, i, j]) * cm
                    W[c, i, j] = w
                    U[c, i, j] = U[c, i, j] + w
        return carry

    lax.fori_loop(0, STEPS, one_step, 0)
    for i in range(5):
        for j in range(5):
            for c in range(3):
                U[c, i, j] = U[c, i, j] - W[c, i, j]
    store_pairs(disp_out, U)
    store_pairs(veloc_out, W)


def to_rows(x):
    lead = x.shape[:-2]
    n = len(lead)
    y = x.reshape(lead + (2, 2, EC))
    return jnp.swapaxes(y, n, n + 1).reshape(lead + (4, EC))


def from_rows(x):
    lead = x.shape[:-2]
    n = len(lead)
    y = jnp.swapaxes(x.reshape(lead + (2, 2, EC)), n, n + 1)
    return y.reshape(lead + (2, 2 * EC))


def shards(
    nd,
    ns,
    displacement,
    velocity,
    lame_lambda,
    shear_modulus,
    density,
    traces,
    section_weights,
    owner,
    element_idx,
    node_weights,
    encode_bits,
):
    devices = nd * ns
    rows = traces.shape[0]
    payload = pl.pallas_call(
        functools.partial(pack_kernel, devices),
        out_shape=jax.ShapeDtypeStruct((devices, CAP * 256), BF16),
        scratch_shapes=[pltpu.VMEM((3, 128, section_weights.shape[1]), F32)],
        name="pack_rows",
    )(
        traces,
        section_weights,
        owner.reshape(1, rows),
        element_idx.reshape(1, rows),
        node_weights,
        encode_bits.T,
    )
    got = lax.all_to_all(payload, ("dom", "slab"), split_axis=0, concat_axis=0, tiled=True)
    field = (5, 5, 3, 8, 128)
    vm = lambda *shape: pltpu.VMEM(shape, F32)
    tiles, scales, ends = sizes(4)
    messages = [pltpu.VMEM((2, tiles, 16, 128), jnp.int16) for side in range(4)]
    messages += [vm(2, ends, 8, 128) for side in range(4)]
    factors = [vm(2, scales, 8, 128) for side in range(4)]
    out = jax.ShapeDtypeStruct((3, 5, 5, 5, 4, EC), F32)
    disp, veloc = pl.pallas_call(
        functools.partial(step_kernel, nd, ns),
        out_shape=(out, out),
        scratch_shapes=[
            vm(3, *field),
            vm(3, *field),
            vm(*field),
            vm(*field),
            vm(*field),
            vm(3, 3, *field),
            vm(6, *field),
            vm(4, *field),
            vm(1808, 128),
            vm(256, CAP * devices),
            pltpu.VMEM((CAP * devices, 512), BF16),
            *messages,
            *messages,
            *factors,
            *factors,
            pltpu.SemaphoreType.DMA((12, 2)),
            pltpu.SemaphoreType.DMA((12, 2)),
        ],
        compiler_params=pltpu.CompilerParams(collective_id=1, has_side_effects=True),
        name="time_steps",
    )(
        to_rows(displacement),
        to_rows(velocity),
        to_rows(lame_lambda),
        to_rows(shear_modulus),
        to_rows(density),
        got,
    )
    return from_rows(disp + veloc), from_rows(veloc * (1.0 / DT))


def solution(mesh):
    nd, ns = mesh.shape["dom"], mesh.shape["slab"]
    both = P(("dom", "slab"), None)
    fields = P(None, None, None, None, "dom", "slab")
    params = P(None, None, None, "dom", "slab")
    return jax.shard_map(
        functools.partial(shards, nd, ns),
        mesh=mesh,
        in_specs=(
            fields,
            fields,
            params,
            params,
            params,
            both,
            P(),
            both,
            P(("dom", "slab")),
            both,
            both,
        ),
        out_specs=(fields, fields),
        check_vma=False,
    )
```

```python
import functools
import math

import jax
import jax.numpy as jnp
import numpy as np
from jax import lax
from jax.experimental import pallas as pl
from jax.experimental.pallas import tpu as pltpu
from jax.sharding import PartitionSpec as P

EC = 128
CAP = 4
G = 4
STEPS = 4
DT = 0.025
NODES6 = 150
HI, LO, EL = 160, 176, 192
F32, BF16 = jnp.float32, jnp.bfloat16
MESH = pl.DeviceIdType.MESH


def gll():
    inner_point = math.sqrt(3.0 / 7.0)
    points = np.array([-1.0, -inner_point, 0.0, inner_point, 1.0])
    weights = np.array([0.1, 49.0 / 90.0, 32.0 / 45.0, 49.0 / 90.0, 0.1])
    legendre = (35.0 * points**4 - 30.0 * points**2 + 3.0) / 8.0
    derivative = np.zeros((5, 5))
    for i in range(5):
        for j in range(5):
            if i != j:
                derivative[i, j] = legendre[i] / (legendre[j] * (points[i] - points[j]))
    derivative[0, 0] = -5.0
    derivative[4, 4] = 5.0
    return 2.0 * derivative, weights


D2, WEIGHTS = gll()
FORWARD, BACKWARD = D2, -D2.T


def pack_rows(devices, traces, weights, owner, element, nodew, bits, out, wsel):
    rows = traces.shape[0]
    nt = weights.shape[1]
    signs = (2 * bits[...] - 1).astype(F32).T.astype(BF16)
    wsel[...] = jnp.zeros_like(wsel)
    for c in range(3):
        wsel[c, c * STEPS : (c + 1) * STEPS, :] = weights[...].astype(F32)
    source = jnp.zeros((rows, 128), F32)
    for g in range(G):
        sign = signs[:, g : g + 1]
        for c in range(3):
            first = (g * 3 + c) * nt
            block = traces[:, first : first + nt] * sign
            source = source + lax.dot_general(
                block,
                wsel[c].astype(BF16),
                (((1,), (1,)), ((), ())),
                preferred_element_type=F32,
            )
    high = source.astype(BF16).astype(F32)
    low = source - high
    lane = lax.broadcasted_iota(jnp.int32, (rows, 128), 1)
    where_el = jnp.broadcast_to(element[...], (128, rows)).astype(F32).T
    el_high = jnp.floor(where_el * (1.0 / 256.0))
    el_low = where_el - 256.0 * el_high
    base = HI - 128
    extra = pltpu.roll(high, base, 1) + pltpu.roll(low, LO - 128, 1)
    extra = jnp.where(lane == EL - 128, el_low, extra)
    extra = jnp.where(lane == EL - 127, el_high, extra)
    node = lax.broadcasted_iota(jnp.int32, (125, 256), 0)
    column = lax.broadcasted_iota(jnp.int32, (125, 256), 1)
    slot6 = (node // 5) * 6 + node % 5
    spread = (column == slot6) | ((node % 5 == 4) & (column == slot6 + 1))
    wide = jnp.dot(nodew[...], spread.astype(F32).astype(BF16), preferred_element_type=F32)
    right = jnp.concatenate([wide[:, :128], wide[:, 128:] + extra], axis=1).astype(BF16)
    device = lax.broadcasted_iota(jnp.int32, (devices, rows), 0)
    member = (owner[...] == device).astype(F32)
    earlier = lax.broadcasted_iota(jnp.int32, (rows, rows), 0) < lax.broadcasted_iota(
        jnp.int32, (rows, rows), 1
    )
    before = jnp.dot(
        member.astype(BF16), earlier.astype(F32).astype(BF16), preferred_element_type=F32
    )
    for k in range(CAP):
        choose = jnp.where(before == float(k), member, 0.0).astype(BF16)
        packed = jnp.dot(choose, right, preferred_element_type=F32)
        out[pl.ds(k, devices, stride=8), :] = packed[:, :128]
        out[pl.ds(CAP + k, devices, stride=8), :] = packed[:, 128:]


def line(m, u):
    e0, e1, o0, o1 = u[0] + u[4], u[1] + u[3], u[0] - u[4], u[1] - u[3]
    even, odd = [], []
    for i in range(2):
        ce = [float((m[i, l] + m[i, 4 - l]) / 2) for l in range(2)]
        co = [float((m[i, l] - m[i, 4 - l]) / 2) for l in range(2)]
        even.append(ce[0] * e0 + ce[1] * e1 + float(m[i, 2]) * u[2])
        odd.append(co[0] * o0 + co[1] * o1)
    middle = float(m[2, 0]) * o0 + float(m[2, 1]) * o1
    return [even[0] + odd[0], even[1] + odd[1], middle, odd[1] - even[1], odd[0] - even[0]]


def half_row(lower, upper, half):
    return jnp.where(half == 0, float(lower), float(upper)).astype(F32)


def kline(m, p0, p1, p2, half):
    first = half == 0
    ce = [[(m[i, l] + m[i, 4 - l]) / 2 for l in range(2)] for i in range(2)]
    co = [[(m[i, l] - m[i, 4 - l]) / 2 for l in range(2)] for i in range(2)]
    back = jnp.where(first, p2, p1)
    even, odd = p0 + back, p0 - back
    mid = jnp.where(first, p1, pltpu.roll(p1, 4, 1))
    evens, odds = pltpu.roll(even, 4, 1), pltpu.roll(odd, 4, 1)
    eout = (
        half_row(ce[0][0], ce[1][1], half) * even
        + half_row(ce[0][1], ce[1][0], half) * evens
        + half_row(m[0, 2], m[1, 2], half) * mid
    )
    oout = half_row(co[0][0], co[1][1], half) * odd + half_row(co[0][1], co[1][0], half) * odds
    q0 = eout + oout
    q43 = oout - eout
    q22 = half_row(m[2, 0], m[2, 1], half) * odd + half_row(m[2, 1], m[2, 0], half) * odds
    q1 = jnp.where(first, q22, q43)
    q2 = jnp.where(first, q43, pltpu.roll(q43, 4, 1))
    return q0, q1, q2


SIDES = [(-1, 0), (1, 0), (0, -1), (0, 1), (-1, -1), (-1, 1), (1, -1), (1, 1)]
OPPOSITE = [1, 0, 3, 2, 7, 6, 5, 4]


GROUPS = {3: ((0, 1, 2),), 4: ((0, 1, 2), (3,))}


def tiles_of(group):
    return (5 * len(group) + 2) // 2


def sizes(comps):
    groups = GROUPS[comps]
    return sum(tiles_of(g) for g in groups), len(groups), (comps + 2) // 2


def step_kernel(
    nd,
    ns,
    disp,
    veloc,
    lame,
    shear,
    density,
    traces,
    weights,
    owner,
    element,
    nodew,
    bits,
    disp_out,
    veloc_out,
    raw_disp,
    raw_veloc,
    raw_lame,
    raw_shear,
    raw_density,
    raw_traces,
    WSEL,
    ROWS,
    OUT,
    IN,
    U,
    W,
    LAM,
    MU,
    CM,
    GR,
    SG,
    F,
    DEP,
    TT,
    OH,
    *rest,
):
    send, recv = rest[0:8], rest[8:16]
    send_scale, recv_scale = rest[16:20], rest[20:24]
    send_sem, recv_sem, load_sem, all_send, all_recv = rest[24:29]
    dom, slab = lax.axis_index("dom"), lax.axis_index("slab")

    def exists(side):
        da, db = SIDES[side]
        cond = None
        for shift, index, count in ((da, dom, nd), (db, slab, ns)):
            if shift:
                one = index > 0 if shift < 0 else index < count - 1
                cond = one if cond is None else jnp.logical_and(cond, one)
        return cond

    def target(side):
        return (dom + SIDES[side][0], slab + SIDES[side][1])

    for side in range(8):
        recv[side][...] = jnp.zeros_like(recv[side])
        if side < 4:
            recv_scale[side][...] = jnp.zeros_like(recv_scale[side])
    devices = nd * ns
    me = dom * ns + slab
    barrier = pltpu.get_barrier_semaphore()

    def other(step):
        number = lax.rem(me + step, devices)
        return number, (lax.div(number, ns), lax.rem(number, ns))

    def greet(step, carry):
        pl.semaphore_signal(barrier, inc=1, device_id=other(step)[1], device_id_type=MESH)
        return carry

    loads = [
        pltpu.make_async_copy(src, dst, load_sem.at[n])
        for n, (src, dst) in enumerate(
            (
                (traces, raw_traces),
                (disp, raw_disp),
                (density, raw_density),
                (lame, raw_lame),
                (shear, raw_shear),
                (veloc, raw_veloc),
            )
        )
    ]
    for one in loads:
        one.start()
    lax.fori_loop(1, devices, greet, 0)

    def row_copy(step):
        number, there = other(step)
        return pltpu.make_async_remote_copy(
            src_ref=OUT.at[number],
            dst_ref=IN.at[me],
            send_sem=all_send,
            recv_sem=all_recv,
            device_id=there,
            device_id_type=MESH,
        )

    def send_row(step, carry):
        row_copy(step).start()
        return carry

    own_rows = pltpu.make_async_copy(OUT.at[me], IN.at[me], load_sem.at[6])

    loads[0].wait()
    pack_rows(devices, raw_traces, weights, owner, element, nodew, bits, ROWS, WSEL)
    OUT[...] = ROWS[...].reshape(devices, 8, 128).astype(BF16)
    pl.semaphore_wait(barrier, devices - 1)
    own_rows.start()
    lax.fori_loop(1, devices, send_row, 0)

    def finish_rows():
        own_rows.wait()
        pltpu.make_async_remote_copy(
            src_ref=OUT.at[pl.ds(0, devices - 1)],
            dst_ref=IN.at[pl.ds(0, devices - 1)],
            send_sem=all_send,
            recv_sem=all_recv,
            device_id=other(1)[1],
            device_id_type=MESH,
        ).wait()

    sub = lax.broadcasted_iota(jnp.int32, (1, 8, 128), 1)
    lane = lax.broadcasted_iota(jnp.int32, (1, 8, 128), 2)
    half, bit_b, bit_a = sub // 4, (sub // 2) % 2, sub % 2

    def roll_s(x, shift):
        return pltpu.roll(x, shift % 8, 1)

    def roll_l(x, shift):
        return pltpu.roll(x, shift % 128, 2)

    def load_pairs(dst, src):
        lead = (slice(None),) * (len(dst.shape) - 3)
        for kp in range(3):
            dst[lead + (kp, slice(0, 4))] = src[lead + (2 * kp,)]
            dst[lead + (kp, slice(4, 8))] = src[lead + (min(2 * kp + 1, 4),)]

    def store_pairs(dst, src):
        lead = (slice(None),) * (len(src.shape) - 3)
        for k in range(5):
            first = 4 * (k % 2)
            dst[lead + (k,)] = src[lead + (k // 2, slice(first, first + 4))]

    def local_sums(comps, extra=None):
        for c in range(comps):
            for i in range(5):
                p0, p1, p2 = (F[c, i, :, kp] for kp in range(3))
                if extra is not None:
                    at = (c * 75 + i * 15) * 8
                    add = extra[at : at + 120, :].reshape(5, 3, 8, 128)
                    p0, p2 = p0 + add[:, 0], p2 + add[:, 2]
                    F[c, i, :, 1] = p1 + add[:, 1]
                    F[c, i, :, 2] = p2
                F[c, i, :, 0] = p0 + jnp.where((half == 0) & (lane > 0), roll_l(p2, 1), 0.0)
            for j in range(5):
                x0, x4 = F[c, 0, j], F[c, 4, j]
                F[c, 0, j] = x0 + jnp.where(bit_a == 1, roll_s(x4, 1), 0.0)
                F[c, 4, j] = x4 + jnp.where(bit_a == 0, roll_s(x0, -1), 0.0)
            for i in range(5):
                x0, x4 = F[c, i, 0], F[c, i, 4]
                F[c, i, 0] = x0 + jnp.where(bit_b == 1, roll_s(x4, 2), 0.0)
                F[c, i, 4] = x4 + jnp.where(bit_b == 0, roll_s(x0, -2), 0.0)

    def close_k(x):
        x0 = x[0:1]
        dup = jnp.where(half == 0, x0, roll_s(x0, 4))
        x2 = jnp.where(lane < 127, roll_l(dup, -1), x[2:3])
        return jnp.concatenate([x[0:2], x2], axis=0)

    def merge(x, y, bit, width, value):
        toward = width if value == 0 else -width
        return jnp.where(bit == value, x, roll_s(y, toward))

    def unmerge(m, bit, width, value):
        toward = -width if value == 0 else width
        keep = bit == value
        return jnp.where(keep, roll_s(m, toward), 0.0), jnp.where(keep, m, 0.0)

    def ends(zs):
        out = jnp.zeros((1, 8, 128), F32)
        for n, z in enumerate(zs):
            out = jnp.where(lane == n, roll_l(z, n + 1), out)
        return out

    def end_of(row, n):
        return jnp.where(lane == 127, roll_l(row, 127 - n), 0.0)

    def face(side):
        axis, value = side // 2, side % 2
        bit, width = ((bit_a, 1), (bit_b, 2))[axis]
        node = 4 * value

        def at(c, n, kp):
            return (c, node, n, kp) if axis == 0 else (c, n, node, kp)

        def line_at(c, kp):
            return (c, node, slice(None), kp) if axis == 0 else (c, slice(None), node, kp)

        return bit, width, value, at, line_at

    def pack(comps, slot):
        for side in (2, 3, 0, 1):
            bit, width, value, at, line_at = face(side)
            tile = 0
            for g, group in enumerate(GROUPS[comps]):
                rows = []
                for c in group:
                    merged = merge(F[line_at(c, 0)], F[line_at(c, 1)], bit, width, value)
                    rows.extend(merged[n : n + 1] for n in range(5))
                rows.append(ends([F[at(c, n, 2)][None] for c in group for n in range(5)]))
                largest = jnp.abs(rows[0])
                for row in rows[1:]:
                    largest = jnp.maximum(largest, jnp.abs(row))
                scale = largest * (1.0 / 32000.0) + 1e-30
                send_scale[side][slot, g : g + 1] = scale
                inverse = 1.0 / scale
                for n in range(0, len(rows), 2):
                    x = jnp.concatenate([rows[n][0] * inverse[0], rows[n + 1][0] * inverse[0]], 0)
                    x = x + jnp.where(x < 0.0, -0.5, 0.5)
                    send[side][slot, tile] = x.astype(jnp.int32).astype(jnp.int16)
                    tile += 1
            start(side, comps, slot)
        for side in range(4, 8):
            da, db = SIDES[side]
            va, vb = (da + 1) // 2, (db + 1) // 2
            items = []
            for c in range(comps):
                x = F[c, 4 * va, 4 * vb]
                items.append(merge(x[0:1], x[1:2], bit_a, 1, va))
            items.append(ends([F[c, 4 * va, 4 * vb, 2:3] for c in range(comps)]))
            for n in range(0, len(items), 2):
                y = items[min(n + 1, len(items) - 1)]
                send[side][slot, n // 2 : n // 2 + 1] = merge(items[n], y, bit_b, 2, vb)
            start(side, comps, slot)

    def unpack(comps, slot):
        for side in range(4):
            bit, width, value, at, line_at = face(side)
            tile = 0
            for g, group in enumerate(GROUPS[comps]):
                scale = recv_scale[side][slot, g : g + 1]
                rows = []
                for _ in range(tiles_of(group)):
                    x = recv[side][slot, tile].astype(jnp.int32).astype(F32)
                    rows.extend([x[None, 0:8] * scale, x[None, 8:16] * scale])
                    tile += 1
                for m, c in enumerate(group):
                    merged = jnp.concatenate(rows[5 * m : 5 * m + 5], axis=0)
                    for kp, add in enumerate(unmerge(merged, bit, width, value)):
                        F[line_at(c, kp)] = F[line_at(c, kp)] + add
                last, _ = unmerge(rows[5 * len(group)], bit, width, value)
                for m, c in enumerate(group):
                    for n in range(5):
                        F[at(c, n, 2)] = F[at(c, n, 2)] + end_of(last, 5 * m + n)[0]
        for side in range(4, 8):
            da, db = SIDES[side]
            va, vb = (da + 1) // 2, (db + 1) // 2
            items = []
            for n in range(sizes(comps)[2]):
                items.extend(unmerge(recv[side][slot, n : n + 1], bit_b, 2, vb))
            last, _ = unmerge(items[comps], bit_a, 1, va)
            for c in range(comps):
                x, y = unmerge(items[c], bit_a, 1, va)
                add = jnp.concatenate([x, y, end_of(last, c)], axis=0)
                F[c, 4 * va, 4 * vb] = F[c, 4 * va, 4 * vb] + add

    def copies(side, comps, slot, source):
        tiles, scales, rows = sizes(comps)
        parts = [(send, recv, tiles, side)] if side < 4 else [(send, recv, rows, side)]
        if side < 4:
            parts.append((send_scale, recv_scale, scales, 8 + side))
        out = []
        for src, dst, count, number in parts:
            there = number - side + OPPOSITE[side] if source else number
            out.append(
                pltpu.make_async_remote_copy(
                    src_ref=src[side].at[slot, pl.ds(0, count)],
                    dst_ref=dst[OPPOSITE[side] if source else side].at[slot, pl.ds(0, count)],
                    send_sem=send_sem.at[number, slot],
                    recv_sem=recv_sem.at[there, slot],
                    device_id=target(side),
                    device_id_type=MESH,
                )
            )
        return out

    def start(side, comps, slot):
        @pl.when(exists(side))
        def _():
            for one in copies(side, comps, slot, True):
                one.start()

    def finish(comps, slot):
        for side in range(8):

            @pl.when(exists(side))
            def _():
                for one in copies(side, comps, slot, False):
                    one.wait()

    def quad(i, j):
        w = WEIGHTS
        scale = w[i] * w[j] / 8.0
        return jnp.concatenate(
            [half_row(scale * w[2 * kp], scale * w[min(2 * kp + 1, 4)], half) for kp in range(3)],
            axis=0,
        )

    def share(i, j):
        one = jnp.ones((1, 8, 128), F32)

        def along(n, bit, index, devices):
            if n == 0:
                return jnp.where((bit == 1) | (index > 0), 0.5, 1.0)
            if n == 4:
                return jnp.where((bit == 0) | (index < devices - 1), 0.5, 1.0)
            return one

        ab = along(i, bit_a, dom, nd) * along(j, bit_b, slab, ns)
        k0 = jnp.where((half == 0) & (lane > 0), 0.5, 1.0)
        k4 = jnp.where(lane < 127, 0.5, 1.0)
        return jnp.concatenate([ab * k0, ab * one, ab * k4], axis=0)

    loads[1].wait()
    loads[2].wait()
    load_pairs(U, raw_disp)
    load_pairs(CM, raw_density)
    for i in range(5):
        for j in range(5):
            F[3, i, j] = CM[i, j] * quad(i, j)
            for c in range(3):
                F[c, i, j] = U[c, i, j]
    local_sums(4)
    pack(4, 0)
    for one in loads[3:]:
        one.wait()
    load_pairs(LAM, raw_lame)
    load_pairs(MU, raw_shear)
    load_pairs(W, raw_veloc)
    for i in range(5):
        for j in range(5):
            q = quad(i, j)
            LAM[i, j] = LAM[i, j] * q
            MU[i, j] = MU[i, j] * q

    def take_rows():
        finish_rows()
        ROWS[...] = IN[...].astype(F32).reshape(8 * devices, 128)
        for k in range(CAP):
            first = ROWS[pl.ds(k, devices, stride=8), :]
            second = ROWS[pl.ds(CAP + k, devices, stride=8), :]
            TT[0:128, k * devices : (k + 1) * devices] = first.T
            TT[128:256, k * devices : (k + 1) * devices] = second.T
            el = second[:, EL - 128 : EL - 127] + 256.0 * second[:, EL - 127 : EL - 126]
            cols = lax.broadcasted_iota(jnp.int32, (devices, 512), 1)
            OH[k * devices : (k + 1) * devices, :] = (
                (cols == el.astype(jnp.int32)).astype(F32).astype(BF16)
            )

    def deposit(s):
        for c in range(3):
            row = c * STEPS + s
            src = TT[pl.ds(HI + row, 1), :] + TT[pl.ds(LO + row, 1), :]
            term = TT[0:152, :] * src
            high = term.astype(BF16)
            low = (term - high.astype(F32)).astype(BF16)
            sums = jnp.dot(high, OH[...], preferred_element_type=F32) + jnp.dot(
                low, OH[...], preferred_element_type=F32
            )
            for a in range(2):
                for b in range(2):
                    q, first = b * 2 + a, (a * 2 + b) * 128
                    DEP[pl.ds(c * 600 + q, NODES6, stride=4), :] = sums[
                        0:NODES6, first : first + 128
                    ]

    finish(4, 0)
    unpack(4, 0)
    for i in range(5):
        for j in range(5):
            part = share(i, j)
            mass = close_k(F[3, i, j])
            CM[i, j] = (DT * DT) / mass
            scaled = mass * part * (1.0 / DT)
            for c in range(3):
                U[c, i, j] = close_k(F[c, i, j]) * part
                W[c, i, j] = W[c, i, j] * scaled

    pair = {(0, 0): 0, (1, 1): 1, (2, 2): 2, (0, 1): 3, (0, 2): 4, (1, 2): 5}

    def stress(c, d):
        return pair[(min(c, d), max(c, d))]

    def one_step(s, carry):
        for c in range(3):
            for j in range(5):
                outs = line(FORWARD, [U[c, i, j] for i in range(5)])
                for i in range(5):
                    GR[0, c, i, j] = outs[i]
            for i in range(5):
                outs = line(FORWARD, [U[c, i, j] for j in range(5)])
                for j in range(5):
                    GR[1, c, i, j] = outs[j]
                outs = kline(FORWARD, U[c, i, :, 0], U[c, i, :, 1], U[c, i, :, 2], half)
                for kp in range(3):
                    GR[2, c, i, :, kp] = outs[kp]
        for i in range(5):
            for j in range(5):
                g = [[GR[d, c, i, j] for c in range(3)] for d in range(3)]
                mu = MU[i, j]
                mu2 = mu + mu
                vol = LAM[i, j] * (g[0][0] + g[1][1] + g[2][2])
                for c in range(3):
                    SG[c, i, j] = mu2 * g[c][c] + vol
                    for d in range(c):
                        SG[stress(c, d), i, j] = mu * (g[c][d] + g[d][c])
        for c in range(3):
            for j in range(5):
                outs = line(BACKWARD, [SG[stress(c, 0), i, j] for i in range(5)])
                for i in range(5):
                    F[c, i, j] = outs[i]
            for i in range(5):
                outs = line(BACKWARD, [SG[stress(c, 1), i, j] for j in range(5)])
                for j in range(5):
                    F[c, i, j] = F[c, i, j] + outs[j]
                p = stress(c, 2)
                outs = kline(BACKWARD, SG[p, i, :, 0], SG[p, i, :, 1], SG[p, i, :, 2], half)
                for kp in range(3):
                    F[c, i, :, kp] = F[c, i, :, kp] + outs[kp]
        slot = (s + 1) % 2

        @pl.when(s == 0)
        def _():
            take_rows()
            deposit(0)
            for c in range(3):
                for i in range(5):
                    at = (c * 75 + i * 15) * 8
                    DEP[at : at + 120, :] = DEP[at : at + 120, :] + W[c, i].reshape(120, 128)
                    W[c, i] = jnp.zeros((5, 3, 8, 128), F32)

        local_sums(3, DEP)
        pack(3, slot)

        @pl.when(s < STEPS - 1)
        def _():
            deposit(s + 1)

        finish(3, slot)
        unpack(3, slot)
        for i in range(5):
            for j in range(5):
                cm = CM[i, j]
                for c in range(3):
                    w = W[c, i, j] + close_k(F[c, i, j]) * cm
                    W[c, i, j] = w
                    U[c, i, j] = U[c, i, j] + w
        return carry

    lax.fori_loop(0, STEPS, one_step, 0)
    for i in range(5):
        for j in range(5):
            for c in range(3):
                U[c, i, j] = U[c, i, j] - W[c, i, j]
    store_pairs(disp_out, U)
    store_pairs(veloc_out, W)


def to_rows(x):
    lead = x.shape[:-2]
    n = len(lead)
    y = x.reshape(lead + (2, 2, EC))
    return jnp.swapaxes(y, n, n + 1).reshape(lead + (4, EC))


def from_rows(x):
    lead = x.shape[:-2]
    n = len(lead)
    y = jnp.swapaxes(x.reshape(lead + (2, 2, EC)), n, n + 1)
    return y.reshape(lead + (2, 2 * EC))


def shards(
    nd,
    ns,
    displacement,
    velocity,
    lame_lambda,
    shear_modulus,
    density,
    traces,
    section_weights,
    owner,
    element_idx,
    node_weights,
    encode_bits,
):
    devices = nd * ns
    rows = traces.shape[0]
    field = (5, 5, 3, 8, 128)
    vm = lambda *shape: pltpu.VMEM(shape, F32)
    tiles, scales, ends = sizes(4)
    messages = [pltpu.VMEM((2, tiles, 16, 128), jnp.int16) for side in range(4)]
    messages += [vm(2, ends, 8, 128) for side in range(4)]
    factors = [vm(2, scales, 8, 128) for side in range(4)]
    out = jax.ShapeDtypeStruct((3, 5, 5, 5, 4, EC), F32)
    disp, veloc = pl.pallas_call(
        functools.partial(step_kernel, nd, ns),
        out_shape=(out, out),
        in_specs=[pl.BlockSpec(memory_space=pl.ANY)] * 6
        + [pl.BlockSpec(memory_space=pltpu.VMEM)] * 5,
        out_specs=(pl.BlockSpec(memory_space=pltpu.VMEM),) * 2,
        scratch_shapes=[
            vm(3, 5, 5, 5, 4, EC),
            vm(3, 5, 5, 5, 4, EC),
            vm(5, 5, 5, 4, EC),
            vm(5, 5, 5, 4, EC),
            vm(5, 5, 5, 4, EC),
            pltpu.VMEM(traces.shape, BF16),
            vm(3, 128, section_weights.shape[1]),
            vm(8 * devices, 128),
            pltpu.VMEM((devices, 8, 128), BF16),
            pltpu.VMEM((devices, 8, 128), BF16),
            vm(3, *field),
            vm(3, *field),
            vm(*field),
            vm(*field),
            vm(*field),
            vm(3, 3, *field),
            vm(6, *field),
            vm(4, *field),
            vm(1808, 128),
            vm(256, CAP * devices),
            pltpu.VMEM((CAP * devices, 512), BF16),
            *messages,
            *messages,
            *factors,
            *factors,
            pltpu.SemaphoreType.DMA((12, 2)),
            pltpu.SemaphoreType.DMA((12, 2)),
            pltpu.SemaphoreType.DMA((7,)),
            pltpu.SemaphoreType.DMA,
            pltpu.SemaphoreType.DMA,
        ],
        compiler_params=pltpu.CompilerParams(collective_id=1, has_side_effects=True),
        name="time_steps",
    )(
        to_rows(displacement),
        to_rows(velocity),
        to_rows(lame_lambda),
        to_rows(shear_modulus),
        to_rows(density),
        traces,
        section_weights,
        owner.reshape(1, rows),
        element_idx.reshape(1, rows),
        node_weights,
        encode_bits.T,
    )
    return from_rows(disp + veloc), from_rows(veloc * (1.0 / DT))


def solution(mesh):
    nd, ns = mesh.shape["dom"], mesh.shape["slab"]
    both = P(("dom", "slab"), None)
    fields = P(None, None, None, None, "dom", "slab")
    params = P(None, None, None, "dom", "slab")
    return jax.shard_map(
        functools.partial(shards, nd, ns),
        mesh=mesh,
        in_specs=(
            fields,
            fields,
            params,
            params,
            params,
            both,
            P(),
            both,
            P(("dom", "slab")),
            both,
            both,
        ),
        out_specs=(fields, fields),
        check_vma=False,
    )
```

```python
import functools
import math

import jax
import jax.numpy as jnp
import numpy as np
from jax import lax
from jax.experimental import pallas as pl
from jax.experimental.pallas import tpu as pltpu
from jax.sharding import PartitionSpec as P

EC = 128
CAP = 4
G = 4
STEPS = 4
DT = 0.025
NODES6 = 150
HI, LO, EL = 160, 176, 192
F32, BF16 = jnp.float32, jnp.bfloat16
MESH = pl.DeviceIdType.MESH


def gll():
    inner_point = math.sqrt(3.0 / 7.0)
    points = np.array([-1.0, -inner_point, 0.0, inner_point, 1.0])
    weights = np.array([0.1, 49.0 / 90.0, 32.0 / 45.0, 49.0 / 90.0, 0.1])
    legendre = (35.0 * points**4 - 30.0 * points**2 + 3.0) / 8.0
    derivative = np.zeros((5, 5))
    for i in range(5):
        for j in range(5):
            if i != j:
                derivative[i, j] = legendre[i] / (legendre[j] * (points[i] - points[j]))
    derivative[0, 0] = -5.0
    derivative[4, 4] = 5.0
    return 2.0 * derivative, weights


D2, WEIGHTS = gll()
FORWARD, BACKWARD = D2, -D2.T


def choose_rows(devices, weights, owner, nodew, choose, wide, wsel):
    rows = nodew.shape[0]
    wsel[...] = jnp.zeros_like(wsel)
    for c in range(3):
        wsel[c, c * STEPS : (c + 1) * STEPS, :] = weights[...].astype(F32)
    node = lax.broadcasted_iota(jnp.int32, (125, 256), 0)
    column = lax.broadcasted_iota(jnp.int32, (125, 256), 1)
    slot6 = (node // 5) * 6 + node % 5
    spread = (column == slot6) | ((node % 5 == 4) & (column == slot6 + 1))
    wide[...] = jnp.dot(nodew[...], spread.astype(F32).astype(BF16), preferred_element_type=F32)
    device = lax.broadcasted_iota(jnp.int32, (devices, rows), 0)
    member = (owner[...] == device).astype(F32)
    earlier = lax.broadcasted_iota(jnp.int32, (rows, rows), 0) < lax.broadcasted_iota(
        jnp.int32, (rows, rows), 1
    )
    before = jnp.dot(
        member.astype(BF16), earlier.astype(F32).astype(BF16), preferred_element_type=F32
    )
    for k in range(CAP):
        choose[k] = jnp.where(before == float(k), member, 0.0).astype(BF16)


def pack_first(devices, choose, wide, out):
    right = wide[:, :128].astype(BF16)
    for k in range(CAP):
        out[pl.ds(k, devices, stride=8), :] = jnp.dot(
            choose[k], right, preferred_element_type=F32
        )


def pack_second(devices, traces, element, bits, choose, wide, wsel, out):
    rows = traces.shape[0]
    nt = wsel.shape[2]
    signs = (2 * bits[...] - 1).astype(F32).T.astype(BF16)
    sources = []
    for c in range(3):
        source = jnp.zeros((rows, 128), F32)
        for g in range(G):
            first = (g * 3 + c) * nt
            block = traces[:, first : first + nt] * signs[:, g : g + 1]
            source = source + lax.dot_general(
                block,
                wsel[c].astype(BF16),
                (((1,), (1,)), ((), ())),
                preferred_element_type=F32,
            )
        sources.append(source)
    source = sources[0] + sources[1] + sources[2]
    high = source.astype(BF16).astype(F32)
    low = source - high
    lane = lax.broadcasted_iota(jnp.int32, (rows, 128), 1)
    where_el = jnp.broadcast_to(element[...], (128, rows)).astype(F32).T
    el_high = jnp.floor(where_el * (1.0 / 256.0))
    el_low = where_el - 256.0 * el_high
    extra = pltpu.roll(high, HI - 128, 1) + pltpu.roll(low, LO - 128, 1)
    extra = jnp.where(lane == EL - 128, el_low, extra)
    extra = jnp.where(lane == EL - 127, el_high, extra)
    right = (wide[:, 128:] + extra).astype(BF16)
    for k in range(CAP):
        out[pl.ds(CAP + k, devices, stride=8), :] = jnp.dot(
            choose[k], right, preferred_element_type=F32
        )


def line(m, u):
    e0, e1, o0, o1 = u[0] + u[4], u[1] + u[3], u[0] - u[4], u[1] - u[3]
    even, odd = [], []
    for i in range(2):
        ce = [float((m[i, l] + m[i, 4 - l]) / 2) for l in range(2)]
        co = [float((m[i, l] - m[i, 4 - l]) / 2) for l in range(2)]
        even.append(ce[0] * e0 + ce[1] * e1 + float(m[i, 2]) * u[2])
        odd.append(co[0] * o0 + co[1] * o1)
    middle = float(m[2, 0]) * o0 + float(m[2, 1]) * o1
    return [even[0] + odd[0], even[1] + odd[1], middle, odd[1] - even[1], odd[0] - even[0]]


def half_row(lower, upper, half):
    return jnp.where(half == 0, float(lower), float(upper)).astype(F32)


def kline(m, p0, p1, p2, half):
    first = half == 0
    ce = [[(m[i, l] + m[i, 4 - l]) / 2 for l in range(2)] for i in range(2)]
    co = [[(m[i, l] - m[i, 4 - l]) / 2 for l in range(2)] for i in range(2)]
    back = jnp.where(first, p2, p1)
    even, odd = p0 + back, p0 - back
    mid = jnp.where(first, p1, pltpu.roll(p1, 4, 1))
    evens, odds = pltpu.roll(even, 4, 1), pltpu.roll(odd, 4, 1)
    eout = (
        half_row(ce[0][0], ce[1][1], half) * even
        + half_row(ce[0][1], ce[1][0], half) * evens
        + half_row(m[0, 2], m[1, 2], half) * mid
    )
    oout = half_row(co[0][0], co[1][1], half) * odd + half_row(co[0][1], co[1][0], half) * odds
    q0 = eout + oout
    q43 = oout - eout
    q22 = half_row(m[2, 0], m[2, 1], half) * odd + half_row(m[2, 1], m[2, 0], half) * odds
    q1 = jnp.where(first, q22, q43)
    q2 = jnp.where(first, q43, pltpu.roll(q43, 4, 1))
    return q0, q1, q2


SIDES = [(-1, 0), (1, 0), (0, -1), (0, 1), (-1, -1), (-1, 1), (1, -1), (1, 1)]
OPPOSITE = [1, 0, 3, 2, 7, 6, 5, 4]


GROUPS = {3: ((0, 1, 2),), 4: ((0, 1, 2), (3,))}


def tiles_of(group):
    return (5 * len(group) + 2) // 2


def far_first(nd, ns):
    zs = max(nd // 4, 1)

    def ring(d, n):
        return min(d % n, -d % n)

    def way(k, j):
        total = 0
        for d in range(nd):
            e = (d + k) % nd
            total += ns * (2 * (d // (2 * zs) != e // (2 * zs)) + ring(d // 2 - e // 2, zs))
        for b in range(ns):
            e = (b + j) % ns
            total += nd * (ring(b // 2 - e // 2, max(ns // 2, 1)) + (b % 2 != e % 2))
        return total

    steps = [(k, j) for k in range(nd) for j in range(ns) if (k, j) != (0, 0)]
    return sorted(steps, key=lambda step: (-way(*step), step))


def sizes(comps):
    groups = GROUPS[comps]
    return sum(tiles_of(g) for g in groups), len(groups), (comps + 2) // 2


def step_kernel(
    nd,
    ns,
    disp,
    veloc,
    lame,
    shear,
    density,
    traces,
    weights_in,
    owner_in,
    element_in,
    nodew_in,
    bits_in,
    disp_out,
    veloc_out,
    weights,
    owner,
    element,
    nodew,
    bits,
    raw_disp,
    raw_veloc,
    raw_lame,
    raw_shear,
    raw_density,
    raw_traces,
    CHOOSE,
    WIDE,
    WSEL,
    ROWS,
    OUT,
    IN,
    U,
    W,
    LAM,
    MU,
    CM,
    GR,
    SG,
    F,
    DEP,
    TT,
    OH,
    *rest,
):
    send, recv = rest[0:8], rest[8:16]
    send_scale, recv_scale = rest[16:20], rest[20:24]
    send_sem, recv_sem, load_sem, all_send, all_recv = rest[24:29]
    dom, slab = lax.axis_index("dom"), lax.axis_index("slab")

    def exists(side):
        da, db = SIDES[side]
        cond = None
        for shift, index, count in ((da, dom, nd), (db, slab, ns)):
            if shift:
                one = index > 0 if shift < 0 else index < count - 1
                cond = one if cond is None else jnp.logical_and(cond, one)
        return cond

    def target(side):
        return (dom + SIDES[side][0], slab + SIDES[side][1])

    for side in range(8):
        recv[side][...] = jnp.zeros_like(recv[side])
        if side < 4:
            recv_scale[side][...] = jnp.zeros_like(recv_scale[side])
    devices = nd * ns
    me = dom * ns + slab
    barrier = pltpu.get_barrier_semaphore()

    doms = [lax.rem(dom + k, nd) for k in range(nd)]
    slabs = [lax.rem(slab + k, ns) for k in range(ns)]
    order = far_first(nd, ns)

    loads = [
        pltpu.make_async_copy(src, dst, load_sem.at[n])
        for n, (src, dst) in enumerate(
            (
                (traces, raw_traces),
                (disp, raw_disp),
                (density, raw_density),
                (lame, raw_lame),
                (shear, raw_shear),
                (veloc, raw_veloc),
            )
        )
    ]
    small = [
        pltpu.make_async_copy(src, dst, load_sem.at[7 + n])
        for n, (src, dst) in enumerate(
            (
                (owner_in, owner),
                (nodew_in, nodew),
                (weights_in, weights),
                (bits_in, bits),
                (element_in, element),
            )
        )
    ]
    for one in small + loads[:3]:
        one.start()
    for k, j in order:
        pl.semaphore_signal(
            barrier, inc=1, device_id=(doms[k], slabs[j]), device_id_type=MESH
        )
    own_rows = pltpu.make_async_copy(OUT.at[me], IN.at[me], load_sem.at[6])

    def send_rows():
        own_rows.start()
        for k, j in order:
            pltpu.make_async_remote_copy(
                src_ref=OUT.at[doms[k] * ns + slabs[j]],
                dst_ref=IN.at[me],
                send_sem=all_send,
                recv_sem=all_recv,
                device_id=(doms[k], slabs[j]),
                device_id_type=MESH,
            ).start()

    def finish_rows():
        own_rows.wait()
        k, j = order[0]
        pltpu.make_async_remote_copy(
            src_ref=OUT.at[pl.ds(0, devices - 1)],
            dst_ref=IN.at[pl.ds(0, devices - 1)],
            send_sem=all_send,
            recv_sem=all_recv,
            device_id=(doms[k], slabs[j]),
            device_id_type=MESH,
        ).wait()

    for one in small:
        one.wait()
    choose_rows(devices, weights, owner, nodew, CHOOSE, WIDE, WSEL)
    pack_first(devices, CHOOSE, WIDE, ROWS)
    loads[0].wait()
    for one in loads[3:]:
        one.start()
    pack_second(devices, raw_traces, element, bits, CHOOSE, WIDE, WSEL, ROWS)
    OUT[...] = ROWS[...].reshape(devices, 8, 128).astype(BF16)

    sub = lax.broadcasted_iota(jnp.int32, (1, 8, 128), 1)
    lane = lax.broadcasted_iota(jnp.int32, (1, 8, 128), 2)
    half, bit_b, bit_a = sub // 4, (sub // 2) % 2, sub % 2

    def roll_s(x, shift):
        return pltpu.roll(x, shift % 8, 1)

    def roll_l(x, shift):
        return pltpu.roll(x, shift % 128, 2)

    def load_pairs(dst, src):
        lead = (slice(None),) * (len(dst.shape) - 3)
        for kp in range(3):
            dst[lead + (kp, slice(0, 4))] = src[lead + (2 * kp,)]
            dst[lead + (kp, slice(4, 8))] = src[lead + (min(2 * kp + 1, 4),)]

    def store_pairs(dst, src):
        lead = (slice(None),) * (len(src.shape) - 3)
        for k in range(5):
            first = 4 * (k % 2)
            dst[lead + (k,)] = src[lead + (k // 2, slice(first, first + 4))]

    def local_sums(comps, extra=None):
        for c in range(comps):
            for i in range(5):
                p0, p1, p2 = (F[c, i, :, kp] for kp in range(3))
                if extra is not None:
                    at = (c * 75 + i * 15) * 8
                    add = extra[at : at + 120, :].reshape(5, 3, 8, 128)
                    p0, p2 = p0 + add[:, 0], p2 + add[:, 2]
                    F[c, i, :, 1] = p1 + add[:, 1]
                    F[c, i, :, 2] = p2
                F[c, i, :, 0] = p0 + jnp.where((half == 0) & (lane > 0), roll_l(p2, 1), 0.0)
            for j in range(5):
                x0, x4 = F[c, 0, j], F[c, 4, j]
                F[c, 0, j] = x0 + jnp.where(bit_a == 1, roll_s(x4, 1), 0.0)
                F[c, 4, j] = x4 + jnp.where(bit_a == 0, roll_s(x0, -1), 0.0)
            for i in range(5):
                x0, x4 = F[c, i, 0], F[c, i, 4]
                F[c, i, 0] = x0 + jnp.where(bit_b == 1, roll_s(x4, 2), 0.0)
                F[c, i, 4] = x4 + jnp.where(bit_b == 0, roll_s(x0, -2), 0.0)

    def close_k(x):
        x0 = x[0:1]
        dup = jnp.where(half == 0, x0, roll_s(x0, 4))
        x2 = jnp.where(lane < 127, roll_l(dup, -1), x[2:3])
        return jnp.concatenate([x[0:2], x2], axis=0)

    def merge(x, y, bit, width, value):
        toward = width if value == 0 else -width
        return jnp.where(bit == value, x, roll_s(y, toward))

    def unmerge(m, bit, width, value):
        toward = -width if value == 0 else width
        keep = bit == value
        return jnp.where(keep, roll_s(m, toward), 0.0), jnp.where(keep, m, 0.0)

    def ends(zs):
        out = jnp.zeros((1, 8, 128), F32)
        for n, z in enumerate(zs):
            out = jnp.where(lane == n, roll_l(z, n + 1), out)
        return out

    def end_of(row, n):
        return jnp.where(lane == 127, roll_l(row, 127 - n), 0.0)

    def face(side):
        axis, value = side // 2, side % 2
        bit, width = ((bit_a, 1), (bit_b, 2))[axis]
        node = 4 * value

        def at(c, n, kp):
            return (c, node, n, kp) if axis == 0 else (c, n, node, kp)

        def line_at(c, kp):
            return (c, node, slice(None), kp) if axis == 0 else (c, slice(None), node, kp)

        return bit, width, value, at, line_at

    def pack(comps, slot):
        for side in (0, 1, 2, 3):
            bit, width, value, at, line_at = face(side)
            tile = 0
            for g, group in enumerate(GROUPS[comps]):
                rows = []
                for c in group:
                    merged = merge(F[line_at(c, 0)], F[line_at(c, 1)], bit, width, value)
                    rows.extend(merged[n : n + 1] for n in range(5))
                rows.append(ends([F[at(c, n, 2)][None] for c in group for n in range(5)]))
                largest = jnp.abs(rows[0])
                for row in rows[1:]:
                    largest = jnp.maximum(largest, jnp.abs(row))
                scale = largest * (1.0 / 32000.0) + 1e-30
                send_scale[side][slot, g : g + 1] = scale
                inverse = 1.0 / scale
                for n in range(0, len(rows), 2):
                    x = jnp.concatenate([rows[n][0] * inverse[0], rows[n + 1][0] * inverse[0]], 0)
                    x = x + jnp.where(x < 0.0, -0.5, 0.5)
                    send[side][slot, tile] = x.astype(jnp.int32).astype(jnp.int16)
                    tile += 1
            start(side, comps, slot)
        for side in range(4, 8):
            da, db = SIDES[side]
            va, vb = (da + 1) // 2, (db + 1) // 2
            items = []
            for c in range(comps):
                x = F[c, 4 * va, 4 * vb]
                items.append(merge(x[0:1], x[1:2], bit_a, 1, va))
            items.append(ends([F[c, 4 * va, 4 * vb, 2:3] for c in range(comps)]))
            for n in range(0, len(items), 2):
                y = items[min(n + 1, len(items) - 1)]
                send[side][slot, n // 2 : n // 2 + 1] = merge(items[n], y, bit_b, 2, vb)
            start(side, comps, slot)

    def unpack(comps, slot):
        for side in (2, 3, 0, 1):
            finish(side, comps, slot)
            bit, width, value, at, line_at = face(side)
            tile = 0
            for g, group in enumerate(GROUPS[comps]):
                scale = recv_scale[side][slot, g : g + 1]
                rows = []
                for _ in range(tiles_of(group)):
                    x = recv[side][slot, tile].astype(jnp.int32).astype(F32)
                    rows.extend([x[None, 0:8] * scale, x[None, 8:16] * scale])
                    tile += 1
                for m, c in enumerate(group):
                    merged = jnp.concatenate(rows[5 * m : 5 * m + 5], axis=0)
                    for kp, add in enumerate(unmerge(merged, bit, width, value)):
                        F[line_at(c, kp)] = F[line_at(c, kp)] + add
                last, _ = unmerge(rows[5 * len(group)], bit, width, value)
                for m, c in enumerate(group):
                    for n in range(5):
                        F[at(c, n, 2)] = F[at(c, n, 2)] + end_of(last, 5 * m + n)[0]
        for side in range(4, 8):
            da, db = SIDES[side]
            va, vb = (da + 1) // 2, (db + 1) // 2
            items = []
            finish(side, comps, slot)
            for n in range(sizes(comps)[2]):
                items.extend(unmerge(recv[side][slot, n : n + 1], bit_b, 2, vb))
            last, _ = unmerge(items[comps], bit_a, 1, va)
            for c in range(comps):
                x, y = unmerge(items[c], bit_a, 1, va)
                add = jnp.concatenate([x, y, end_of(last, c)], axis=0)
                F[c, 4 * va, 4 * vb] = F[c, 4 * va, 4 * vb] + add

    def copies(side, comps, slot, source):
        tiles, scales, rows = sizes(comps)
        parts = [(send, recv, tiles, side)] if side < 4 else [(send, recv, rows, side)]
        if side < 4:
            parts.append((send_scale, recv_scale, scales, 8 + side))
        out = []
        for src, dst, count, number in parts:
            there = number - side + OPPOSITE[side] if source else number
            out.append(
                pltpu.make_async_remote_copy(
                    src_ref=src[side].at[slot, pl.ds(0, count)],
                    dst_ref=dst[OPPOSITE[side] if source else side].at[slot, pl.ds(0, count)],
                    send_sem=send_sem.at[number, slot],
                    recv_sem=recv_sem.at[there, slot],
                    device_id=target(side),
                    device_id_type=MESH,
                )
            )
        return out

    def start(side, comps, slot):
        @pl.when(exists(side))
        def _():
            for one in copies(side, comps, slot, True):
                one.start()

    def finish(side, comps, slot):
        @pl.when(exists(side))
        def _():
            for one in copies(side, comps, slot, False):
                one.wait()

    def quad(i, j):
        w = WEIGHTS
        scale = w[i] * w[j] / 8.0
        return jnp.concatenate(
            [half_row(scale * w[2 * kp], scale * w[min(2 * kp + 1, 4)], half) for kp in range(3)],
            axis=0,
        )

    def share(i, j):
        one = jnp.ones((1, 8, 128), F32)

        def along(n, bit, index, devices):
            if n == 0:
                return jnp.where((bit == 1) | (index > 0), 0.5, 1.0)
            if n == 4:
                return jnp.where((bit == 0) | (index < devices - 1), 0.5, 1.0)
            return one

        ab = along(i, bit_a, dom, nd) * along(j, bit_b, slab, ns)
        k0 = jnp.where((half == 0) & (lane > 0), 0.5, 1.0)
        k4 = jnp.where(lane < 127, 0.5, 1.0)
        return jnp.concatenate([ab * k0, ab * one, ab * k4], axis=0)

    loads[1].wait()
    loads[2].wait()
    load_pairs(U, raw_disp)
    load_pairs(CM, raw_density)
    for i in range(5):
        for j in range(5):
            F[3, i, j] = CM[i, j] * quad(i, j)
            for c in range(3):
                F[c, i, j] = U[c, i, j]
    local_sums(4)
    pl.semaphore_wait(barrier, devices - 1)
    send_rows()
    pack(4, 0)
    for one in loads[3:]:
        one.wait()
    load_pairs(LAM, raw_lame)
    load_pairs(MU, raw_shear)
    load_pairs(W, raw_veloc)
    for i in range(5):
        for j in range(5):
            q = quad(i, j)
            LAM[i, j] = LAM[i, j] * q
            MU[i, j] = MU[i, j] * q

    def take_rows():
        finish_rows()
        ROWS[...] = IN[...].astype(F32).reshape(8 * devices, 128)
        for k in range(CAP):
            first = ROWS[pl.ds(k, devices, stride=8), :]
            second = ROWS[pl.ds(CAP + k, devices, stride=8), :]
            TT[0:128, k * devices : (k + 1) * devices] = first.T
            TT[128:256, k * devices : (k + 1) * devices] = second.T
            el = second[:, EL - 128 : EL - 127] + 256.0 * second[:, EL - 127 : EL - 126]
            cols = lax.broadcasted_iota(jnp.int32, (devices, 512), 1)
            OH[k * devices : (k + 1) * devices, :] = (
                (cols == el.astype(jnp.int32)).astype(F32).astype(BF16)
            )

    def deposit(s):
        for c in range(3):
            row = c * STEPS + s
            src = TT[pl.ds(HI + row, 1), :] + TT[pl.ds(LO + row, 1), :]
            term = TT[0:152, :] * src
            high = term.astype(BF16)
            low = (term - high.astype(F32)).astype(BF16)
            sums = jnp.dot(high, OH[...], preferred_element_type=F32) + jnp.dot(
                low, OH[...], preferred_element_type=F32
            )
            for a in range(2):
                for b in range(2):
                    q, first = b * 2 + a, (a * 2 + b) * 128
                    DEP[pl.ds(c * 600 + q, NODES6, stride=4), :] = sums[
                        0:NODES6, first : first + 128
                    ]

    unpack(4, 0)
    for i in range(5):
        for j in range(5):
            part = share(i, j)
            mass = close_k(F[3, i, j])
            CM[i, j] = (DT * DT) / mass
            scaled = mass * part * (1.0 / DT)
            for c in range(3):
                U[c, i, j] = close_k(F[c, i, j]) * part
                W[c, i, j] = W[c, i, j] * scaled

    pair = {(0, 0): 0, (1, 1): 1, (2, 2): 2, (0, 1): 3, (0, 2): 4, (1, 2): 5}

    def stress(c, d):
        return pair[(min(c, d), max(c, d))]

    def one_step(s, carry):
        for c in range(3):
            for j in range(5):
                outs = line(FORWARD, [U[c, i, j] for i in range(5)])
                for i in range(5):
                    GR[0, c, i, j] = outs[i]
            for i in range(5):
                outs = line(FORWARD, [U[c, i, j] for j in range(5)])
                for j in range(5):
                    GR[1, c, i, j] = outs[j]
                outs = kline(FORWARD, U[c, i, :, 0], U[c, i, :, 1], U[c, i, :, 2], half)
                for kp in range(3):
                    GR[2, c, i, :, kp] = outs[kp]
        for i in range(5):
            for j in range(5):
                g = [[GR[d, c, i, j] for c in range(3)] for d in range(3)]
                mu = MU[i, j]
                mu2 = mu + mu
                vol = LAM[i, j] * (g[0][0] + g[1][1] + g[2][2])
                for c in range(3):
                    SG[c, i, j] = mu2 * g[c][c] + vol
                    for d in range(c):
                        SG[stress(c, d), i, j] = mu * (g[c][d] + g[d][c])
        for c in range(3):
            for j in range(5):
                outs = line(BACKWARD, [SG[stress(c, 0), i, j] for i in range(5)])
                for i in range(5):
                    F[c, i, j] = outs[i]
            for i in range(5):
                outs = line(BACKWARD, [SG[stress(c, 1), i, j] for j in range(5)])
                for j in range(5):
                    F[c, i, j] = F[c, i, j] + outs[j]
                p = stress(c, 2)
                outs = kline(BACKWARD, SG[p, i, :, 0], SG[p, i, :, 1], SG[p, i, :, 2], half)
                for kp in range(3):
                    F[c, i, :, kp] = F[c, i, :, kp] + outs[kp]
        slot = (s + 1) % 2

        @pl.when(s == 0)
        def _():
            take_rows()
            deposit(0)
            for c in range(3):
                for i in range(5):
                    at = (c * 75 + i * 15) * 8
                    DEP[at : at + 120, :] = DEP[at : at + 120, :] + W[c, i].reshape(120, 128)
                    W[c, i] = jnp.zeros((5, 3, 8, 128), F32)

        local_sums(3, DEP)
        pack(3, slot)

        @pl.when(s < STEPS - 1)
        def _():
            deposit(s + 1)

        inner = [(i, j) for i in range(1, 4) for j in range(1, 4)]
        update(inner)
        unpack(3, slot)
        update([(i, j) for i in range(5) for j in range(5) if (i, j) not in inner])
        return carry

    def update(lines):
        for i, j in lines:
            cm = CM[i, j]
            for c in range(3):
                w = W[c, i, j] + close_k(F[c, i, j]) * cm
                W[c, i, j] = w
                U[c, i, j] = U[c, i, j] + w

    lax.fori_loop(0, STEPS, one_step, 0)
    for i in range(5):
        for j in range(5):
            for c in range(3):
                U[c, i, j] = U[c, i, j] - W[c, i, j]
    store_pairs(disp_out, U)
    store_pairs(veloc_out, W)


def to_rows(x):
    lead = x.shape[:-2]
    n = len(lead)
    y = x.reshape(lead + (2, 2, EC))
    return jnp.swapaxes(y, n, n + 1).reshape(lead + (4, EC))


def from_rows(x):
    lead = x.shape[:-2]
    n = len(lead)
    y = jnp.swapaxes(x.reshape(lead + (2, 2, EC)), n, n + 1)
    return y.reshape(lead + (2, 2 * EC))


def shards(
    nd,
    ns,
    displacement,
    velocity,
    lame_lambda,
    shear_modulus,
    density,
    traces,
    section_weights,
    owner,
    element_idx,
    node_weights,
    encode_bits,
):
    devices = nd * ns
    rows = traces.shape[0]
    field = (5, 5, 3, 8, 128)
    vm = lambda *shape: pltpu.VMEM(shape, F32)
    tiles, scales, ends = sizes(4)
    messages = [pltpu.VMEM((2, tiles, 16, 128), jnp.int16) for side in range(4)]
    messages += [vm(2, ends, 8, 128) for side in range(4)]
    factors = [vm(2, scales, 8, 128) for side in range(4)]
    out = jax.ShapeDtypeStruct((3, 5, 5, 5, 4, EC), F32)
    disp, veloc = pl.pallas_call(
        functools.partial(step_kernel, nd, ns),
        out_shape=(out, out),
        in_specs=[pl.BlockSpec(memory_space=pltpu.HBM)] * 11,
        out_specs=(pl.BlockSpec(memory_space=pltpu.VMEM),) * 2,
        scratch_shapes=[
            pltpu.VMEM(section_weights.shape, BF16),
            pltpu.VMEM((1, rows), jnp.int32),
            pltpu.VMEM((1, rows), jnp.int32),
            pltpu.VMEM(node_weights.shape, BF16),
            pltpu.VMEM((G, rows), jnp.int32),
            vm(3, 5, 5, 5, 4, EC),
            vm(3, 5, 5, 5, 4, EC),
            vm(5, 5, 5, 4, EC),
            vm(5, 5, 5, 4, EC),
            vm(5, 5, 5, 4, EC),
            pltpu.VMEM(traces.shape, BF16),
            pltpu.VMEM((CAP, devices, rows), BF16),
            vm(rows, 256),
            vm(3, 128, section_weights.shape[1]),
            vm(8 * devices, 128),
            pltpu.VMEM((devices, 8, 128), BF16),
            pltpu.VMEM((devices, 8, 128), BF16),
            vm(3, *field),
            vm(3, *field),
            vm(*field),
            vm(*field),
            vm(*field),
            vm(3, 3, *field),
            vm(6, *field),
            vm(4, *field),
            vm(1808, 128),
            vm(256, CAP * devices),
            pltpu.VMEM((CAP * devices, 512), BF16),
            *messages,
            *messages,
            *factors,
            *factors,
            pltpu.SemaphoreType.DMA((12, 2)),
            pltpu.SemaphoreType.DMA((12, 2)),
            pltpu.SemaphoreType.DMA((12,)),
            pltpu.SemaphoreType.DMA,
            pltpu.SemaphoreType.DMA,
        ],
        compiler_params=pltpu.CompilerParams(
            collective_id=1, has_side_effects=True, vmem_limit_bytes=28 * 2**20
        ),
        name="time_steps",
    )(
        *(
            pltpu.with_memory_space_constraint(x, pltpu.HBM)
            for x in (
                to_rows(displacement),
                to_rows(velocity),
                to_rows(lame_lambda),
                to_rows(shear_modulus),
                to_rows(density),
                traces,
                section_weights,
                owner.reshape(1, rows),
                element_idx.reshape(1, rows),
                node_weights,
                encode_bits.T,
            )
        )
    )
    return from_rows(disp + veloc), from_rows(veloc * (1.0 / DT))


def solution(mesh):
    nd, ns = mesh.shape["dom"], mesh.shape["slab"]
    both = P(("dom", "slab"), None)
    fields = P(None, None, None, None, "dom", "slab")
    params = P(None, None, None, "dom", "slab")
    return jax.shard_map(
        functools.partial(shards, nd, ns),
        mesh=mesh,
        in_specs=(
            fields,
            fields,
            params,
            params,
            params,
            both,
            P(),
            both,
            P(("dom", "slab")),
            both,
            both,
        ),
        out_specs=(fields, fields),
        check_vma=False,
    )
```

```python
import functools
import math

import jax
import jax.numpy as jnp
import numpy as np
from jax import lax
from jax.experimental import pallas as pl
from jax.experimental.pallas import tpu as pltpu
from jax.sharding import PartitionSpec as P

EC = 128
CAP = 4
G = 4
STEPS = 4
DT = 0.025
NODES6 = 150
HI, LO, EL = 160, 176, 192
F32, BF16 = jnp.float32, jnp.bfloat16
MESH = pl.DeviceIdType.MESH


def gll():
    inner_point = math.sqrt(3.0 / 7.0)
    points = np.array([-1.0, -inner_point, 0.0, inner_point, 1.0])
    weights = np.array([0.1, 49.0 / 90.0, 32.0 / 45.0, 49.0 / 90.0, 0.1])
    legendre = (35.0 * points**4 - 30.0 * points**2 + 3.0) / 8.0
    derivative = np.zeros((5, 5))
    for i in range(5):
        for j in range(5):
            if i != j:
                derivative[i, j] = legendre[i] / (legendre[j] * (points[i] - points[j]))
    derivative[0, 0] = -5.0
    derivative[4, 4] = 5.0
    return 2.0 * derivative, weights


D2, WEIGHTS = gll()
FORWARD, BACKWARD = D2, -D2.T


def choose_rows(devices, weights, owner, nodew, choose, wide, wsel):
    rows = nodew.shape[0]
    wsel[...] = jnp.zeros_like(wsel)
    for c in range(3):
        wsel[c, c * STEPS : (c + 1) * STEPS, :] = weights[...].astype(F32)
    node = lax.broadcasted_iota(jnp.int32, (125, 256), 0)
    column = lax.broadcasted_iota(jnp.int32, (125, 256), 1)
    slot6 = (node // 5) * 6 + node % 5
    spread = (column == slot6) | ((node % 5 == 4) & (column == slot6 + 1))
    wide[...] = jnp.dot(nodew[...], spread.astype(F32).astype(BF16), preferred_element_type=F32)
    device = lax.broadcasted_iota(jnp.int32, (devices, rows), 0)
    member = (owner[...] == device).astype(F32)
    earlier = lax.broadcasted_iota(jnp.int32, (rows, rows), 0) < lax.broadcasted_iota(
        jnp.int32, (rows, rows), 1
    )
    before = jnp.dot(
        member.astype(BF16), earlier.astype(F32).astype(BF16), preferred_element_type=F32
    )
    for k in range(CAP):
        choose[k] = jnp.where(before == float(k), member, 0.0).astype(BF16)


def pack_first(devices, choose, wide, out):
    right = wide[:, :128].astype(BF16)
    for k in range(CAP):
        out[pl.ds(k, devices, stride=8), :] = jnp.dot(
            choose[k], right, preferred_element_type=F32
        )


def pack_second(devices, traces, element, bits, choose, wide, wsel, out):
    rows = traces.shape[0]
    nt = wsel.shape[2]
    signs = (2 * bits[...] - 1).astype(F32).T.astype(BF16)
    sources = []
    for c in range(3):
        source = jnp.zeros((rows, 128), F32)
        for g in range(G):
            first = (g * 3 + c) * nt
            block = traces[:, first : first + nt] * signs[:, g : g + 1]
            source = source + lax.dot_general(
                block,
                wsel[c].astype(BF16),
                (((1,), (1,)), ((), ())),
                preferred_element_type=F32,
            )
        sources.append(source)
    source = sources[0] + sources[1] + sources[2]
    high = source.astype(BF16).astype(F32)
    low = source - high
    lane = lax.broadcasted_iota(jnp.int32, (rows, 128), 1)
    where_el = jnp.broadcast_to(element[...], (128, rows)).astype(F32).T
    el_high = jnp.floor(where_el * (1.0 / 256.0))
    el_low = where_el - 256.0 * el_high
    extra = pltpu.roll(high, HI - 128, 1) + pltpu.roll(low, LO - 128, 1)
    extra = jnp.where(lane == EL - 128, el_low, extra)
    extra = jnp.where(lane == EL - 127, el_high, extra)
    right = (wide[:, 128:] + extra).astype(BF16)
    for k in range(CAP):
        out[pl.ds(CAP + k, devices, stride=8), :] = jnp.dot(
            choose[k], right, preferred_element_type=F32
        )


def line(m, u, wanted=(0, 1, 2, 3, 4)):
    e0, e1, o0, o1 = u[0] + u[4], u[1] + u[3], u[0] - u[4], u[1] - u[3]
    out = {}
    for i in range(2):
        if i in wanted or 4 - i in wanted:
            ce = [float((m[i, l] + m[i, 4 - l]) / 2) for l in range(2)]
            co = [float((m[i, l] - m[i, 4 - l]) / 2) for l in range(2)]
            even = ce[0] * e0 + ce[1] * e1 + float(m[i, 2]) * u[2]
            odd = co[0] * o0 + co[1] * o1
            out[i], out[4 - i] = odd + even, odd - even
    if 2 in wanted:
        out[2] = float(m[2, 0]) * o0 + float(m[2, 1]) * o1
    return out


def half_row(lower, upper, half):
    return jnp.where(half == 0, float(lower), float(upper)).astype(F32)


def kline(m, p0, p1, p2, half):
    first = half == 0
    ce = [[(m[i, l] + m[i, 4 - l]) / 2 for l in range(2)] for i in range(2)]
    co = [[(m[i, l] - m[i, 4 - l]) / 2 for l in range(2)] for i in range(2)]
    back = jnp.where(first, p2, p1)
    even, odd = p0 + back, p0 - back
    mid = jnp.where(first, p1, pltpu.roll(p1, 4, 1))
    evens, odds = pltpu.roll(even, 4, 1), pltpu.roll(odd, 4, 1)
    eout = (
        half_row(ce[0][0], ce[1][1], half) * even
        + half_row(ce[0][1], ce[1][0], half) * evens
        + half_row(m[0, 2], m[1, 2], half) * mid
    )
    oout = half_row(co[0][0], co[1][1], half) * odd + half_row(co[0][1], co[1][0], half) * odds
    q0 = eout + oout
    q43 = oout - eout
    q22 = half_row(m[2, 0], m[2, 1], half) * odd + half_row(m[2, 1], m[2, 0], half) * odds
    q1 = jnp.where(first, q22, q43)
    q2 = jnp.where(first, q43, pltpu.roll(q43, 4, 1))
    return q0, q1, q2


SIDES = [(-1, 0), (1, 0), (0, -1), (0, 1), (-1, -1), (-1, 1), (1, -1), (1, 1)]
OPPOSITE = [1, 0, 3, 2, 7, 6, 5, 4]
ENDS, SLABS = (0, 1, 4, 5, 6, 7), (2, 3)


GROUPS = {3: ((0, 1, 2),), 4: ((0, 1, 2), (3,))}


def tiles_of(group):
    return (5 * len(group) + 2) // 2


def far_first(nd, ns):
    zs = max(nd // 4, 1)

    def ring(d, n):
        return min(d % n, -d % n)

    def way(k, j):
        total = 0
        for d in range(nd):
            e = (d + k) % nd
            total += ns * (2 * (d // (2 * zs) != e // (2 * zs)) + ring(d // 2 - e // 2, zs))
        for b in range(ns):
            e = (b + j) % ns
            total += nd * (ring(b // 2 - e // 2, max(ns // 2, 1)) + (b % 2 != e % 2))
        return total

    steps = [(k, j) for k in range(nd) for j in range(ns) if (k, j) != (0, 0)]
    return sorted(steps, key=lambda step: (-way(*step), step))


def sizes(comps):
    groups = GROUPS[comps]
    return sum(tiles_of(g) for g in groups), len(groups), (comps + 2) // 2


def step_kernel(
    nd,
    ns,
    disp,
    veloc,
    lame,
    shear,
    density,
    traces,
    weights_in,
    owner_in,
    element_in,
    nodew_in,
    bits_in,
    disp_out,
    veloc_out,
    weights,
    owner,
    element,
    nodew,
    bits,
    raw_disp,
    raw_veloc,
    raw_lame,
    raw_shear,
    raw_density,
    raw_traces,
    CHOOSE,
    WIDE,
    WSEL,
    ROWS,
    OUT,
    IN,
    U,
    W,
    LAM,
    MU,
    CM,
    GR,
    SG,
    F,
    DEP,
    TT,
    OH,
    *rest,
):
    send, recv = rest[0:8], rest[8:16]
    send_scale, recv_scale = rest[16:20], rest[20:24]
    send_sem, recv_sem, load_sem, all_send, all_recv = rest[24:29]
    dom, slab = lax.axis_index("dom"), lax.axis_index("slab")

    def exists(side):
        da, db = SIDES[side]
        cond = None
        for shift, index, count in ((da, dom, nd), (db, slab, ns)):
            if shift:
                one = index > 0 if shift < 0 else index < count - 1
                cond = one if cond is None else jnp.logical_and(cond, one)
        return cond

    def target(side):
        return (dom + SIDES[side][0], slab + SIDES[side][1])

    for side in range(8):

        @pl.when(jnp.logical_not(exists(side)))
        def _():
            recv[side][...] = jnp.zeros_like(recv[side])
            if side < 4:
                recv_scale[side][...] = jnp.zeros_like(recv_scale[side])

    devices = nd * ns
    me = dom * ns + slab
    barrier = pltpu.get_barrier_semaphore()

    doms = [lax.rem(dom + k, nd) for k in range(nd)]
    slabs = [lax.rem(slab + k, ns) for k in range(ns)]
    order = far_first(nd, ns)

    loads = [
        pltpu.make_async_copy(src, dst, load_sem.at[n])
        for n, (src, dst) in enumerate(
            (
                (traces, raw_traces),
                (disp, raw_disp),
                (density, raw_density),
                (lame, raw_lame),
                (shear, raw_shear),
                (veloc, raw_veloc),
            )
        )
    ]
    small = [
        pltpu.make_async_copy(src, dst, load_sem.at[7 + n])
        for n, (src, dst) in enumerate(
            (
                (owner_in, owner),
                (nodew_in, nodew),
                (weights_in, weights),
                (bits_in, bits),
                (element_in, element),
            )
        )
    ]
    for one in small + loads[:3]:
        one.start()
    for k, j in order:
        pl.semaphore_signal(
            barrier, inc=1, device_id=(doms[k], slabs[j]), device_id_type=MESH
        )
    own_rows = pltpu.make_async_copy(OUT.at[me], IN.at[me], load_sem.at[6])

    def send_rows():
        own_rows.start()
        for k, j in order:
            pltpu.make_async_remote_copy(
                src_ref=OUT.at[doms[k] * ns + slabs[j]],
                dst_ref=IN.at[me],
                send_sem=all_send,
                recv_sem=all_recv,
                device_id=(doms[k], slabs[j]),
                device_id_type=MESH,
            ).start()

    def finish_rows():
        own_rows.wait()
        k, j = order[0]
        pltpu.make_async_remote_copy(
            src_ref=OUT.at[pl.ds(0, devices - 1)],
            dst_ref=IN.at[pl.ds(0, devices - 1)],
            send_sem=all_send,
            recv_sem=all_recv,
            device_id=(doms[k], slabs[j]),
            device_id_type=MESH,
        ).wait()

    for one in small:
        one.wait()
    choose_rows(devices, weights, owner, nodew, CHOOSE, WIDE, WSEL)
    pack_first(devices, CHOOSE, WIDE, ROWS)
    loads[0].wait()
    for one in loads[3:]:
        one.start()
    pack_second(devices, raw_traces, element, bits, CHOOSE, WIDE, WSEL, ROWS)
    OUT[...] = ROWS[...].reshape(devices, 8, 128).astype(BF16)

    sub = lax.broadcasted_iota(jnp.int32, (1, 8, 128), 1)
    lane = lax.broadcasted_iota(jnp.int32, (1, 8, 128), 2)
    half, bit_b, bit_a = sub // 4, (sub // 2) % 2, sub % 2

    def roll_s(x, shift):
        return pltpu.roll(x, shift % 8, 1)

    def roll_l(x, shift):
        return pltpu.roll(x, shift % 128, 2)

    def load_pairs(dst, src):
        lead = (slice(None),) * (len(dst.shape) - 3)
        for kp in range(3):
            dst[lead + (kp, slice(0, 4))] = src[lead + (2 * kp,)]
            dst[lead + (kp, slice(4, 8))] = src[lead + (min(2 * kp + 1, 4),)]

    def store_pairs(dst, src):
        lead = (slice(None),) * (len(src.shape) - 3)
        for k in range(5):
            first = 4 * (k % 2)
            dst[lead + (k,)] = src[lead + (k // 2, slice(first, first + 4))]

    def local_sums(comps, planes, extra=None):
        for c in range(comps):
            for i in planes:
                p0, p1, p2 = (F[c, i, :, kp] for kp in range(3))
                if extra is not None:
                    at = (c * 75 + i * 15) * 8
                    add = extra[at : at + 120, :].reshape(5, 3, 8, 128)
                    p0, p2 = p0 + add[:, 0], p2 + add[:, 2]
                    F[c, i, :, 1] = p1 + add[:, 1]
                    F[c, i, :, 2] = p2
                F[c, i, :, 0] = p0 + jnp.where((half == 0) & (lane > 0), roll_l(p2, 1), 0.0)
            if 0 in planes:
                for j in range(5):
                    x0, x4 = F[c, 0, j], F[c, 4, j]
                    F[c, 0, j] = x0 + jnp.where(bit_a == 1, roll_s(x4, 1), 0.0)
                    F[c, 4, j] = x4 + jnp.where(bit_a == 0, roll_s(x0, -1), 0.0)
            for i in planes:
                x0, x4 = F[c, i, 0], F[c, i, 4]
                F[c, i, 0] = x0 + jnp.where(bit_b == 1, roll_s(x4, 2), 0.0)
                F[c, i, 4] = x4 + jnp.where(bit_b == 0, roll_s(x0, -2), 0.0)

    def close_k(x):
        x0 = x[0:1]
        dup = jnp.where(half == 0, x0, roll_s(x0, 4))
        x2 = jnp.where(lane < 127, roll_l(dup, -1), x[2:3])
        return jnp.concatenate([x[0:2], x2], axis=0)

    def merge(x, y, bit, width, value):
        toward = width if value == 0 else -width
        return jnp.where(bit == value, x, roll_s(y, toward))

    def unmerge(m, bit, width, value):
        toward = -width if value == 0 else width
        keep = bit == value
        return jnp.where(keep, roll_s(m, toward), 0.0), jnp.where(keep, m, 0.0)

    def ends(zs):
        out = jnp.zeros((1, 8, 128), F32)
        for n, z in enumerate(zs):
            out = jnp.where(lane == n, roll_l(z, n + 1), out)
        return out

    def end_of(row, n):
        return jnp.where(lane == 127, roll_l(row, 127 - n), 0.0)

    def face(side):
        axis, value = side // 2, side % 2
        bit, width = ((bit_a, 1), (bit_b, 2))[axis]
        node = 4 * value

        def at(c, n, kp):
            return (c, node, n, kp) if axis == 0 else (c, n, node, kp)

        def line_at(c, kp):
            return (c, node, slice(None), kp) if axis == 0 else (c, slice(None), node, kp)

        return bit, width, value, at, line_at

    def pack(comps, slot, sides):
        pack_corners(comps, slot, [side for side in sides if side >= 4])
        for side in [side for side in sides if side < 4]:
            bit, width, value, at, line_at = face(side)
            tile = 0
            for g, group in enumerate(GROUPS[comps]):
                rows = []
                for c in group:
                    merged = merge(F[line_at(c, 0)], F[line_at(c, 1)], bit, width, value)
                    rows.extend(merged[n : n + 1] for n in range(5))
                rows.append(ends([F[at(c, n, 2)][None] for c in group for n in range(5)]))
                largest = jnp.abs(rows[0])
                for row in rows[1:]:
                    largest = jnp.maximum(largest, jnp.abs(row))
                scale = largest * (1.0 / 32000.0) + 1e-30
                send_scale[side][slot, g : g + 1] = scale
                inverse = 1.0 / scale
                for n in range(0, len(rows), 2):
                    x = jnp.concatenate([rows[n][0] * inverse[0], rows[n + 1][0] * inverse[0]], 0)
                    x = x + jnp.where(x < 0.0, -0.5, 0.5)
                    send[side][slot, tile] = x.astype(jnp.int32).astype(jnp.int16)
                    tile += 1
            start(side, comps, slot)

    def pack_corners(comps, slot, sides):
        for side in sides:
            da, db = SIDES[side]
            va, vb = (da + 1) // 2, (db + 1) // 2
            items = []
            for c in range(comps):
                x = F[c, 4 * va, 4 * vb]
                items.append(merge(x[0:1], x[1:2], bit_a, 1, va))
            items.append(ends([F[c, 4 * va, 4 * vb, 2:3] for c in range(comps)]))
            for n in range(0, len(items), 2):
                y = items[min(n + 1, len(items) - 1)]
                send[side][slot, n // 2 : n // 2 + 1] = merge(items[n], y, bit_b, 2, vb)
            start(side, comps, slot)

    def unpack(comps, slot, sides):
        for side in [side for side in sides if side < 4]:
            finish(side, comps, slot)
            bit, width, value, at, line_at = face(side)
            tile = 0
            for g, group in enumerate(GROUPS[comps]):
                scale = recv_scale[side][slot, g : g + 1]
                rows = []
                for _ in range(tiles_of(group)):
                    x = recv[side][slot, tile].astype(jnp.int32).astype(F32)
                    rows.extend([x[None, 0:8] * scale, x[None, 8:16] * scale])
                    tile += 1
                for m, c in enumerate(group):
                    merged = jnp.concatenate(rows[5 * m : 5 * m + 5], axis=0)
                    for kp, add in enumerate(unmerge(merged, bit, width, value)):
                        F[line_at(c, kp)] = F[line_at(c, kp)] + add
                last, _ = unmerge(rows[5 * len(group)], bit, width, value)
                for m, c in enumerate(group):
                    for n in range(5):
                        F[at(c, n, 2)] = F[at(c, n, 2)] + end_of(last, 5 * m + n)[0]
        for side in [side for side in sides if side >= 4]:
            da, db = SIDES[side]
            va, vb = (da + 1) // 2, (db + 1) // 2
            items = []
            finish(side, comps, slot)
            for n in range(sizes(comps)[2]):
                items.extend(unmerge(recv[side][slot, n : n + 1], bit_b, 2, vb))
            last, _ = unmerge(items[comps], bit_a, 1, va)
            for c in range(comps):
                x, y = unmerge(items[c], bit_a, 1, va)
                add = jnp.concatenate([x, y, end_of(last, c)], axis=0)
                F[c, 4 * va, 4 * vb] = F[c, 4 * va, 4 * vb] + add

    def copies(side, comps, slot, source):
        tiles, scales, rows = sizes(comps)
        parts = [(send, recv, tiles, side)] if side < 4 else [(send, recv, rows, side)]
        if side < 4:
            parts.append((send_scale, recv_scale, scales, 8 + side))
        out = []
        for src, dst, count, number in parts:
            there = number - side + OPPOSITE[side] if source else number
            out.append(
                pltpu.make_async_remote_copy(
                    src_ref=src[side].at[slot, pl.ds(0, count)],
                    dst_ref=dst[OPPOSITE[side] if source else side].at[slot, pl.ds(0, count)],
                    send_sem=send_sem.at[number, slot],
                    recv_sem=recv_sem.at[there, slot],
                    device_id=target(side),
                    device_id_type=MESH,
                )
            )
        return out

    def start(side, comps, slot):
        @pl.when(exists(side))
        def _():
            for one in copies(side, comps, slot, True):
                one.start()

    def finish(side, comps, slot):
        @pl.when(exists(side))
        def _():
            for one in copies(side, comps, slot, False):
                one.wait()

    def quad(i, j):
        w = WEIGHTS
        scale = w[i] * w[j] / 8.0
        return jnp.concatenate(
            [half_row(scale * w[2 * kp], scale * w[min(2 * kp + 1, 4)], half) for kp in range(3)],
            axis=0,
        )

    def share(i, j):
        one = jnp.ones((1, 8, 128), F32)

        def along(n, bit, index, devices):
            if n == 0:
                return jnp.where((bit == 1) | (index > 0), 0.5, 1.0)
            if n == 4:
                return jnp.where((bit == 0) | (index < devices - 1), 0.5, 1.0)
            return one

        ab = along(i, bit_a, dom, nd) * along(j, bit_b, slab, ns)
        k0 = jnp.where((half == 0) & (lane > 0), 0.5, 1.0)
        k4 = jnp.where(lane < 127, 0.5, 1.0)
        return jnp.concatenate([ab * k0, ab * one, ab * k4], axis=0)

    loads[1].wait()
    loads[2].wait()
    load_pairs(U, raw_disp)
    load_pairs(CM, raw_density)
    for i in range(5):
        for j in range(5):
            F[3, i, j] = CM[i, j] * quad(i, j)
            for c in range(3):
                F[c, i, j] = U[c, i, j]
    local_sums(4, (0, 4, 1, 2, 3))
    pl.semaphore_wait(barrier, devices - 1)
    send_rows()
    pack(4, 0, ENDS + SLABS)
    for one in loads[3:]:
        one.wait()
    load_pairs(LAM, raw_lame)
    load_pairs(MU, raw_shear)
    load_pairs(W, raw_veloc)
    for i in range(5):
        for j in range(5):
            q = quad(i, j)
            LAM[i, j] = LAM[i, j] * q
            MU[i, j] = MU[i, j] * q

    def take_rows():
        finish_rows()
        ROWS[...] = IN[...].astype(F32).reshape(8 * devices, 128)
        for k in range(CAP):
            first = ROWS[pl.ds(k, devices, stride=8), :]
            second = ROWS[pl.ds(CAP + k, devices, stride=8), :]
            TT[0:128, k * devices : (k + 1) * devices] = first.T
            TT[128:256, k * devices : (k + 1) * devices] = second.T
            el = second[:, EL - 128 : EL - 127] + 256.0 * second[:, EL - 127 : EL - 126]
            cols = lax.broadcasted_iota(jnp.int32, (devices, 512), 1)
            OH[k * devices : (k + 1) * devices, :] = (
                (cols == el.astype(jnp.int32)).astype(F32).astype(BF16)
            )

    def deposit(s):
        for c in range(3):
            row = c * STEPS + s
            src = TT[pl.ds(HI + row, 1), :] + TT[pl.ds(LO + row, 1), :]
            term = TT[0:152, :] * src
            high = term.astype(BF16)
            low = (term - high.astype(F32)).astype(BF16)
            sums = jnp.dot(high, OH[...], preferred_element_type=F32) + jnp.dot(
                low, OH[...], preferred_element_type=F32
            )
            for a in range(2):
                for b in range(2):
                    q, first = b * 2 + a, (a * 2 + b) * 128
                    DEP[pl.ds(c * 600 + q, NODES6, stride=4), :] = sums[
                        0:NODES6, first : first + 128
                    ]

    unpack(4, 0, SLABS + ENDS)
    for i in range(5):
        for j in range(5):
            part = share(i, j)
            mass = close_k(F[3, i, j])
            CM[i, j] = (DT * DT) / mass
            scaled = mass * part * (1.0 / DT)
            for c in range(3):
                U[c, i, j] = close_k(F[c, i, j]) * part
                W[c, i, j] = W[c, i, j] * scaled

    pair = {(0, 0): 0, (1, 1): 1, (2, 2): 2, (0, 1): 3, (0, 2): 4, (1, 2): 5}

    def stress(c, d):
        return pair[(min(c, d), max(c, d))]

    def along_k(planes, js):
        for c in range(3):
            for i in planes:
                for first, last in js:
                    outs = kline(FORWARD, *(U[c, i, first:last, kp] for kp in range(3)), half)
                    for kp in range(3):
                        GR[2, c, i, first:last, kp] = outs[kp]

    def along_j(planes):
        for c in range(3):
            for i in planes:
                outs = line(FORWARD, [U[c, i, j] for j in range(5)])
                for j in range(5):
                    GR[1, c, i, j] = outs[j]

    def one_step(s, carry):
        along_j((0, 4))
        along_k((0, 4), ((0, 5),))
        for c in range(3):
            for j in range(5):
                outs = line(FORWARD, [U[c, i, j] for i in range(5)])
                for i in range(5):
                    GR[0, c, i, j] = outs[i]
        for i in range(5):
            for j in range(5):
                g = [[GR[d, c, i, j] for c in range(3)] for d in range(3)]
                mu = MU[i, j]
                mu2 = mu + mu
                vol = LAM[i, j] * (g[0][0] + g[1][1] + g[2][2])
                for c in range(3):
                    SG[c, i, j] = mu2 * g[c][c] + vol
                    for d in range(c):
                        SG[stress(c, d), i, j] = mu * (g[c][d] + g[d][c])
        slot = (s + 1) % 2
        force((0, 4))

        @pl.when(s == 0)
        def _():
            take_rows()
            deposit(0)
            for c in range(3):
                for i in range(5):
                    at = (c * 75 + i * 15) * 8
                    DEP[at : at + 120, :] = DEP[at : at + 120, :] + W[c, i].reshape(120, 128)
                    W[c, i] = jnp.zeros((5, 3, 8, 128), F32)

        local_sums(3, (0, 4), DEP)
        pack(3, slot, ENDS)
        force((1, 2, 3))
        local_sums(3, (1, 2, 3), DEP)
        pack(3, slot, SLABS)

        @pl.when(s < STEPS - 1)
        def _():
            deposit(s + 1)

        update([(i, j) for i in range(1, 4) for j in range(1, 4)])
        along_k((1, 2, 3), ((1, 4),))
        unpack(3, slot, SLABS)
        update([(i, j) for i in range(1, 4) for j in (0, 4)])

        @pl.when(s < STEPS - 1)
        def _():
            along_k((1, 2, 3), ((0, 1), (4, 5)))
            along_j((1, 2, 3))

        unpack(3, slot, ENDS)
        update([(i, j) for i in (0, 4) for j in range(5)])
        return carry

    def force(planes):
        for c in range(3):
            for j in range(5):
                outs = line(BACKWARD, [SG[stress(c, 0), i, j] for i in range(5)], planes)
                for i in planes:
                    F[c, i, j] = outs[i]
            for i in planes:
                outs = line(BACKWARD, [SG[stress(c, 1), i, j] for j in range(5)])
                for j in range(5):
                    F[c, i, j] = F[c, i, j] + outs[j]
                p = stress(c, 2)
                outs = kline(BACKWARD, SG[p, i, :, 0], SG[p, i, :, 1], SG[p, i, :, 2], half)
                for kp in range(3):
                    F[c, i, :, kp] = F[c, i, :, kp] + outs[kp]

    def update(lines):
        for i, j in lines:
            cm = CM[i, j]
            for c in range(3):
                w = W[c, i, j] + close_k(F[c, i, j]) * cm
                W[c, i, j] = w
                U[c, i, j] = U[c, i, j] + w

    along_k((1, 2, 3), ((0, 5),))
    along_j((1, 2, 3))
    lax.fori_loop(0, STEPS, one_step, 0)
    for i in range(5):
        for j in range(5):
            for c in range(3):
                U[c, i, j] = U[c, i, j] - W[c, i, j]
    store_pairs(disp_out, U)
    store_pairs(veloc_out, W)


def to_rows(x):
    lead = x.shape[:-2]
    n = len(lead)
    y = x.reshape(lead + (2, 2, EC))
    return jnp.swapaxes(y, n, n + 1).reshape(lead + (4, EC))


def from_rows(x):
    lead = x.shape[:-2]
    n = len(lead)
    y = jnp.swapaxes(x.reshape(lead + (2, 2, EC)), n, n + 1)
    return y.reshape(lead + (2, 2 * EC))


def shards(
    nd,
    ns,
    displacement,
    velocity,
    lame_lambda,
    shear_modulus,
    density,
    traces,
    section_weights,
    owner,
    element_idx,
    node_weights,
    encode_bits,
):
    devices = nd * ns
    rows = traces.shape[0]
    field = (5, 5, 3, 8, 128)
    vm = lambda *shape: pltpu.VMEM(shape, F32)
    tiles, scales, ends = sizes(4)
    messages = [pltpu.VMEM((2, tiles, 16, 128), jnp.int16) for side in range(4)]
    messages += [vm(2, ends, 8, 128) for side in range(4)]
    factors = [vm(2, scales, 8, 128) for side in range(4)]
    out = jax.ShapeDtypeStruct((3, 5, 5, 5, 4, EC), F32)
    disp, veloc = pl.pallas_call(
        functools.partial(step_kernel, nd, ns),
        out_shape=(out, out),
        in_specs=[pl.BlockSpec(memory_space=pltpu.HBM)] * 11,
        out_specs=(pl.BlockSpec(memory_space=pltpu.VMEM),) * 2,
        scratch_shapes=[
            pltpu.VMEM(section_weights.shape, BF16),
            pltpu.VMEM((1, rows), jnp.int32),
            pltpu.VMEM((1, rows), jnp.int32),
            pltpu.VMEM(node_weights.shape, BF16),
            pltpu.VMEM((G, rows), jnp.int32),
            vm(3, 5, 5, 5, 4, EC),
            vm(3, 5, 5, 5, 4, EC),
            vm(5, 5, 5, 4, EC),
            vm(5, 5, 5, 4, EC),
            vm(5, 5, 5, 4, EC),
            pltpu.VMEM(traces.shape, BF16),
            pltpu.VMEM((CAP, devices, rows), BF16),
            vm(rows, 256),
            vm(3, 128, section_weights.shape[1]),
            vm(8 * devices, 128),
            pltpu.VMEM((devices, 8, 128), BF16),
            pltpu.VMEM((devices, 8, 128), BF16),
            vm(3, *field),
            vm(3, *field),
            vm(*field),
            vm(*field),
            vm(*field),
            vm(3, 3, *field),
            vm(6, *field),
            vm(4, *field),
            vm(1808, 128),
            vm(256, CAP * devices),
            pltpu.VMEM((CAP * devices, 512), BF16),
            *messages,
            *messages,
            *factors,
            *factors,
            pltpu.SemaphoreType.DMA((12, 2)),
            pltpu.SemaphoreType.DMA((12, 2)),
            pltpu.SemaphoreType.DMA((12,)),
            pltpu.SemaphoreType.DMA,
            pltpu.SemaphoreType.DMA,
        ],
        compiler_params=pltpu.CompilerParams(
            collective_id=1, has_side_effects=True, vmem_limit_bytes=28 * 2**20
        ),
        name="time_steps",
    )(
        *(
            pltpu.with_memory_space_constraint(x, pltpu.HBM)
            for x in (
                to_rows(displacement),
                to_rows(velocity),
                to_rows(lame_lambda),
                to_rows(shear_modulus),
                to_rows(density),
                traces,
                section_weights,
                owner.reshape(1, rows),
                element_idx.reshape(1, rows),
                node_weights,
                encode_bits.T,
            )
        )
    )
    return from_rows(disp + veloc), from_rows(veloc * (1.0 / DT))


def solution(mesh):
    nd, ns = mesh.shape["dom"], mesh.shape["slab"]
    both = P(("dom", "slab"), None)
    fields = P(None, None, None, None, "dom", "slab")
    params = P(None, None, None, "dom", "slab")
    return jax.shard_map(
        functools.partial(shards, nd, ns),
        mesh=mesh,
        in_specs=(
            fields,
            fields,
            params,
            params,
            params,
            both,
            P(),
            both,
            P(("dom", "slab")),
            both,
            both,
        ),
        out_specs=(fields, fields),
        check_vma=False,
    )
```

```python
import functools
import math

import jax
import jax.numpy as jnp
import numpy as np
from jax import lax
from jax.experimental import pallas as pl
from jax.experimental.pallas import tpu as pltpu
from jax.sharding import PartitionSpec as P

EC = 128
CAP = 4
G = 4
STEPS = 4
DT = 0.025
NODES6 = 150
HI, LO, EL = 160, 176, 192
F32, BF16 = jnp.float32, jnp.bfloat16
MESH = pl.DeviceIdType.MESH


def gll():
    inner_point = math.sqrt(3.0 / 7.0)
    points = np.array([-1.0, -inner_point, 0.0, inner_point, 1.0])
    weights = np.array([0.1, 49.0 / 90.0, 32.0 / 45.0, 49.0 / 90.0, 0.1])
    legendre = (35.0 * points**4 - 30.0 * points**2 + 3.0) / 8.0
    derivative = np.zeros((5, 5))
    for i in range(5):
        for j in range(5):
            if i != j:
                derivative[i, j] = legendre[i] / (legendre[j] * (points[i] - points[j]))
    derivative[0, 0] = -5.0
    derivative[4, 4] = 5.0
    return 2.0 * derivative, weights


D2, WEIGHTS = gll()
FORWARD, BACKWARD = D2, -D2.T


def choose_rows(devices, weights, owner, nodew, choose, wide, wsel):
    rows = nodew.shape[0]
    wsel[...] = jnp.zeros_like(wsel)
    for c in range(3):
        wsel[c, c * STEPS : (c + 1) * STEPS, :] = weights[...].astype(F32)
    node = lax.broadcasted_iota(jnp.int32, (125, 256), 0)
    column = lax.broadcasted_iota(jnp.int32, (125, 256), 1)
    slot6 = (node // 5) * 6 + node % 5
    spread = (column == slot6) | ((node % 5 == 4) & (column == slot6 + 1))
    wide[...] = jnp.dot(nodew[...], spread.astype(F32).astype(BF16), preferred_element_type=F32)
    device = lax.broadcasted_iota(jnp.int32, (devices, rows), 0)
    member = (owner[...] == device).astype(F32)
    earlier = lax.broadcasted_iota(jnp.int32, (rows, rows), 0) < lax.broadcasted_iota(
        jnp.int32, (rows, rows), 1
    )
    before = jnp.dot(
        member.astype(BF16), earlier.astype(F32).astype(BF16), preferred_element_type=F32
    )
    for k in range(CAP):
        choose[k] = jnp.where(before == float(k), member, 0.0).astype(BF16)


def pack_first(devices, choose, wide, out):
    right = wide[:, :128].astype(BF16)
    for k in range(CAP):
        out[pl.ds(k, devices, stride=8), :] = jnp.dot(
            choose[k], right, preferred_element_type=F32
        )


def pack_second(devices, traces, element, bits, choose, wide, wsel, out):
    rows = traces.shape[0]
    nt = wsel.shape[2]
    signs = (2 * bits[...] - 1).astype(F32).T.astype(BF16)
    sources = []
    for c in range(3):
        source = jnp.zeros((rows, 128), F32)
        for g in range(G):
            first = (g * 3 + c) * nt
            block = traces[:, first : first + nt] * signs[:, g : g + 1]
            source = source + lax.dot_general(
                block,
                wsel[c].astype(BF16),
                (((1,), (1,)), ((), ())),
                preferred_element_type=F32,
            )
        sources.append(source)
    source = sources[0] + sources[1] + sources[2]
    high = source.astype(BF16).astype(F32)
    low = source - high
    lane = lax.broadcasted_iota(jnp.int32, (rows, 128), 1)
    where_el = jnp.broadcast_to(element[...], (128, rows)).astype(F32).T
    el_high = jnp.floor(where_el * (1.0 / 256.0))
    el_low = where_el - 256.0 * el_high
    extra = pltpu.roll(high, HI - 128, 1) + pltpu.roll(low, LO - 128, 1)
    extra = jnp.where(lane == EL - 128, el_low, extra)
    extra = jnp.where(lane == EL - 127, el_high, extra)
    right = (wide[:, 128:] + extra).astype(BF16)
    for k in range(CAP):
        out[pl.ds(CAP + k, devices, stride=8), :] = jnp.dot(
            choose[k], right, preferred_element_type=F32
        )


def line(m, u, wanted=(0, 1, 2, 3, 4)):
    e0, e1, o0, o1 = u[0] + u[4], u[1] + u[3], u[0] - u[4], u[1] - u[3]
    out = {}
    for i in range(2):
        if i in wanted or 4 - i in wanted:
            ce = [float((m[i, l] + m[i, 4 - l]) / 2) for l in range(2)]
            co = [float((m[i, l] - m[i, 4 - l]) / 2) for l in range(2)]
            even = ce[0] * e0 + ce[1] * e1 + float(m[i, 2]) * u[2]
            odd = co[0] * o0 + co[1] * o1
            out[i], out[4 - i] = odd + even, odd - even
    if 2 in wanted:
        out[2] = float(m[2, 0]) * o0 + float(m[2, 1]) * o1
    return out


def half_row(lower, upper, half):
    return jnp.where(half == 0, float(lower), float(upper)).astype(F32)


def kline(m, p0, p1, p2, half):
    first = half == 0
    ce = [[(m[i, l] + m[i, 4 - l]) / 2 for l in range(2)] for i in range(2)]
    co = [[(m[i, l] - m[i, 4 - l]) / 2 for l in range(2)] for i in range(2)]
    back = jnp.where(first, p2, p1)
    even, odd = p0 + back, p0 - back
    mid = jnp.where(first, p1, pltpu.roll(p1, 4, 1))
    evens, odds = pltpu.roll(even, 4, 1), pltpu.roll(odd, 4, 1)
    eout = (
        half_row(ce[0][0], ce[1][1], half) * even
        + half_row(ce[0][1], ce[1][0], half) * evens
        + half_row(m[0, 2], m[1, 2], half) * mid
    )
    oout = half_row(co[0][0], co[1][1], half) * odd + half_row(co[0][1], co[1][0], half) * odds
    q0 = eout + oout
    q43 = oout - eout
    q22 = half_row(m[2, 0], m[2, 1], half) * odd + half_row(m[2, 1], m[2, 0], half) * odds
    q1 = jnp.where(first, q22, q43)
    q2 = jnp.where(first, q43, pltpu.roll(q43, 4, 1))
    return q0, q1, q2


SIDES = [(-1, 0), (1, 0), (0, -1), (0, 1), (-1, -1), (-1, 1), (1, -1), (1, 1)]
OPPOSITE = [1, 0, 3, 2, 7, 6, 5, 4]
ENDS, SLABS = (0, 1, 4, 5, 6, 7), (2, 3)


GROUPS = {3: ((0, 1, 2),), 4: ((0, 1, 2), (3,))}


def tiles_of(group):
    return (5 * len(group) + 2) // 2


def far_first(nd, ns):
    zs = max(nd // 4, 1)

    def ring(d, n):
        return min(d % n, -d % n)

    def way(k, j):
        total = 0
        for d in range(nd):
            e = (d + k) % nd
            total += ns * (2 * (d // (2 * zs) != e // (2 * zs)) + ring(d // 2 - e // 2, zs))
        for b in range(ns):
            e = (b + j) % ns
            total += nd * (ring(b // 2 - e // 2, max(ns // 2, 1)) + (b % 2 != e % 2))
        return total

    steps = [(k, j) for k in range(nd) for j in range(ns) if (k, j) != (0, 0)]
    return sorted(steps, key=lambda step: (-way(*step), step))


def sizes(comps):
    groups = GROUPS[comps]
    return sum(tiles_of(g) for g in groups), len(groups), (comps + 2) // 2


def step_kernel(
    nd,
    ns,
    disp,
    veloc,
    lame,
    shear,
    density,
    traces,
    weights_in,
    owner_in,
    element_in,
    nodew_in,
    bits_in,
    disp_out,
    veloc_out,
    weights,
    owner,
    element,
    nodew,
    bits,
    raw_disp,
    raw_veloc,
    raw_lame,
    raw_shear,
    raw_density,
    raw_traces,
    CHOOSE,
    WIDE,
    WSEL,
    ROWS,
    OUT,
    IN,
    U,
    W,
    LAM,
    MU,
    CM,
    GR,
    SG,
    F,
    DEP,
    TT,
    OH,
    LEFT,
    *rest,
):
    send, recv = rest[0:8], rest[8:16]
    send_scale, recv_scale = rest[16:20], rest[20:24]
    send_sem, recv_sem, load_sem, all_send, all_recv = rest[24:29]
    dom, slab = lax.axis_index("dom"), lax.axis_index("slab")

    def exists(side):
        da, db = SIDES[side]
        cond = None
        for shift, index, count in ((da, dom, nd), (db, slab, ns)):
            if shift:
                one = index > 0 if shift < 0 else index < count - 1
                cond = one if cond is None else jnp.logical_and(cond, one)
        return cond

    def target(side):
        return (dom + SIDES[side][0], slab + SIDES[side][1])

    for side in range(8):

        @pl.when(jnp.logical_not(exists(side)))
        def _():
            recv[side][...] = jnp.zeros_like(recv[side])
            if side < 4:
                recv_scale[side][...] = jnp.zeros_like(recv_scale[side])

    devices = nd * ns
    me = dom * ns + slab
    barrier = pltpu.get_barrier_semaphore()

    doms = [lax.rem(dom + k, nd) for k in range(nd)]
    slabs = [lax.rem(slab + k, ns) for k in range(ns)]
    order = far_first(nd, ns)

    loads = [
        pltpu.make_async_copy(src, dst, load_sem.at[n])
        for n, (src, dst) in enumerate(
            (
                (traces, raw_traces),
                (disp, raw_disp),
                (density, raw_density),
                (lame, raw_lame),
                (shear, raw_shear),
                (veloc, raw_veloc),
            )
        )
    ]
    small = [
        pltpu.make_async_copy(src, dst, load_sem.at[7 + n])
        for n, (src, dst) in enumerate(
            (
                (owner_in, owner),
                (nodew_in, nodew),
                (weights_in, weights),
                (bits_in, bits),
                (element_in, element),
            )
        )
    ]
    for one in small + loads[:3]:
        one.start()
    for k, j in order:
        pl.semaphore_signal(
            barrier, inc=1, device_id=(doms[k], slabs[j]), device_id_type=MESH
        )
    own_rows = pltpu.make_async_copy(OUT.at[me], IN.at[me], load_sem.at[6])

    def send_rows():
        own_rows.start()
        for k, j in order:
            pltpu.make_async_remote_copy(
                src_ref=OUT.at[doms[k] * ns + slabs[j]],
                dst_ref=IN.at[me],
                send_sem=all_send,
                recv_sem=all_recv,
                device_id=(doms[k], slabs[j]),
                device_id_type=MESH,
            ).start()

    def finish_rows():
        own_rows.wait()
        k, j = order[0]
        pltpu.make_async_remote_copy(
            src_ref=OUT.at[pl.ds(0, devices - 1)],
            dst_ref=IN.at[pl.ds(0, devices - 1)],
            send_sem=all_send,
            recv_sem=all_recv,
            device_id=(doms[k], slabs[j]),
            device_id_type=MESH,
        ).wait()

    for one in small:
        one.wait()
    choose_rows(devices, weights, owner, nodew, CHOOSE, WIDE, WSEL)
    pack_first(devices, CHOOSE, WIDE, ROWS)
    loads[0].wait()
    for one in loads[3:]:
        one.start()
    pack_second(devices, raw_traces, element, bits, CHOOSE, WIDE, WSEL, ROWS)
    OUT[...] = ROWS[...].reshape(devices, 8, 128).astype(BF16)

    sub = lax.broadcasted_iota(jnp.int32, (1, 8, 128), 1)
    lane = lax.broadcasted_iota(jnp.int32, (1, 8, 128), 2)
    half, bit_b, bit_a = sub // 4, (sub // 2) % 2, sub % 2

    def roll_s(x, shift):
        return pltpu.roll(x, shift % 8, 1)

    def roll_l(x, shift):
        return pltpu.roll(x, shift % 128, 2)

    def load_pairs(dst, src):
        lead = (slice(None),) * (len(dst.shape) - 3)
        for kp in range(3):
            dst[lead + (kp, slice(0, 4))] = src[lead + (2 * kp,)]
            dst[lead + (kp, slice(4, 8))] = src[lead + (min(2 * kp + 1, 4),)]

    def local_sums(comps, planes, extra=None):
        for c in range(comps):
            for i in planes:
                p0, p1, p2 = (F[c, i, :, kp] for kp in range(3))
                if extra is not None:
                    at = (c * 75 + i * 15) * 8
                    add = extra[at : at + 120, :].reshape(5, 3, 8, 128)
                    p0, p2 = p0 + add[:, 0], p2 + add[:, 2]
                    F[c, i, :, 1] = p1 + add[:, 1]
                    F[c, i, :, 2] = p2
                F[c, i, :, 0] = p0 + jnp.where((half == 0) & (lane > 0), roll_l(p2, 1), 0.0)
            if 0 in planes:
                for j in range(5):
                    x0, x4 = F[c, 0, j], F[c, 4, j]
                    F[c, 0, j] = x0 + jnp.where(bit_a == 1, roll_s(x4, 1), 0.0)
                    F[c, 4, j] = x4 + jnp.where(bit_a == 0, roll_s(x0, -1), 0.0)
            for i in planes:
                x0, x4 = F[c, i, 0], F[c, i, 4]
                F[c, i, 0] = x0 + jnp.where(bit_b == 1, roll_s(x4, 2), 0.0)
                F[c, i, 4] = x4 + jnp.where(bit_b == 0, roll_s(x0, -2), 0.0)

    def close_k(x):
        x0 = x[0:1]
        dup = jnp.where(half == 0, x0, roll_s(x0, 4))
        x2 = jnp.where(lane < 127, roll_l(dup, -1), x[2:3])
        return jnp.concatenate([x[0:2], x2], axis=0)

    def merge(x, y, bit, width, value):
        toward = width if value == 0 else -width
        return jnp.where(bit == value, x, roll_s(y, toward))

    def unmerge(m, bit, width, value):
        toward = -width if value == 0 else width
        keep = bit == value
        return jnp.where(keep, roll_s(m, toward), 0.0), jnp.where(keep, m, 0.0)

    def ends(zs):
        out = jnp.zeros((1, 8, 128), F32)
        for n, z in enumerate(zs):
            out = jnp.where(lane == n, roll_l(z, n + 1), out)
        return out

    def end_of(row, n):
        return jnp.where(lane == 127, roll_l(row, 127 - n), 0.0)

    def face(side):
        axis, value = side // 2, side % 2
        bit, width = ((bit_a, 1), (bit_b, 2))[axis]
        node = 4 * value

        def at(c, n, kp):
            return (c, node, n, kp) if axis == 0 else (c, n, node, kp)

        def line_at(c, kp):
            return (c, node, slice(None), kp) if axis == 0 else (c, slice(None), node, kp)

        return bit, width, value, at, line_at

    def pack(comps, slot, sides):
        for side in [side for side in sides if side < 4]:
            bit, width, value, at, line_at = face(side)
            tile = 0
            for g, group in enumerate(GROUPS[comps]):
                rows = []
                for c in group:
                    merged = merge(F[line_at(c, 0)], F[line_at(c, 1)], bit, width, value)
                    rows.extend(merged[n : n + 1] for n in range(5))
                rows.append(ends([F[at(c, n, 2)][None] for c in group for n in range(5)]))
                largest = jnp.abs(rows[0])
                for row in rows[1:]:
                    largest = jnp.maximum(largest, jnp.abs(row))
                for shift in (4, 2, 1):
                    largest = jnp.maximum(largest, roll_s(largest, shift))
                scale = largest * (1.0 / 32000.0) + 1e-30
                send_scale[side][slot, g : g + 1] = scale[:, 0:1]
                inverse = 1.0 / scale
                for n in range(0, len(rows), 2):
                    x = jnp.concatenate([rows[n][0] * inverse[0], rows[n + 1][0] * inverse[0]], 0)
                    x = x + jnp.where(x < 0.0, -0.5, 0.5)
                    send[side][slot, tile] = x.astype(jnp.int32).astype(jnp.int16)
                    tile += 1
            start(side, comps, slot)
        pack_corners(comps, slot, [side for side in sides if side >= 4])

    def pack_corners(comps, slot, sides):
        for side in sides:
            da, db = SIDES[side]
            va, vb = (da + 1) // 2, (db + 1) // 2
            items = []
            for c in range(comps):
                x = F[c, 4 * va, 4 * vb]
                items.append(merge(x[0:1], x[1:2], bit_a, 1, va))
            items.append(ends([F[c, 4 * va, 4 * vb, 2:3] for c in range(comps)]))
            for n in range(0, len(items), 2):
                y = items[min(n + 1, len(items) - 1)]
                send[side][slot, n // 2 : n // 2 + 1] = merge(items[n], y, bit_b, 2, vb)
            start(side, comps, slot)

    def unpack(comps, slot, sides):
        for side in [side for side in sides if side < 4]:
            finish(side, comps, slot)
            bit, width, value, at, line_at = face(side)
            tile = 0
            for g, group in enumerate(GROUPS[comps]):
                scale = jnp.broadcast_to(recv_scale[side][slot, g : g + 1], (1, 8, 128))
                rows = []
                for _ in range(tiles_of(group)):
                    x = recv[side][slot, tile].astype(jnp.int32).astype(F32)
                    rows.extend([x[None, 0:8] * scale, x[None, 8:16] * scale])
                    tile += 1
                for m, c in enumerate(group):
                    merged = jnp.concatenate(rows[5 * m : 5 * m + 5], axis=0)
                    for kp, add in enumerate(unmerge(merged, bit, width, value)):
                        F[line_at(c, kp)] = F[line_at(c, kp)] + add
                last, _ = unmerge(rows[5 * len(group)], bit, width, value)
                for m, c in enumerate(group):
                    for n in range(5):
                        F[at(c, n, 2)] = F[at(c, n, 2)] + end_of(last, 5 * m + n)[0]
        for side in [side for side in sides if side >= 4]:
            da, db = SIDES[side]
            va, vb = (da + 1) // 2, (db + 1) // 2
            items = []
            finish(side, comps, slot)
            for n in range(sizes(comps)[2]):
                items.extend(unmerge(recv[side][slot, n : n + 1], bit_b, 2, vb))
            last, _ = unmerge(items[comps], bit_a, 1, va)
            for c in range(comps):
                x, y = unmerge(items[c], bit_a, 1, va)
                add = jnp.concatenate([x, y, end_of(last, c)], axis=0)
                F[c, 4 * va, 4 * vb] = F[c, 4 * va, 4 * vb] + add

    def copies(side, comps, slot, source):
        tiles, scales, rows = sizes(comps)
        parts = [(send, recv, tiles, side)] if side < 4 else [(send, recv, rows, side)]
        if side < 4:
            parts.append((send_scale, recv_scale, scales, 8 + side))
        out = []
        for src, dst, count, number in parts:
            there = number - side + OPPOSITE[side] if source else number
            out.append(
                pltpu.make_async_remote_copy(
                    src_ref=src[side].at[slot, pl.ds(0, count)],
                    dst_ref=dst[OPPOSITE[side] if source else side].at[slot, pl.ds(0, count)],
                    send_sem=send_sem.at[number, slot],
                    recv_sem=recv_sem.at[there, slot],
                    device_id=target(side),
                    device_id_type=MESH,
                )
            )
        return out

    def start(side, comps, slot):
        @pl.when(exists(side))
        def _():
            for one in copies(side, comps, slot, True):
                one.start()

    def finish(side, comps, slot):
        @pl.when(exists(side))
        def _():
            for one in copies(side, comps, slot, False):
                one.wait()

    def quad(i, j):
        w = WEIGHTS
        scale = w[i] * w[j] / 8.0
        return jnp.concatenate(
            [half_row(scale * w[2 * kp], scale * w[min(2 * kp + 1, 4)], half) for kp in range(3)],
            axis=0,
        )

    def share(i, j):
        one = jnp.ones((1, 8, 128), F32)

        def along(n, bit, index, devices):
            if n == 0:
                return jnp.where((bit == 1) | (index > 0), 0.5, 1.0)
            if n == 4:
                return jnp.where((bit == 0) | (index < devices - 1), 0.5, 1.0)
            return one

        ab = along(i, bit_a, dom, nd) * along(j, bit_b, slab, ns)
        k0 = jnp.where((half == 0) & (lane > 0), 0.5, 1.0)
        k4 = jnp.where(lane < 127, 0.5, 1.0)
        return jnp.concatenate([ab * k0, ab * one, ab * k4], axis=0)

    loads[1].wait()
    loads[2].wait()
    load_pairs(U, raw_disp)
    load_pairs(CM, raw_density)
    for i in range(5):
        for j in range(5):
            F[3, i, j] = CM[i, j] * quad(i, j)
            for c in range(3):
                F[c, i, j] = U[c, i, j]
    local_sums(4, (0, 4, 1, 2, 3))
    pl.semaphore_wait(barrier, devices - 1)
    send_rows()
    pack(4, 0, ENDS + SLABS)
    for one in loads[3:]:
        one.wait()
    load_pairs(LAM, raw_lame)
    load_pairs(MU, raw_shear)
    load_pairs(W, raw_veloc)
    for i in range(5):
        for j in range(5):
            q = quad(i, j)
            LAM[i, j] = LAM[i, j] * q
            MU[i, j] = MU[i, j] * q

    def take_rows():
        finish_rows()
        ROWS[...] = IN[...].astype(F32).reshape(8 * devices, 128)
        for k in range(CAP):
            first = ROWS[pl.ds(k, devices, stride=8), :]
            second = ROWS[pl.ds(CAP + k, devices, stride=8), :]
            TT[0:128, k * devices : (k + 1) * devices] = first.T
            TT[128:256, k * devices : (k + 1) * devices] = second.T
            el = second[:, EL - 128 : EL - 127] + 256.0 * second[:, EL - 127 : EL - 126]
            cols = lax.broadcasted_iota(jnp.int32, (devices, 512), 1)
            OH[k * devices : (k + 1) * devices, :] = (
                (cols == el.astype(jnp.int32)).astype(F32).astype(BF16)
            )

    def deposit(s):
        for c in range(3):
            row = c * STEPS + s
            src = TT[pl.ds(HI + row, 1), :] + TT[pl.ds(LO + row, 1), :]
            term = TT[0:160, :] * src
            high = term.astype(BF16)
            LEFT[c * 320 : c * 320 + 160, :] = high
            LEFT[c * 320 + 160 : c * 320 + 320, :] = (term - high.astype(F32)).astype(BF16)
        sums = jnp.dot(LEFT[...], OH[...], preferred_element_type=F32)
        for c in range(3):
            first = c * 320
            both = sums[first : first + 152, :] + sums[first + 160 : first + 312, :]
            for a in range(2):
                for b in range(2):
                    q, col = b * 2 + a, (a * 2 + b) * 128
                    DEP[pl.ds(c * 600 + q, NODES6, stride=4), :] = both[
                        0:NODES6, col : col + 128
                    ]

    def begin(lines):
        for i, j in lines:
            part = share(i, j)
            mass = close_k(F[3, i, j])
            CM[i, j] = (DT * DT) / mass
            scaled = mass * part * (1.0 / DT)
            for c in range(3):
                U[c, i, j] = close_k(F[c, i, j]) * part
                W[c, i, j] = W[c, i, j] * scaled

    inner = [(i, j) for i in range(1, 4) for j in range(1, 4)]
    rims = [(i, j) for i in range(1, 4) for j in (0, 4)]
    outer = [(i, j) for i in (0, 4) for j in range(5)]

    pair = {(0, 0): 0, (1, 1): 1, (2, 2): 2, (0, 1): 3, (0, 2): 4, (1, 2): 5}

    def stress(c, d):
        return pair[(min(c, d), max(c, d))]

    def along_k(planes, js):
        for c in range(3):
            for i in planes:
                for first, last in js:
                    outs = kline(FORWARD, *(U[c, i, first:last, kp] for kp in range(3)), half)
                    for kp in range(3):
                        GR[2, c, i, first:last, kp] = outs[kp]

    def along_j(planes):
        for c in range(3):
            for i in planes:
                outs = line(FORWARD, [U[c, i, j] for j in range(5)])
                for j in range(5):
                    GR[1, c, i, j] = outs[j]

    def one_step(s, carry):
        along_j((0, 4))
        along_k((0, 4), ((0, 5),))
        for c in range(3):
            for j in range(5):
                outs = line(FORWARD, [U[c, i, j] for i in range(5)])
                for i in range(5):
                    GR[0, c, i, j] = outs[i]
        for i in range(5):
            for j in range(5):
                g = [[GR[d, c, i, j] for c in range(3)] for d in range(3)]
                mu = MU[i, j]
                mu2 = mu + mu
                vol = LAM[i, j] * (g[0][0] + g[1][1] + g[2][2])
                for c in range(3):
                    SG[c, i, j] = mu2 * g[c][c] + vol
                    for d in range(c):
                        SG[stress(c, d), i, j] = mu * (g[c][d] + g[d][c])
        slot = (s + 1) % 2
        force((0, 4))

        @pl.when(s == 0)
        def _():
            take_rows()
            deposit(0)
            for c in range(3):
                for i in range(5):
                    at = (c * 75 + i * 15) * 8
                    DEP[at : at + 120, :] = DEP[at : at + 120, :] + W[c, i].reshape(120, 128)
                    W[c, i] = jnp.zeros((5, 3, 8, 128), F32)

        local_sums(3, (0, 4), DEP)
        pack(3, slot, ENDS)
        force((1, 2, 3))

        local_sums(3, (1, 2, 3), DEP)
        pack(3, slot, SLABS)

        @pl.when(s < STEPS - 1)
        def _():
            deposit(s + 1)

        update(inner)
        along_k((1, 2, 3), ((1, 4),))
        unpack(3, slot, SLABS)
        update(rims)

        @pl.when(s < STEPS - 1)
        def _():
            along_k((1, 2, 3), ((0, 1), (4, 5)))
            along_j((1, 2, 3))

        unpack(3, slot, ENDS)
        update(outer)
        return carry

    def leave(planes):
        for c in range(3):
            for i in planes:
                U[c, i] = U[c, i] - W[c, i]
                for k in range(5):
                    rows = slice(4 * (k % 2), 4 * (k % 2) + 4)
                    disp_out[c, i, :, k] = U[c, i, :, k // 2, rows]
                    veloc_out[c, i, :, k] = W[c, i, :, k // 2, rows]

    def force(planes):
        for c in range(3):
            for j in range(5):
                outs = line(BACKWARD, [SG[stress(c, 0), i, j] for i in range(5)], planes)
                for i in planes:
                    F[c, i, j] = outs[i]
            for i in planes:
                outs = line(BACKWARD, [SG[stress(c, 1), i, j] for j in range(5)])
                for j in range(5):
                    F[c, i, j] = F[c, i, j] + outs[j]
                p = stress(c, 2)
                outs = kline(BACKWARD, SG[p, i, :, 0], SG[p, i, :, 1], SG[p, i, :, 2], half)
                for kp in range(3):
                    F[c, i, :, kp] = F[c, i, :, kp] + outs[kp]

    def update(lines):
        for i, j in lines:
            cm = CM[i, j]
            for c in range(3):
                w = W[c, i, j] + close_k(F[c, i, j]) * cm
                W[c, i, j] = w
                U[c, i, j] = U[c, i, j] + w

    begin(inner)
    along_k((1, 2, 3), ((1, 4),))
    unpack(4, 0, SLABS)
    begin(rims)
    along_k((1, 2, 3), ((0, 1), (4, 5)))
    along_j((1, 2, 3))
    unpack(4, 0, ENDS)
    begin(outer)
    lax.fori_loop(0, STEPS, one_step, 0)
    leave((0, 1, 2, 3, 4))


def to_rows(x):
    lead = x.shape[:-2]
    n = len(lead)
    y = x.reshape(lead + (2, 2, EC))
    return jnp.swapaxes(y, n, n + 1).reshape(lead + (4, EC))


def from_rows(x):
    lead = x.shape[:-2]
    n = len(lead)
    y = jnp.swapaxes(x.reshape(lead + (2, 2, EC)), n, n + 1)
    return y.reshape(lead + (2, 2 * EC))


def shards(
    nd,
    ns,
    displacement,
    velocity,
    lame_lambda,
    shear_modulus,
    density,
    traces,
    section_weights,
    owner,
    element_idx,
    node_weights,
    encode_bits,
):
    devices = nd * ns
    rows = traces.shape[0]
    field = (5, 5, 3, 8, 128)
    vm = lambda *shape: pltpu.VMEM(shape, F32)
    tiles, scales, ends = sizes(4)
    messages = [pltpu.VMEM((2, tiles, 16, 128), jnp.int16) for side in range(4)]
    messages += [vm(2, ends, 8, 128) for side in range(4)]
    factors = [vm(2, scales, 1, 128) for side in range(4)]
    out = jax.ShapeDtypeStruct((3, 5, 5, 5, 4, EC), F32)
    disp, veloc = pl.pallas_call(
        functools.partial(step_kernel, nd, ns),
        out_shape=(out, out),
        in_specs=[pl.BlockSpec(memory_space=pltpu.HBM)] * 11,
        out_specs=(pl.BlockSpec(memory_space=pltpu.VMEM),) * 2,
        scratch_shapes=[
            pltpu.VMEM(section_weights.shape, BF16),
            pltpu.VMEM((1, rows), jnp.int32),
            pltpu.VMEM((1, rows), jnp.int32),
            pltpu.VMEM(node_weights.shape, BF16),
            pltpu.VMEM((G, rows), jnp.int32),
            vm(3, 5, 5, 5, 4, EC),
            vm(3, 5, 5, 5, 4, EC),
            vm(5, 5, 5, 4, EC),
            vm(5, 5, 5, 4, EC),
            vm(5, 5, 5, 4, EC),
            pltpu.VMEM(traces.shape, BF16),
            pltpu.VMEM((CAP, devices, rows), BF16),
            vm(rows, 256),
            vm(3, 128, section_weights.shape[1]),
            vm(8 * devices, 128),
            pltpu.VMEM((devices, 8, 128), BF16),
            pltpu.VMEM((devices, 8, 128), BF16),
            vm(3, *field),
            vm(3, *field),
            vm(*field),
            vm(*field),
            vm(*field),
            vm(3, 3, *field),
            vm(6, *field),
            vm(4, *field),
            vm(1808, 128),
            vm(256, CAP * devices),
            pltpu.VMEM((CAP * devices, 512), BF16),
            pltpu.VMEM((960, CAP * devices), BF16),
            *messages,
            *messages,
            *factors,
            *factors,
            pltpu.SemaphoreType.DMA((12, 2)),
            pltpu.SemaphoreType.DMA((12, 2)),
            pltpu.SemaphoreType.DMA((12,)),
            pltpu.SemaphoreType.DMA,
            pltpu.SemaphoreType.DMA,
        ],
        compiler_params=pltpu.CompilerParams(
            collective_id=1, has_side_effects=True, vmem_limit_bytes=28 * 2**20
        ),
        name="time_steps",
    )(
        *(
            pltpu.with_memory_space_constraint(x, pltpu.HBM)
            for x in (
                to_rows(displacement),
                to_rows(velocity),
                to_rows(lame_lambda),
                to_rows(shear_modulus),
                to_rows(density),
                traces,
                section_weights,
                owner.reshape(1, rows),
                element_idx.reshape(1, rows),
                node_weights,
                encode_bits.T,
            )
        )
    )
    return from_rows(disp + veloc), from_rows(veloc * (1.0 / DT))


def solution(mesh):
    nd, ns = mesh.shape["dom"], mesh.shape["slab"]
    both = P(("dom", "slab"), None)
    fields = P(None, None, None, None, "dom", "slab")
    params = P(None, None, None, "dom", "slab")
    return jax.shard_map(
        functools.partial(shards, nd, ns),
        mesh=mesh,
        in_specs=(
            fields,
            fields,
            params,
            params,
            params,
            both,
            P(),
            both,
            P(("dom", "slab")),
            both,
            both,
        ),
        out_specs=(fields, fields),
        check_vma=False,
    )
```

```python
import functools
import math

import jax
import jax.numpy as jnp
import numpy as np
from jax import lax
from jax.experimental import pallas as pl
from jax.experimental.pallas import tpu as pltpu
from jax.sharding import PartitionSpec as P

EC = 128
CAP = 4
G = 4
STEPS = 4
DT = 0.025
NODES6 = 150
HI, LO, EL = 160, 176, 192
F32, BF16 = jnp.float32, jnp.bfloat16
MESH = pl.DeviceIdType.MESH


def gll():
    inner_point = math.sqrt(3.0 / 7.0)
    points = np.array([-1.0, -inner_point, 0.0, inner_point, 1.0])
    weights = np.array([0.1, 49.0 / 90.0, 32.0 / 45.0, 49.0 / 90.0, 0.1])
    legendre = (35.0 * points**4 - 30.0 * points**2 + 3.0) / 8.0
    derivative = np.zeros((5, 5))
    for i in range(5):
        for j in range(5):
            if i != j:
                derivative[i, j] = legendre[i] / (legendre[j] * (points[i] - points[j]))
    derivative[0, 0] = -5.0
    derivative[4, 4] = 5.0
    return 2.0 * derivative, weights


D2, WEIGHTS = gll()
FORWARD, BACKWARD = D2, -D2.T


def choose_rows(devices, weights, owner, nodew, choose, wide, wsel):
    rows = nodew.shape[0]
    wsel[...] = jnp.zeros_like(wsel)
    for c in range(3):
        wsel[c, c * STEPS : (c + 1) * STEPS, :] = weights[...].astype(F32)
    node = lax.broadcasted_iota(jnp.int32, (125, 256), 0)
    column = lax.broadcasted_iota(jnp.int32, (125, 256), 1)
    slot6 = (node // 5) * 6 + node % 5
    spread = (column == slot6) | ((node % 5 == 4) & (column == slot6 + 1))
    wide[...] = jnp.dot(nodew[...], spread.astype(F32).astype(BF16), preferred_element_type=F32)
    device = lax.broadcasted_iota(jnp.int32, (devices, rows), 0)
    member = (owner[...] == device).astype(F32)
    earlier = lax.broadcasted_iota(jnp.int32, (rows, rows), 0) < lax.broadcasted_iota(
        jnp.int32, (rows, rows), 1
    )
    before = jnp.dot(
        member.astype(BF16), earlier.astype(F32).astype(BF16), preferred_element_type=F32
    )
    for k in range(CAP):
        choose[k] = jnp.where(before == float(k), member, 0.0).astype(BF16)


def pack_first(devices, choose, wide, out):
    right = wide[:, :128].astype(BF16)
    for k in range(CAP):
        out[pl.ds(k, devices, stride=8), :] = jnp.dot(
            choose[k], right, preferred_element_type=F32
        )


def pack_second(devices, traces, element, bits, choose, wide, wsel, out):
    rows = traces.shape[0]
    nt = wsel.shape[2]
    signs = (2 * bits[...] - 1).astype(F32).T.astype(BF16)
    sources = []
    for c in range(3):
        source = jnp.zeros((rows, 128), F32)
        for g in range(G):
            first = (g * 3 + c) * nt
            block = traces[:, first : first + nt] * signs[:, g : g + 1]
            source = source + lax.dot_general(
                block,
                wsel[c].astype(BF16),
                (((1,), (1,)), ((), ())),
                preferred_element_type=F32,
            )
        sources.append(source)
    source = sources[0] + sources[1] + sources[2]
    high = source.astype(BF16).astype(F32)
    low = source - high
    lane = lax.broadcasted_iota(jnp.int32, (rows, 128), 1)
    where_el = jnp.broadcast_to(element[...], (128, rows)).astype(F32).T
    el_high = jnp.floor(where_el * (1.0 / 256.0))
    el_low = where_el - 256.0 * el_high
    extra = pltpu.roll(high, HI - 128, 1) + pltpu.roll(low, LO - 128, 1)
    extra = jnp.where(lane == EL - 128, el_low, extra)
    extra = jnp.where(lane == EL - 127, el_high, extra)
    right = (wide[:, 128:] + extra).astype(BF16)
    for k in range(CAP):
        out[pl.ds(CAP + k, devices, stride=8), :] = jnp.dot(
            choose[k], right, preferred_element_type=F32
        )


def line(m, u, wanted=(0, 1, 2, 3, 4)):
    e0, e1, o0, o1 = u[0] + u[4], u[1] + u[3], u[0] - u[4], u[1] - u[3]
    out = {}
    for i in range(2):
        if i in wanted or 4 - i in wanted:
            ce = [float((m[i, l] + m[i, 4 - l]) / 2) for l in range(2)]
            co = [float((m[i, l] - m[i, 4 - l]) / 2) for l in range(2)]
            even = ce[0] * e0 + ce[1] * e1 + float(m[i, 2]) * u[2]
            odd = co[0] * o0 + co[1] * o1
            out[i], out[4 - i] = odd + even, odd - even
    if 2 in wanted:
        out[2] = float(m[2, 0]) * o0 + float(m[2, 1]) * o1
    return out


def half_row(lower, upper, half):
    return jnp.where(half == 0, float(lower), float(upper)).astype(F32)


def kline(m, p0, p1, p2, half):
    first = half == 0
    ce = [[(m[i, l] + m[i, 4 - l]) / 2 for l in range(2)] for i in range(2)]
    co = [[(m[i, l] - m[i, 4 - l]) / 2 for l in range(2)] for i in range(2)]
    back = jnp.where(first, p2, p1)
    even, odd = p0 + back, p0 - back
    mid = jnp.where(first, p1, pltpu.roll(p1, 4, 1))
    evens, odds = pltpu.roll(even, 4, 1), pltpu.roll(odd, 4, 1)
    eout = (
        half_row(ce[0][0], ce[1][1], half) * even
        + half_row(ce[0][1], ce[1][0], half) * evens
        + half_row(m[0, 2], m[1, 2], half) * mid
    )
    oout = half_row(co[0][0], co[1][1], half) * odd + half_row(co[0][1], co[1][0], half) * odds
    q0 = eout + oout
    q43 = oout - eout
    q22 = half_row(m[2, 0], m[2, 1], half) * odd + half_row(m[2, 1], m[2, 0], half) * odds
    q1 = jnp.where(first, q22, q43)
    q2 = jnp.where(first, q43, pltpu.roll(q43, 4, 1))
    return q0, q1, q2


SIDES = [(-1, 0), (1, 0), (0, -1), (0, 1), (-1, -1), (-1, 1), (1, -1), (1, 1)]
OPPOSITE = [1, 0, 3, 2, 7, 6, 5, 4]
ENDS, SLABS = (0, 1, 4, 5, 6, 7), (2, 3)


GROUPS = {3: ((0, 1, 2),), 4: ((0, 1, 2), (3,))}


def tiles_of(group):
    return (5 * len(group) + 2) // 2


def far_first(nd, ns):
    zs = max(nd // 4, 1)

    def ring(d, n):
        return min(d % n, -d % n)

    def way(k, j):
        total = 0
        for d in range(nd):
            e = (d + k) % nd
            total += ns * (2 * (d // (2 * zs) != e // (2 * zs)) + ring(d // 2 - e // 2, zs))
        for b in range(ns):
            e = (b + j) % ns
            total += nd * (ring(b // 2 - e // 2, max(ns // 2, 1)) + (b % 2 != e % 2))
        return total

    steps = [(k, j) for k in range(nd) for j in range(ns) if (k, j) != (0, 0)]
    return sorted(steps, key=lambda step: (-way(*step), step))


def sizes(comps):
    groups = GROUPS[comps]
    return sum(tiles_of(g) for g in groups), len(groups), (comps + 2) // 2


def step_kernel(
    nd,
    ns,
    disp,
    veloc,
    lame,
    shear,
    density,
    traces,
    weights_in,
    owner_in,
    element_in,
    nodew_in,
    bits_in,
    disp_out,
    veloc_out,
    weights,
    owner,
    element,
    nodew,
    bits,
    raw_disp,
    raw_veloc,
    raw_lame,
    raw_shear,
    raw_density,
    raw_traces,
    CHOOSE,
    WIDE,
    WSEL,
    ROWS,
    OUT,
    IN,
    U,
    W,
    LAM,
    MU,
    CM,
    GR,
    SG,
    F,
    DEP,
    TT,
    OH,
    LEFT,
    *rest,
):
    send, recv = rest[0:8], rest[8:16]
    send_scale, recv_scale = rest[16:20], rest[20:24]
    send_sem, recv_sem, load_sem, all_send, all_recv = rest[24:29]
    dom, slab = lax.axis_index("dom"), lax.axis_index("slab")

    def exists(side):
        da, db = SIDES[side]
        cond = None
        for shift, index, count in ((da, dom, nd), (db, slab, ns)):
            if shift:
                one = index > 0 if shift < 0 else index < count - 1
                cond = one if cond is None else jnp.logical_and(cond, one)
        return cond

    def target(side):
        return (dom + SIDES[side][0], slab + SIDES[side][1])

    for side in range(8):

        @pl.when(jnp.logical_not(exists(side)))
        def _():
            recv[side][...] = jnp.zeros_like(recv[side])
            if side < 4:
                recv_scale[side][...] = jnp.zeros_like(recv_scale[side])

    devices = nd * ns
    me = dom * ns + slab
    barrier = pltpu.get_barrier_semaphore()

    doms = [lax.rem(dom + k, nd) for k in range(nd)]
    slabs = [lax.rem(slab + k, ns) for k in range(ns)]
    order = far_first(nd, ns)

    loads = [
        pltpu.make_async_copy(src, dst, load_sem.at[n])
        for n, (src, dst) in enumerate(
            (
                (traces, raw_traces),
                (disp, raw_disp),
                (density, raw_density),
                (lame, raw_lame),
                (shear, raw_shear),
                (veloc, raw_veloc),
            )
        )
    ]
    small = [
        pltpu.make_async_copy(src, dst, load_sem.at[7 + n])
        for n, (src, dst) in enumerate(
            (
                (owner_in, owner),
                (nodew_in, nodew),
                (weights_in, weights),
                (bits_in, bits),
                (element_in, element),
            )
        )
    ]
    for one in small + loads[:3]:
        one.start()
    for k, j in order:
        pl.semaphore_signal(
            barrier, inc=1, device_id=(doms[k], slabs[j]), device_id_type=MESH
        )
    own_rows = pltpu.make_async_copy(OUT.at[me], IN.at[me], load_sem.at[6])

    def send_rows():
        own_rows.start()
        for k, j in order:
            pltpu.make_async_remote_copy(
                src_ref=OUT.at[doms[k] * ns + slabs[j]],
                dst_ref=IN.at[me],
                send_sem=all_send,
                recv_sem=all_recv,
                device_id=(doms[k], slabs[j]),
                device_id_type=MESH,
            ).start()

    def finish_rows():
        own_rows.wait()
        k, j = order[0]
        pltpu.make_async_remote_copy(
            src_ref=OUT.at[pl.ds(0, devices - 1)],
            dst_ref=IN.at[pl.ds(0, devices - 1)],
            send_sem=all_send,
            recv_sem=all_recv,
            device_id=(doms[k], slabs[j]),
            device_id_type=MESH,
        ).wait()

    for one in small:
        one.wait()
    choose_rows(devices, weights, owner, nodew, CHOOSE, WIDE, WSEL)
    pack_first(devices, CHOOSE, WIDE, ROWS)
    loads[0].wait()
    for one in loads[3:]:
        one.start()
    pack_second(devices, raw_traces, element, bits, CHOOSE, WIDE, WSEL, ROWS)
    OUT[...] = ROWS[...].reshape(devices, 8, 128).astype(BF16)

    sub = lax.broadcasted_iota(jnp.int32, (1, 8, 128), 1)
    lane = lax.broadcasted_iota(jnp.int32, (1, 8, 128), 2)
    half, bit_b, bit_a = sub // 4, (sub // 2) % 2, sub % 2

    def roll_s(x, shift):
        return pltpu.roll(x, shift % 8, 1)

    def roll_l(x, shift):
        return pltpu.roll(x, shift % 128, 2)

    def load_pairs(dst, src):
        lead = (slice(None),) * (len(dst.shape) - 3)
        for kp in range(3):
            dst[lead + (kp, slice(0, 4))] = src[lead + (2 * kp,)]
            dst[lead + (kp, slice(4, 8))] = src[lead + (min(2 * kp + 1, 4),)]

    def local_sums(comps, planes, extra=None):
        for c in range(comps):
            for i in planes:
                p0, p1, p2 = (F[c, i, :, kp] for kp in range(3))
                if extra is not None:
                    at = (c * 75 + i * 15) * 8
                    add = extra[at : at + 120, :].reshape(5, 3, 8, 128)
                    p0, p2 = p0 + add[:, 0], p2 + add[:, 2]
                    F[c, i, :, 1] = p1 + add[:, 1]
                    F[c, i, :, 2] = p2
                F[c, i, :, 0] = p0 + jnp.where((half == 0) & (lane > 0), roll_l(p2, 1), 0.0)
            if 0 in planes:
                for j in range(5):
                    x0, x4 = F[c, 0, j], F[c, 4, j]
                    F[c, 0, j] = x0 + jnp.where(bit_a == 1, roll_s(x4, 1), 0.0)
                    F[c, 4, j] = x4 + jnp.where(bit_a == 0, roll_s(x0, -1), 0.0)
            for i in planes:
                x0, x4 = F[c, i, 0], F[c, i, 4]
                F[c, i, 0] = x0 + jnp.where(bit_b == 1, roll_s(x4, 2), 0.0)
                F[c, i, 4] = x4 + jnp.where(bit_b == 0, roll_s(x0, -2), 0.0)

    def close_k(x):
        x0 = x[0:1]
        dup = jnp.where(half == 0, x0, roll_s(x0, 4))
        x2 = jnp.where(lane < 127, roll_l(dup, -1), x[2:3])
        return jnp.concatenate([x[0:2], x2], axis=0)

    def merge(x, y, bit, width, value):
        toward = width if value == 0 else -width
        return jnp.where(bit == value, x, roll_s(y, toward))

    def unmerge(m, bit, width, value):
        toward = -width if value == 0 else width
        keep = bit == value
        return jnp.where(keep, roll_s(m, toward), 0.0), jnp.where(keep, m, 0.0)

    def ends(zs):
        out = jnp.zeros((1, 8, 128), F32)
        for n, z in enumerate(zs):
            out = jnp.where(lane == n, roll_l(z, n + 1), out)
        return out

    def end_of(row, n):
        return jnp.where(lane == 127, roll_l(row, 127 - n), 0.0)

    def face(side):
        axis, value = side // 2, side % 2
        bit, width = ((bit_a, 1), (bit_b, 2))[axis]
        node = 4 * value

        def at(c, n, kp):
            return (c, node, n, kp) if axis == 0 else (c, n, node, kp)

        def line_at(c, kp):
            return (c, node, slice(None), kp) if axis == 0 else (c, slice(None), node, kp)

        return bit, width, value, at, line_at

    def pack(comps, slot, sides):
        for side in [side for side in sides if side < 4]:
            bit, width, value, at, line_at = face(side)
            tile = 0
            for g, group in enumerate(GROUPS[comps]):
                rows = []
                for c in group:
                    merged = merge(F[line_at(c, 0)], F[line_at(c, 1)], bit, width, value)
                    rows.extend(merged[n : n + 1] for n in range(5))
                rows.append(ends([F[at(c, n, 2)][None] for c in group for n in range(5)]))
                largest = jnp.abs(rows[0])
                for row in rows[1:]:
                    largest = jnp.maximum(largest, jnp.abs(row))
                scale = largest * (1.0 / 32000.0) + 1e-30
                send_scale[side][slot, g : g + 1] = scale
                inverse = 1.0 / scale
                for n in range(0, len(rows), 2):
                    x = jnp.concatenate([rows[n][0] * inverse[0], rows[n + 1][0] * inverse[0]], 0)
                    x = x + jnp.where(x < 0.0, -0.5, 0.5)
                    send[side][slot, tile] = x.astype(jnp.int32).astype(jnp.int16)
                    tile += 1
            start(side, comps, slot)
        pack_corners(comps, slot, [side for side in sides if side >= 4])

    def pack_corners(comps, slot, sides):
        for side in sides:
            da, db = SIDES[side]
            va, vb = (da + 1) // 2, (db + 1) // 2
            items = []
            for c in range(comps):
                x = F[c, 4 * va, 4 * vb]
                items.append(merge(x[0:1], x[1:2], bit_a, 1, va))
            items.append(ends([F[c, 4 * va, 4 * vb, 2:3] for c in range(comps)]))
            for n in range(0, len(items), 2):
                y = items[min(n + 1, len(items) - 1)]
                send[side][slot, n // 2 : n // 2 + 1] = merge(items[n], y, bit_b, 2, vb)
            start(side, comps, slot)

    def unpack(comps, slot, sides):
        for side in [side for side in sides if side < 4]:
            finish(side, comps, slot)
            bit, width, value, at, line_at = face(side)
            tile = 0
            for g, group in enumerate(GROUPS[comps]):
                scale = recv_scale[side][slot, g : g + 1]
                rows = []
                for _ in range(tiles_of(group)):
                    x = recv[side][slot, tile].astype(jnp.int32).astype(F32)
                    rows.extend([x[None, 0:8] * scale, x[None, 8:16] * scale])
                    tile += 1
                for m, c in enumerate(group):
                    merged = jnp.concatenate(rows[5 * m : 5 * m + 5], axis=0)
                    for kp, add in enumerate(unmerge(merged, bit, width, value)):
                        F[line_at(c, kp)] = F[line_at(c, kp)] + add
                last, _ = unmerge(rows[5 * len(group)], bit, width, value)
                for m, c in enumerate(group):
                    for n in range(5):
                        F[at(c, n, 2)] = F[at(c, n, 2)] + end_of(last, 5 * m + n)[0]
        for side in [side for side in sides if side >= 4]:
            da, db = SIDES[side]
            va, vb = (da + 1) // 2, (db + 1) // 2
            items = []
            finish(side, comps, slot)
            for n in range(sizes(comps)[2]):
                items.extend(unmerge(recv[side][slot, n : n + 1], bit_b, 2, vb))
            last, _ = unmerge(items[comps], bit_a, 1, va)
            for c in range(comps):
                x, y = unmerge(items[c], bit_a, 1, va)
                add = jnp.concatenate([x, y, end_of(last, c)], axis=0)
                F[c, 4 * va, 4 * vb] = F[c, 4 * va, 4 * vb] + add

    def copies(side, comps, slot, source):
        tiles, scales, rows = sizes(comps)
        parts = [(send, recv, tiles, side)] if side < 4 else [(send, recv, rows, side)]
        if side < 4:
            parts.append((send_scale, recv_scale, scales, 8 + side))
        out = []
        for src, dst, count, number in parts:
            there = number - side + OPPOSITE[side] if source else number
            out.append(
                pltpu.make_async_remote_copy(
                    src_ref=src[side].at[slot, pl.ds(0, count)],
                    dst_ref=dst[OPPOSITE[side] if source else side].at[slot, pl.ds(0, count)],
                    send_sem=send_sem.at[number, slot],
                    recv_sem=recv_sem.at[there, slot],
                    device_id=target(side),
                    device_id_type=MESH,
                )
            )
        return out

    def start(side, comps, slot):
        @pl.when(exists(side))
        def _():
            for one in copies(side, comps, slot, True):
                one.start()

    def finish(side, comps, slot):
        @pl.when(exists(side))
        def _():
            for one in copies(side, comps, slot, False):
                one.wait()

    def quad(i, j):
        w = WEIGHTS
        scale = w[i] * w[j] / 8.0
        return jnp.concatenate(
            [half_row(scale * w[2 * kp], scale * w[min(2 * kp + 1, 4)], half) for kp in range(3)],
            axis=0,
        )

    def share(i, j):
        one = jnp.ones((1, 8, 128), F32)

        def along(n, bit, index, devices):
            if n == 0:
                return jnp.where((bit == 1) | (index > 0), 0.5, 1.0)
            if n == 4:
                return jnp.where((bit == 0) | (index < devices - 1), 0.5, 1.0)
            return one

        ab = along(i, bit_a, dom, nd) * along(j, bit_b, slab, ns)
        k0 = jnp.where((half == 0) & (lane > 0), 0.5, 1.0)
        k4 = jnp.where(lane < 127, 0.5, 1.0)
        return jnp.concatenate([ab * k0, ab * one, ab * k4], axis=0)

    loads[1].wait()
    loads[2].wait()
    load_pairs(U, raw_disp)
    load_pairs(CM, raw_density)
    for i in range(5):
        for j in range(5):
            F[3, i, j] = CM[i, j] * quad(i, j)
            for c in range(3):
                F[c, i, j] = U[c, i, j]
    local_sums(4, (0, 4, 1, 2, 3))
    pl.semaphore_wait(barrier, devices - 1)
    send_rows()
    pack(4, 0, ENDS + SLABS)
    for one in loads[3:]:
        one.wait()
    load_pairs(LAM, raw_lame)
    load_pairs(MU, raw_shear)
    load_pairs(W, raw_veloc)
    for i in range(5):
        for j in range(5):
            q = quad(i, j)
            LAM[i, j] = LAM[i, j] * q
            MU[i, j] = MU[i, j] * q

    def take_rows():
        finish_rows()
        ROWS[...] = IN[...].astype(F32).reshape(8 * devices, 128)
        for k in range(CAP):
            first = ROWS[pl.ds(k, devices, stride=8), :]
            second = ROWS[pl.ds(CAP + k, devices, stride=8), :]
            TT[0:128, k * devices : (k + 1) * devices] = first.T
            TT[128:256, k * devices : (k + 1) * devices] = second.T
            el = second[:, EL - 128 : EL - 127] + 256.0 * second[:, EL - 127 : EL - 126]
            cols = lax.broadcasted_iota(jnp.int32, (devices, 512), 1)
            OH[k * devices : (k + 1) * devices, :] = (
                (cols == el.astype(jnp.int32)).astype(F32).astype(BF16)
            )

    def deposit(s):
        for c in range(3):
            row = c * STEPS + s
            src = TT[pl.ds(HI + row, 1), :] + TT[pl.ds(LO + row, 1), :]
            term = TT[0:160, :] * src
            high = term.astype(BF16)
            LEFT[c * 320 : c * 320 + 160, :] = high
            LEFT[c * 320 + 160 : c * 320 + 320, :] = (term - high.astype(F32)).astype(BF16)
        sums = jnp.dot(LEFT[...], OH[...], preferred_element_type=F32)
        for c in range(3):
            first = c * 320
            both = sums[first : first + 152, :] + sums[first + 160 : first + 312, :]
            for a in range(2):
                for b in range(2):
                    q, col = b * 2 + a, (a * 2 + b) * 128
                    DEP[pl.ds(c * 600 + q, NODES6, stride=4), :] = both[
                        0:NODES6, col : col + 128
                    ]

    def begin(lines):
        for i, j in lines:
            part = share(i, j)
            mass = close_k(F[3, i, j])
            CM[i, j] = (DT * DT) / mass
            scaled = mass * part * (1.0 / DT)
            for c in range(3):
                U[c, i, j] = close_k(F[c, i, j]) * part
                W[c, i, j] = W[c, i, j] * scaled

    inner = [(i, j) for i in range(1, 4) for j in range(1, 4)]
    rims = [(i, j) for i in range(1, 4) for j in (0, 4)]
    outer = [(i, j) for i in (0, 4) for j in range(5)]

    pair = {(0, 0): 0, (1, 1): 1, (2, 2): 2, (0, 1): 3, (0, 2): 4, (1, 2): 5}

    def stress(c, d):
        return pair[(min(c, d), max(c, d))]

    def along_k(planes, js):
        for c in range(3):
            for i in planes:
                for first, last in js:
                    outs = kline(FORWARD, *(U[c, i, first:last, kp] for kp in range(3)), half)
                    for kp in range(3):
                        GR[2, c, i, first:last, kp] = outs[kp]

    def along_j(planes):
        for c in range(3):
            for i in planes:
                outs = line(FORWARD, [U[c, i, j] for j in range(5)])
                for j in range(5):
                    GR[1, c, i, j] = outs[j]

    def one_step(s, carry):
        along_j((0, 4))
        along_k((0, 4), ((0, 5),))
        for c in range(3):
            for j in range(5):
                outs = line(FORWARD, [U[c, i, j] for i in range(5)])
                for i in range(5):
                    GR[0, c, i, j] = outs[i]
        for i in range(5):
            for j in range(5):
                g = [[GR[d, c, i, j] for c in range(3)] for d in range(3)]
                mu = MU[i, j]
                mu2 = mu + mu
                vol = LAM[i, j] * (g[0][0] + g[1][1] + g[2][2])
                for c in range(3):
                    SG[c, i, j] = mu2 * g[c][c] + vol
                    for d in range(c):
                        SG[stress(c, d), i, j] = mu * (g[c][d] + g[d][c])
        slot = (s + 1) % 2
        force((0, 4))

        @pl.when(s == 0)
        def _():
            take_rows()
            deposit(0)
            for c in range(3):
                for i in range(5):
                    at = (c * 75 + i * 15) * 8
                    DEP[at : at + 120, :] = DEP[at : at + 120, :] + W[c, i].reshape(120, 128)
                    W[c, i] = jnp.zeros((5, 3, 8, 128), F32)

        local_sums(3, (0, 4), DEP)
        pack(3, slot, ENDS)
        force((1, 2, 3))

        local_sums(3, (1, 2, 3), DEP)
        pack(3, slot, SLABS)

        @pl.when(s < STEPS - 1)
        def _():
            deposit(s + 1)

        update(inner)
        along_k((1, 2, 3), ((1, 4),))
        unpack(3, slot, SLABS)
        update(rims)

        @pl.when(s < STEPS - 1)
        def _():
            along_k((1, 2, 3), ((0, 1), (4, 5)))
            along_j((1, 2, 3))

        unpack(3, slot, ENDS)
        update(outer)
        return carry

    def leave(planes):
        for c in range(3):
            for i in planes:
                U[c, i] = U[c, i] - W[c, i]
                for k in range(5):
                    rows = slice(4 * (k % 2), 4 * (k % 2) + 4)
                    disp_out[c, i, :, k] = U[c, i, :, k // 2, rows]
                    veloc_out[c, i, :, k] = W[c, i, :, k // 2, rows]

    def force(planes):
        for c in range(3):
            for j in range(5):
                outs = line(BACKWARD, [SG[stress(c, 0), i, j] for i in range(5)], planes)
                for i in planes:
                    F[c, i, j] = outs[i]
            for i in planes:
                outs = line(BACKWARD, [SG[stress(c, 1), i, j] for j in range(5)])
                for j in range(5):
                    F[c, i, j] = F[c, i, j] + outs[j]
                p = stress(c, 2)
                outs = kline(BACKWARD, SG[p, i, :, 0], SG[p, i, :, 1], SG[p, i, :, 2], half)
                for kp in range(3):
                    F[c, i, :, kp] = F[c, i, :, kp] + outs[kp]

    def update(lines):
        for i, j in lines:
            cm = CM[i, j]
            for c in range(3):
                w = W[c, i, j] + close_k(F[c, i, j]) * cm
                W[c, i, j] = w
                U[c, i, j] = U[c, i, j] + w

    begin(inner)
    along_k((1, 2, 3), ((1, 4),))
    unpack(4, 0, SLABS)
    begin(rims)
    along_k((1, 2, 3), ((0, 1), (4, 5)))
    along_j((1, 2, 3))
    unpack(4, 0, ENDS)
    begin(outer)
    lax.fori_loop(0, STEPS, one_step, 0)
    leave((0, 1, 2, 3, 4))


def to_rows(x):
    lead = x.shape[:-2]
    n = len(lead)
    y = x.reshape(lead + (2, 2, EC))
    return jnp.swapaxes(y, n, n + 1).reshape(lead + (4, EC))


def from_rows(x):
    lead = x.shape[:-2]
    n = len(lead)
    y = jnp.swapaxes(x.reshape(lead + (2, 2, EC)), n, n + 1)
    return y.reshape(lead + (2, 2 * EC))


def shards(
    nd,
    ns,
    displacement,
    velocity,
    lame_lambda,
    shear_modulus,
    density,
    traces,
    section_weights,
    owner,
    element_idx,
    node_weights,
    encode_bits,
):
    devices = nd * ns
    rows = traces.shape[0]
    field = (5, 5, 3, 8, 128)
    vm = lambda *shape: pltpu.VMEM(shape, F32)
    tiles, scales, ends = sizes(4)
    messages = [pltpu.VMEM((2, tiles, 16, 128), jnp.int16) for side in range(4)]
    messages += [vm(2, ends, 8, 128) for side in range(4)]
    factors = [vm(2, scales, 8, 128) for side in range(4)]
    out = jax.ShapeDtypeStruct((3, 5, 5, 5, 4, EC), F32)
    disp, veloc = pl.pallas_call(
        functools.partial(step_kernel, nd, ns),
        out_shape=(out, out),
        in_specs=[pl.BlockSpec(memory_space=pltpu.HBM)] * 11,
        out_specs=(pl.BlockSpec(memory_space=pltpu.VMEM),) * 2,
        scratch_shapes=[
            pltpu.VMEM(section_weights.shape, BF16),
            pltpu.VMEM((1, rows), jnp.int32),
            pltpu.VMEM((1, rows), jnp.int32),
            pltpu.VMEM(node_weights.shape, BF16),
            pltpu.VMEM((G, rows), jnp.int32),
            vm(3, 5, 5, 5, 4, EC),
            vm(3, 5, 5, 5, 4, EC),
            vm(5, 5, 5, 4, EC),
            vm(5, 5, 5, 4, EC),
            vm(5, 5, 5, 4, EC),
            pltpu.VMEM(traces.shape, BF16),
            pltpu.VMEM((CAP, devices, rows), BF16),
            vm(rows, 256),
            vm(3, 128, section_weights.shape[1]),
            vm(8 * devices, 128),
            pltpu.VMEM((devices, 8, 128), BF16),
            pltpu.VMEM((devices, 8, 128), BF16),
            vm(3, *field),
            vm(3, *field),
            vm(*field),
            vm(*field),
            vm(*field),
            vm(3, 3, *field),
            vm(6, *field),
            vm(4, *field),
            vm(1808, 128),
            vm(256, CAP * devices),
            pltpu.VMEM((CAP * devices, 512), BF16),
            pltpu.VMEM((960, CAP * devices), BF16),
            *messages,
            *messages,
            *factors,
            *factors,
            pltpu.SemaphoreType.DMA((12, 2)),
            pltpu.SemaphoreType.DMA((12, 2)),
            pltpu.SemaphoreType.DMA((12,)),
            pltpu.SemaphoreType.DMA,
            pltpu.SemaphoreType.DMA,
        ],
        compiler_params=pltpu.CompilerParams(
            collective_id=1, has_side_effects=True, vmem_limit_bytes=28 * 2**20
        ),
        name="time_steps",
    )(
        *(
            pltpu.with_memory_space_constraint(x, pltpu.HBM)
            for x in (
                to_rows(displacement),
                to_rows(velocity),
                to_rows(lame_lambda),
                to_rows(shear_modulus),
                to_rows(density),
                traces,
                section_weights,
                owner.reshape(1, rows),
                element_idx.reshape(1, rows),
                node_weights,
                encode_bits.T,
            )
        )
    )
    return from_rows(disp + veloc), from_rows(veloc * (1.0 / DT))


def solution(mesh):
    nd, ns = mesh.shape["dom"], mesh.shape["slab"]
    both = P(("dom", "slab"), None)
    fields = P(None, None, None, None, "dom", "slab")
    params = P(None, None, None, "dom", "slab")
    return jax.shard_map(
        functools.partial(shards, nd, ns),
        mesh=mesh,
        in_specs=(
            fields,
            fields,
            params,
            params,
            params,
            both,
            P(),
            both,
            P(("dom", "slab")),
            both,
            both,
        ),
        out_specs=(fields, fields),
        check_vma=False,
    )
```
